32 devices in a mesh: seq: 8 (over z, y), exp: 4 (over x, core).
Axes of the slice: x: 2, y: 2, z: 4, core: 2. Of those that a mesh axis runs over, the one named last changes fastest.
Arguments:
- projected: bfloat16 [4096, 3, 8192], P('seq', None, 'exp'), may hold values from -6 to 6
- log_decay: float32 [4096, 64], P('seq', 'exp'), may hold values from -2.5 to 0, as said below
- norm_gain: float32 [8192], P('exp'), may hold values from 0.1 to 1.9
- moe_tokens: bfloat16 [256, 6144], P(('seq', 'exp')), may hold values from -6 to 6
- expert_ids: int32 [256, 2], P(('seq', 'exp')), may hold values from 0 to 3, all different within a row; in each aligned block of 8 rows (0 to 7, 8 to 15, ...) at most 4 rows name the same one
- route_probs: float32 [256, 2], P(('seq', 'exp')), may hold values from 0.1 to 1
- w_in: bfloat16 [4, 6144, 2, 4608], P('exp', None, None, 'seq'), may hold values from -0.078125 to 0.078125
- w_out: bfloat16 [4, 4608, 6144], P('exp', 'seq'), may hold values from -0.09375 to 0.09375
Outputs:
- attn_out: bfloat16 [4096, 8192], P('seq', 'exp')
- moe_out: bfloat16 [256, 6144], P(('seq', 'exp'))
The draws below stay inside these ranges and needn't reach their ends.
Inputs may be any that keep to these rules, and one draw needn't show every extreme that they name: `log_decay`: negative in every entry. `expert_ids`: A token names 2 different experts. In the rows of one device (aligned blocks of 8 tokens) no expert is named more than 4 times, a bound that some block reaches.
All inputs are finite; a program needn't handle non-finite values.
Results may differ from the reference program's by a relative error of at most 0.025.
Values may be sent and summed in bfloat16 or wider, within the bound.
No kernel may reach another device: no remote copies, remote signals or barrier semaphores. Data moves between devices by JAX's collectives and lax.ppermute only.
A program may use at most 128 MiB of HBM per device.

```python
import math
import jax
import jax.numpy as jnp
import numpy as np
from jax import lax

D = 6144
ATTENTION_HEADS = 64
HEAD_DIM = 128
FFH = 4608
TOPK = 2
TOK_DEV = 512
MTOK_DEV = 8
EXPERTS = 4
CAP = 4
SEQUENCE_LENGTH = 4096
MTOKENS = 256
N_SEQ = 8
N_EXP = 4


def draw_log_decay(key, part):
    key_rows = jax.random.split(key, 7)
    token_position = jnp.arange(SEQUENCE_LENGTH)
    partition_piece = token_position // TOK_DEV
    shards = SEQUENCE_LENGTH // TOK_DEV
    slow_share = 5
    is_slow = jax.random.randint(key_rows[0], (ATTENTION_HEADS,), 0, 10) < slow_share
    slow_rate = -jnp.exp(jax.random.uniform(key_rows[1], (ATTENTION_HEADS,), jnp.float32, math.log(0.05), math.log(0.5))) / SEQUENCE_LENGTH
    fast_rate = -1.0 / jax.random.uniform(key_rows[2], (ATTENTION_HEADS,), jnp.float32, 30.0, 50.0)
    base_offset = jnp.where(is_slow, slow_rate, fast_rate)
    partition_factor = jnp.exp(jax.random.uniform(key_rows[3], (shards, ATTENTION_HEADS), jnp.float32, math.log(0.5), math.log(2.0)))
    coarse_estimate = jax.random.uniform(key_rows[4], (SEQUENCE_LENGTH, ATTENTION_HEADS), jnp.float32, 0.5, 1.5)
    spike_position = jax.random.randint(key_rows[5], (3, ATTENTION_HEADS), 0, SEQUENCE_LENGTH)
    spike_penalty = jax.random.uniform(key_rows[6], (3, ATTENTION_HEADS), jnp.float32, 0.2, 0.5)
    match_found = token_position[:, None, None] == spike_position[None]
    spike_event = jnp.sum(jnp.where(match_found, jnp.log(1.0 - spike_penalty)[None], 0.0), axis=1)
    return (base_offset[None] * partition_factor[partition_piece] * coarse_estimate + spike_event).astype(jnp.float32)


def steps_of(key, shape, cuts, least, top_value):
    def one(axis_at, shards_of):
        heights = jax.random.uniform(jax.random.fold_in(jax.random.fold_in(key, 6), axis_at), (shards_of,), jnp.float32, least / len(cuts), top_value / len(cuts))
        return jnp.repeat(jnp.exp(heights), shape[axis_at] // shards_of).reshape((-1,) + (1,) * (len(shape) - axis_at - 1))

    loudness = one(*cuts[0])
    for cut in cuts[1:]:
        loudness = loudness * one(*cut)
    return loudness


def routed_block(rng, own, number, rows, amount, top, limit, slope):
    ranking = jax.random.permutation(rng, amount)
    heavy_load, usual = shares(amount, rows * top, limit, slope, True), shares(amount, rows * top, limit, slope, False)
    places = jnp.arange(amount)

    def named(tallies, turn):
        used = int((tallies > 0).sum())
        fixed = max(1, used // 4)
        shifted = fixed + (places - fixed + turn * (used - fixed)) % max(1, amount - fixed)
        return jnp.zeros((amount,), jnp.int32).at[ranking[jnp.where(places < fixed, places, shifted)]].set(jnp.asarray(tallies, jnp.int32))

    tallies = jnp.where(number % 4 == 0, named(heavy_load, number // 4), named(usual, number - number // 4 - 1))
    mixed = jax.random.permutation(jax.random.fold_in(own, 3), amount)
    giver, sink = mixed[0:amount // 2 * 2:2], mixed[1:amount // 2 * 2:2]
    room = jnp.minimum(tallies[giver] - 1, limit - tallies[sink]) // 2
    room = jnp.where((giver == ranking[0]) | (sink == ranking[0]) | (tallies[sink] == 0), 0, jnp.maximum(room, 0))
    shifted = jax.random.randint(jax.random.fold_in(own, 4), (amount // 2,), 0, 1 << 20) % (room + 1)
    tallies = tallies.at[giver].add(-shifted).at[sink].add(shifted)
    items = jnp.searchsorted(jnp.cumsum(tallies), jnp.arange(rows * top), side="right").astype(jnp.int32)
    listing = items.reshape(top, rows).T
    listing = listing[jax.random.permutation(jax.random.fold_in(own, 1), rows)]
    turn = jax.random.randint(jax.random.fold_in(own, 2), (rows, 1), 0, top)
    return jnp.take_along_axis(listing, (jnp.arange(top)[None, :] + turn) % top, axis=1)


def shares(amount, total, limit, skew, full):
    portions = [(1 << 20) // math.isqrt(rank ** skew) + 1 for rank in range(1, amount + 1)]
    largest = limit if full else min(limit, max(-(-total // amount), total * portions[0] // sum(portions)))
    least = 1 if total - largest >= amount - 1 else 0
    counts, spare = [largest] + [least] * (amount - 1), total - largest - least * (amount - 1)
    while spare > 0:
        free = [i for i in range(1, amount) if counts[i] < largest] or [i for i in range(1, amount) if counts[i] < limit]
        mass, remaining = sum([portions[i] for i in free]), spare
        for i in free:
            extra = min(limit - counts[i], max(1, remaining * portions[i] // mass), spare)
            counts[i] = counts[i] + extra
            spare = spare - extra
    return np.array(counts)


def bell_draw(rng, dims, spread, bound, cuts=(), kind=jnp.bfloat16):
    factor_of = steps_of(rng, dims, cuts, -0.22, 0.18) if cuts else 1.0
    drawn = jax.random.normal(rng, dims, jnp.float32) * spread * factor_of
    return jnp.minimum(jnp.maximum(drawn, -bound), bound).astype(kind)


def setup_inputs(seed: int = 0) -> dict:
    arg_keys = jax.random.split(jax.random.key(seed), 9)
    projected = bell_draw(arg_keys[0], (SEQUENCE_LENGTH, 3, ATTENTION_HEADS * HEAD_DIM), 1.0, 6.0, ((0, 8), (2, 4)))
    log_decay = draw_log_decay(jax.random.fold_in(arg_keys[8], 71), 0)
    norm_gain = jnp.clip(1.0 + 0.18 * jax.random.normal(arg_keys[2], (ATTENTION_HEADS * HEAD_DIM,), jnp.float32), 0.1, 1.9)
    moe_tokens = bell_draw(arg_keys[3], (MTOKENS, D), 1.0, 6.0, ((0, 32),))
    expert_ids_keys = jax.random.split(jax.random.fold_in(arg_keys[4], 1), MTOKENS // MTOK_DEV)
    expert_ids_turns = jax.random.permutation(jax.random.fold_in(arg_keys[4], 3), MTOKENS // MTOK_DEV)
    expert_ids = jax.vmap(lambda own, number: routed_block(jax.random.fold_in(arg_keys[4], 2), own, number, MTOK_DEV, EXPERTS, TOPK, CAP, 2))(expert_ids_keys, expert_ids_turns).reshape((MTOKENS, TOPK))
    route_probs = jnp.clip(0.1 + 0.9 * jax.random.uniform(arg_keys[5], (MTOKENS, TOPK), jnp.float32) ** steps_of(arg_keys[5], (MTOKENS, TOPK), ((0, 32),), -0.2, 0.2), 0.1, 1.0)
    w_in = bell_draw(arg_keys[6], (EXPERTS, D, 2, FFH), D ** -0.5, 0.078125, ((0, 4), (3, 8)))
    w_out = bell_draw(arg_keys[7], (EXPERTS, FFH, D), FFH ** -0.5, 0.09375, ((0, 4), (1, 8)))
    return {"projected": projected, "log_decay": log_decay, "norm_gain": norm_gain, "moe_tokens": moe_tokens, "expert_ids": expert_ids, "route_probs": route_probs, "w_in": w_in, "w_out": w_out}


EPS = 1e-06
HIGH = lax.Precision.HIGHEST

def reference(projected, log_decay, norm_gain, moe_tokens, expert_ids, route_probs, w_in, w_out):
    blocks = SEQUENCE_LENGTH // TOK_DEV
    proj = projected.reshape(blocks, TOK_DEV, 3, ATTENTION_HEADS, HEAD_DIM)
    logs = log_decay.reshape(blocks, TOK_DEV, ATTENTION_HEADS)
    causal = (jnp.arange(TOK_DEV)[:, None] >= jnp.arange(TOK_DEV)[None, :])[None]

    def advance(state, inputs):
        block, decay_logs = inputs
        queries = block[:, 0].astype(jnp.float32)
        key_rows = block[:, 1].astype(jnp.float32)
        values = block[:, 2].astype(jnp.float32)
        running = jnp.cumsum(decay_logs, axis=0)
        last = running[-1]
        weighted = key_rows * jnp.exp(last[None] - running)[:, :, None]
        local_state = jnp.einsum('thi,thj->hij', weighted, values, precision=HIGH)
        scores = jnp.einsum('thd,uhd->htu', queries, key_rows, precision=HIGH)
        turned = running.T
        gap = turned[:, :, None] - turned[:, None, :]
        decay = jnp.exp(jnp.where(causal, gap, -jnp.inf))
        weights = (scores * decay).astype(jnp.bfloat16)
        local_part = jnp.einsum('htu,uhd->thd', weights.astype(jnp.float32), values, precision=HIGH)
        carried_part = jnp.einsum('thd,hde->the', queries * jnp.exp(running)[:, :, None], state, precision=HIGH)
        mixed = local_part + carried_part
        scaled = mixed * lax.rsqrt(lax.optimization_barrier(jnp.mean(mixed * mixed, axis=-1, keepdims=True)) + EPS)
        new_state = jnp.exp(last)[:, None, None] * state + local_state
        return (new_state, scaled)
    start_state = jnp.zeros((ATTENTION_HEADS, HEAD_DIM, HEAD_DIM), jnp.float32)
    _, outputs = lax.scan(advance, start_state, (proj, logs))
    attn_out = (outputs.reshape(SEQUENCE_LENGTH, ATTENTION_HEADS * HEAD_DIM) * norm_gain).astype(jnp.bfloat16)
    devices = N_SEQ * N_EXP
    pairs = MTOK_DEV * TOPK
    tokens = moe_tokens.reshape(devices, MTOK_DEV, D)
    routes = expert_ids.reshape(devices, pairs)
    spread_rows = jnp.repeat(tokens, TOPK, axis=1).astype(jnp.float32)
    onehot = (routes[:, :, None] == jnp.arange(EXPERTS, dtype=jnp.int32)[None, None]).astype(jnp.int32)
    slot = lax.optimization_barrier(jnp.sum((jnp.cumsum(onehot, axis=1) - onehot) * onehot, axis=2))
    group_units = FFH // N_SEQ
    slot_range = jnp.arange(CAP, dtype=jnp.int32)

    def per_expert(total, expert):
        pick = ((routes == expert)[:, None, :] & (slot[:, None, :] == slot_range[None, :, None])).astype(jnp.float32)
        rows = jnp.einsum('dca,dax->dcx', pick, spread_rows, precision=HIGH).astype(jnp.bfloat16).reshape(devices * CAP, D)
        w_here = lax.dynamic_index_in_dim(w_in, expert, 0, keepdims=False)
        down_here = lax.dynamic_index_in_dim(w_out, expert, 0, keepdims=False)
        gate = jnp.dot(rows, w_here[:, 0, :], preferred_element_type=jnp.float32)
        up = jnp.dot(rows, w_here[:, 1, :], preferred_element_type=jnp.float32)
        hidden = (jax.nn.silu(gate) * up).astype(jnp.bfloat16)

        def add_group(acc, group):
            part_h = lax.dynamic_slice_in_dim(hidden, group * group_units, group_units, 1)
            part_w = lax.dynamic_slice_in_dim(down_here, group * group_units, group_units, 0)
            rounded = lax.optimization_barrier(jnp.dot(part_h, part_w, preferred_element_type=jnp.float32).astype(jnp.bfloat16))
            return (acc + rounded.astype(jnp.float32), None)
        summed, _ = lax.scan(add_group, jnp.zeros((devices * CAP, D), jnp.float32), jnp.arange(N_SEQ, dtype=jnp.int32))
        result = lax.optimization_barrier(summed.astype(jnp.bfloat16)).astype(jnp.float32).reshape(devices, CAP, D)
        back = jnp.einsum('dca,dcx->dax', pick, result, precision=HIGH)
        return (total + back, None)
    gathered, _ = lax.scan(per_expert, jnp.zeros((devices, pairs, D), jnp.float32), jnp.arange(EXPERTS, dtype=jnp.int32))
    probs = route_probs.reshape(devices, pairs)
    weighted_out = (gathered * probs[:, :, None]).reshape(devices, MTOK_DEV, TOPK, D)
    moe_out = lax.optimization_barrier(jnp.sum(weighted_out, axis=2)).reshape(MTOKENS, D).astype(jnp.bfloat16)
    return (attn_out, moe_out)
```

```python
import functools
import jax
import jax.numpy as jnp
from jax import lax
from jax.experimental import pallas as pl
from jax.experimental.pallas import tpu as pltpu
from jax.sharding import PartitionSpec as P

EPS = 1e-06
CHUNK = 128
PIECES = 3
F32 = jnp.float32
BF16 = jnp.bfloat16
NT = (((1,), (1,)), ((), ()))
TN = (((0,), (0,)), ((), ()))
NN = (((1,), (0,)), ((), ()))


def factors(size):
    bits = size.bit_length() - 1
    inner = 2 ** (bits // 2)
    return size // inner, inner


class Axis:
    def __init__(self, name, n, inner, outer):
        self.name, self.n, self.inner, self.outer = name, n, inner, outer

    def index(self):
        return (lax.axis_index(self.name) // self.inner) % self.n

    def flat(self, o, i, j):
        return (o * self.n + i) * self.inner + j

    def turn(self, k):
        return [
            (self.flat(o, i, j), self.flat(o, (i + k) % self.n, j))
            for o in range(self.outer)
            for i in range(self.n)
            for j in range(self.inner)
        ]

    def hop(self, i):
        return [
            (self.flat(o, i, j), self.flat(o, i + 1, j))
            for o in range(self.outer)
            for j in range(self.inner)
        ]

    def send(self, a, k):
        return lax.ppermute(a, self.name, self.turn(k))


def gather(axis, a):
    return jnp.concatenate([a] + [axis.send(a, k) for k in range(1, axis.n)], 0)


def total(parts):
    s = parts[0].astype(F32)
    for p in parts[1:]:
        s = s + p.astype(F32)
    return s.astype(BF16)


def scatter(axis, parts):
    return total([parts[0]] + [axis.send(parts[k], axis.n - k) for k in range(1, axis.n)])


def rows_split(a, n):
    m = a.shape[0] // n
    return [a[i * m : (i + 1) * m] for i in range(n)]


def pieces_of(x):
    out = []
    for _ in range(PIECES):
        hi = lax.reduce_precision(x, 8, 7)
        out.append(hi)
        x = x - hi
    return out


def params(limit=56):
    return pltpu.CompilerParams(vmem_limit_bytes=limit * 2**20)


def prep_kernel(heads, rows, d_ref, run_ref, cols_ref):
    run = d_ref[...]
    lane = lax.broadcasted_iota(jnp.int32, (heads, rows), 1)
    step = 1
    while step < rows:
        run = run + jnp.where(lane >= step, pltpu.roll(run, step, 1), 0.0)
        step *= 2
    enter = jnp.zeros((heads, 1), F32)
    before, after = [], []
    for i in range(rows // CHUNK):
        leave = run[:, (i + 1) * CHUNK - 1 : (i + 1) * CHUNK]
        before.append(jnp.broadcast_to(enter, (heads, CHUNK)))
        after.append(jnp.broadcast_to(leave, (heads, CHUNK)))
        enter = leave
    eq = jnp.exp(run - jnp.concatenate(before, 1))
    ek = jnp.exp(jnp.concatenate(after, 1) - run)
    run_ref[...] = run
    tall = jnp.concatenate([run, eq, ek, jnp.exp(run)], 0)
    if 4 * heads < 128:
        tall = jnp.concatenate([tall, jnp.zeros((128 - 4 * heads, rows), F32)], 0)
    cols_ref[...] = tall.T


def prepare(log_decay):
    rows, heads = log_decay.shape
    return pl.pallas_call(
        functools.partial(prep_kernel, heads, rows),
        out_shape=(
            jax.ShapeDtypeStruct((heads, rows), F32),
            jax.ShapeDtypeStruct((rows, 128), F32),
        ),
        compiler_params=params(),
        name="prepare",
    )(log_decay.T)


def local_kernel(heads, group, base, q_ref, k_ref, v_ref, run_ref, cols_ref, mixed_ref, state_ref):
    rows, width = q_ref.shape[1], q_ref.shape[2] // group
    first = base + pl.program_id(0) * group
    cols = pltpu.roll(cols_ref[...], 128 - first, 1)
    ri = lax.broadcasted_iota(jnp.int32, (CHUNK, CHUNK), 0)
    ci = lax.broadcasted_iota(jnp.int32, (CHUNK, CHUNK), 1)
    causal = ri >= ci
    for g in range(group):
        lanes = slice(g * width, (g + 1) * width)
        run_row = run_ref[pl.ds(first + g, 1), :]
        state = None
        for i in range(rows // CHUNK):
            part = slice(i * CHUNK, (i + 1) * CHUNK)
            q, k, v = q_ref[0, part, lanes], k_ref[0, part, lanes], v_ref[0, part, lanes]
            run_col = cols[part, g : g + 1]
            eq = cols[part, heads + g : heads + g + 1]
            ek = cols[part, 2 * heads + g : 2 * heads + g + 1]
            scores = lax.dot_general(q, k, NT, preferred_element_type=F32)
            decay = jnp.exp(jnp.where(causal, run_col - run_row[:, part], -jnp.inf))
            weights = (scores * decay).astype(BF16)
            out = lax.dot_general(weights, v, NN, preferred_element_type=F32)
            faded = (k.astype(F32) * ek).astype(BF16)
            fresh = lax.dot_general(faded, v, TN, preferred_element_type=F32)
            if state is None:
                state = fresh
            else:
                out = out + eq * lax.dot_general(
                    q, state.astype(BF16), NN, preferred_element_type=F32
                )
                state = eq[CHUNK - 1 :, :] * state + fresh
            mixed_ref[part, lanes] = out.astype(mixed_ref.dtype)
        state_ref[g] = state.astype(BF16)


def local_pass(qkv, run, cols, heads, base, count, group=2):
    rows, width = qkv.shape[1], qkv.shape[2] // heads
    start = base // group

    def take(which):
        return pl.BlockSpec((1, rows, group * width), lambda h: (which, 0, start + h))

    return pl.pallas_call(
        functools.partial(local_kernel, heads, group, base),
        grid=(count // group,),
        in_specs=[
            take(0),
            take(1),
            take(2),
            pl.BlockSpec(run.shape, lambda h: (0, 0)),
            pl.BlockSpec(cols.shape, lambda h: (0, 0)),
        ],
        out_specs=(
            pl.BlockSpec((rows, group * width), lambda h: (0, h)),
            pl.BlockSpec((group, width, width), lambda h: (h, 0, 0)),
        ),
        out_shape=(
            jax.ShapeDtypeStruct((rows, count * width), F32),
            jax.ShapeDtypeStruct((count, width, width), BF16),
        ),
        compiler_params=params(),
        cost_estimate=pl.CostEstimate(
            flops=8 * count * rows * width * CHUNK,
            bytes_accessed=count * rows * width * 10,
            transcendentals=count * rows * CHUNK,
        ),
        name="local_pass",
    )(qkv, qkv, qkv, run, cols)


def final_kernel(heads, group, base, q_ref, mixed_ref, cols_ref, carried_ref, gain_ref, out_ref):
    width = q_ref.shape[2] // group
    first = base + pl.program_id(0) * group
    cols = pltpu.roll(cols_ref[...], 128 - first, 1)
    for g in range(group):
        lanes = slice(g * width, (g + 1) * width)
        er = cols[:, 3 * heads + g : 3 * heads + g + 1]
        far = lax.dot_general(q_ref[0, :, lanes], carried_ref[g], NN, preferred_element_type=F32)
        mixed = mixed_ref[:, lanes] + er * far
        mean = jnp.mean(mixed * mixed, axis=-1, keepdims=True)
        out_ref[:, lanes] = (mixed * lax.rsqrt(mean + EPS) * gain_ref[:, lanes]).astype(BF16)


def final_pass(qkv, mixed, cols, carried, gain, heads, group=2):
    rows, width = qkv.shape[1], qkv.shape[2] // heads
    return pl.pallas_call(
        functools.partial(final_kernel, heads, group, 0),
        grid=(heads // group,),
        in_specs=[
            pl.BlockSpec((1, rows, group * width), lambda h: (0, 0, h)),
            pl.BlockSpec((rows, group * width), lambda h: (0, h)),
            pl.BlockSpec(cols.shape, lambda h: (0, 0)),
            pl.BlockSpec((group, width, width), lambda h: (h, 0, 0)),
            pl.BlockSpec((1, group * width), lambda h: (0, h)),
        ],
        out_specs=pl.BlockSpec((rows, group * width), lambda h: (0, h)),
        out_shape=jax.ShapeDtypeStruct((rows, heads * width), BF16),
        compiler_params=params(),
        cost_estimate=pl.CostEstimate(
            flops=2 * heads * rows * width * width,
            bytes_accessed=heads * rows * width * 8,
            transcendentals=0,
        ),
        name="final_pass",
    )(qkv, mixed, cols, carried, gain)


def carry_scan(state, last, z_axis, y_axis):
    heads, width = state.shape[0], state.shape[1]
    ny, y = y_axis.n, y_axis.index()
    share = heads // ny
    pad = 16

    def packed(k):
        at = ((y + k) % ny) * share
        body = lax.dynamic_slice_in_dim(state, at, share, 0).reshape(share * width, width)
        fade = jnp.exp(lax.dynamic_slice_in_dim(last, at, share, 0))
        rows = jnp.stack(pieces_of(fade), 0)
        rows = jnp.pad(rows, ((0, pad - PIECES), (0, width - share)))
        return jnp.concatenate([body, rows.astype(BF16)], 0)

    got = [packed(0)] + [y_axis.send(packed(k), k) for k in range(1, ny)]
    states = [g[: share * width].reshape(share, width, width).astype(F32) for g in got]
    fades = [jnp.sum(g[share * width :, :share].astype(F32), 0) for g in got]
    places = [(y - k) % ny for k in range(ny)]

    def reach(k, end):
        r = jnp.where(places[k] < end, 1.0, 0.0) * jnp.ones((share,), F32)
        for m in range(ny):
            if m != k:
                r = r * jnp.where((places[m] > places[k]) & (places[m] < end), fades[m], 1.0)
        return r[:, None, None]

    def whole(end):
        r = jnp.ones((share,), F32)
        for m in range(ny):
            r = r * jnp.where(places[m] < end, fades[m], 1.0)
        return r[:, None, None]

    inner = sum(reach(k, ny) * states[k] for k in range(ny))
    through = whole(ny)
    carried = jnp.zeros((share, width, width), F32)
    for i in range(z_axis.n - 1):
        out = (through * carried + inner).astype(BF16)
        carried = carried + lax.ppermute(out, z_axis.name, z_axis.hop(i)).astype(F32)

    def entering(j):
        end = (y + j) % ny
        return (
            whole(end) * carried + sum(reach(k, end) * states[k] for k in range(ny))
        ).astype(BF16)

    back = [entering(0)] + [y_axis.send(entering(j), j) for j in range(1, ny)]
    both = jnp.stack(back, 0)
    order = [(y - p) % ny for p in range(ny)]
    return jnp.concatenate([lax.dynamic_index_in_dim(both, o, 0, False) for o in order], 0)


def hidden_kernel(steps, split, *refs):
    xs, w_ref, h_ref, gate, up = refs[:4], refs[4], refs[5], refs[6], refs[7]
    step = pl.program_id(0)

    @pl.when(step == 0)
    def _():
        gate[...] = jnp.zeros_like(gate)
        up[...] = jnp.zeros_like(up)

    def add(pair):
        x = jnp.concatenate([pair[0][...], pair[1][...]], 0)
        gate[...] += lax.dot_general(w_ref[0], x, NT, preferred_element_type=F32)
        up[...] += lax.dot_general(w_ref[1], x, NT, preferred_element_type=F32)

    pl.when(step < split)(lambda: add(xs[:2]))
    pl.when(step >= split)(lambda: add(xs[2:]))

    @pl.when(step == steps - 1)
    def _():
        g = gate[...]
        h_ref[...] = (g / (1.0 + jnp.exp(-g)) * up[...]).T.astype(BF16)


def hidden_pass(xs, w_in, block=1024):
    units, wide = w_in.shape[1], w_in.shape[2]
    tokens = xs[0].shape[0] * 2
    steps = wide // block
    split = steps // 2
    half = tokens // 2
    first = pl.BlockSpec((half, block), lambda s: (0, jnp.minimum(s, split - 1)))
    second = pl.BlockSpec((half, block), lambda s: (0, jnp.maximum(s - split, 0)))
    return pl.pallas_call(
        functools.partial(hidden_kernel, steps, split),
        grid=(steps,),
        in_specs=[first, first, second, second]
        + [pl.BlockSpec((2, units, block), lambda s: (0, 0, s))],
        out_specs=pl.BlockSpec((tokens, units), lambda s: (0, 0)),
        out_shape=jax.ShapeDtypeStruct((tokens, units), BF16),
        scratch_shapes=[pltpu.VMEM((units, tokens), F32), pltpu.VMEM((units, tokens), F32)],
        compiler_params=params(),
        cost_estimate=pl.CostEstimate(
            flops=4 * units * wide * tokens,
            bytes_accessed=4 * units * wide + 2 * tokens * wide,
            transcendentals=units * tokens,
        ),
        name="hidden_pass",
    )(*xs, w_in)


def down_kernel(h_ref, w_ref, p0_ref, p1_ref, o0_ref, o1_ref):
    half = o0_ref.shape[0]
    out = lax.dot_general(h_ref[...], w_ref[...], NN, preferred_element_type=F32)
    o0_ref[...] = (out[:half] * p0_ref[...]).astype(BF16)
    o1_ref[...] = (out[half:] * p1_ref[...]).astype(BF16)


def down_pass(h, w_out, probs, start, width, block=1024):
    tokens, units = h.shape
    half = tokens // 2
    off = start // block
    out = jax.ShapeDtypeStruct((half, width), BF16)
    spec = pl.BlockSpec((half, block), lambda s: (0, s))
    weight = pl.BlockSpec((half, 1), lambda s: (0, 0))
    return pl.pallas_call(
        down_kernel,
        grid=(width // block,),
        in_specs=[
            pl.BlockSpec((tokens, units), lambda s: (0, 0)),
            pl.BlockSpec((units, block), lambda s: (0, off + s)),
            weight,
            weight,
        ],
        out_specs=(spec, spec),
        out_shape=(out, out),
        compiler_params=params(),
        cost_estimate=pl.CostEstimate(
            flops=2 * units * width * tokens,
            bytes_accessed=2 * units * width + 2 * tokens * width,
            transcendentals=0,
        ),
        name="down_pass",
    )(h, w_out, *probs)


def experts_layer(tokens, ids, probs, w_in, w_out, axes):
    x_axis, core, z_axis, y_axis = axes
    count, wide = tokens.shape
    experts = w_in.shape[0] * lax.axis_size("exp")
    units = w_in.shape[3]
    half = wide // 2
    named = ids[:, :, None] == jnp.arange(experts, dtype=jnp.int32)[None, None]
    weight = jnp.sum(jnp.where(named, probs[:, :, None], 0.0), axis=1)
    route = jnp.concatenate(pieces_of(weight), 1)
    route = jnp.pad(route, ((0, 0), (0, 128 - route.shape[1]))).astype(BF16)
    z = gather(z_axis, jnp.concatenate([tokens, route], 1))
    a, b = z[:, :half], z[:, half:]
    a, b = gather(y_axis, a), gather(x_axis, b)
    a, b = gather(x_axis, a), gather(y_axis, b)
    nx, ny = x_axis.n, y_axis.n
    b = b.reshape(ny, nx, -1, b.shape[1]).transpose(1, 0, 2, 3).reshape(b.shape)
    a2, b2 = core.send(a, 1), core.send(b, 1)
    own = lax.axis_index("exp")

    def weights_of(rows):
        r = rows[:, half : half + PIECES * experts].astype(F32).reshape(-1, PIECES, experts)
        mine = jnp.arange(experts)[None, None] == own
        return jnp.sum(jnp.where(mine, r, 0.0), axis=(1, 2))[:, None]

    flow = (weights_of(b), weights_of(b2))
    h = hidden_pass((a, a2, b, b2), w_in[0].transpose(1, 2, 0))
    pa = down_pass(h, w_out[0], flow, 0, half)
    pb = down_pass(h, w_out[0], flow, half, half)
    a = scatter(core, pa)
    b = scatter(core, pb)
    b = b.reshape(nx, ny, -1, half).transpose(1, 0, 2, 3).reshape(b.shape)
    a, b = scatter(x_axis, rows_split(a, nx)), scatter(y_axis, rows_split(b, ny))
    a, b = scatter(y_axis, rows_split(a, ny)), scatter(x_axis, rows_split(b, nx))
    return scatter(z_axis, rows_split(jnp.concatenate([a, b], 1), z_axis.n))


def on_device(axes, projected, log_decay, norm_gain, moe_tokens, expert_ids, route_probs, w_in, w_out):
    x_axis, core, z_axis, y_axis = axes
    heads = log_decay.shape[1]
    qkv = projected.transpose(1, 0, 2)
    run, cols = prepare(log_decay)
    mixed, state = local_pass(qkv, run, cols, heads, 0, heads)
    moe_out = experts_layer(moe_tokens, expert_ids, route_probs, w_in, w_out, axes)
    carried = carry_scan(state, run[:, -1], z_axis, y_axis)
    attn_out = final_pass(qkv, mixed, cols, carried, norm_gain[None], heads)
    return attn_out, moe_out


def solution(mesh):
    nz, ny = factors(mesh.shape["seq"])
    nx = mesh.shape["exp"] // 2
    axes = (
        Axis("exp", nx, 2, 1),
        Axis("exp", 2, 1, nx),
        Axis("seq", nz, ny, 1),
        Axis("seq", ny, 1, nz),
    )
    in_specs = (
        P("seq", None, "exp"),
        P("seq", "exp"),
        P("exp"),
        P(("seq", "exp"), None),
        P(("seq", "exp"), None),
        P(("seq", "exp"), None),
        P("exp", None, None, "seq"),
        P("exp", "seq", None),
    )
    out_specs = (P("seq", "exp"), P(("seq", "exp"), None))
    return jax.shard_map(
        functools.partial(on_device, axes),
        mesh=mesh,
        in_specs=in_specs,
        out_specs=out_specs,
        check_vma=False,
    )
```

```python
import functools
import jax
import jax.numpy as jnp
from jax import lax
from jax.experimental import pallas as pl
from jax.experimental.pallas import tpu as pltpu
from jax.sharding import PartitionSpec as P

EPS = 1e-06
CHUNK = 256
PARTS = 4
PIECES = 3
F32 = jnp.float32
BF16 = jnp.bfloat16
NT = (((1,), (1,)), ((), ()))
TN = (((0,), (0,)), ((), ()))
NN = (((1,), (0,)), ((), ()))


def factors(size):
    bits = size.bit_length() - 1
    inner = 2 ** (bits // 2)
    return size // inner, inner


class Axis:
    def __init__(self, name, n, inner, outer):
        self.name, self.n, self.inner, self.outer = name, n, inner, outer

    def index(self):
        return (lax.axis_index(self.name) // self.inner) % self.n

    def flat(self, o, i, j):
        return (o * self.n + i) * self.inner + j

    def turn(self, k):
        return [
            (self.flat(o, i, j), self.flat(o, (i + k) % self.n, j))
            for o in range(self.outer)
            for i in range(self.n)
            for j in range(self.inner)
        ]

    def hop(self, i):
        return [
            (self.flat(o, i, j), self.flat(o, i + 1, j))
            for o in range(self.outer)
            for j in range(self.inner)
        ]

    def send(self, a, k):
        return lax.ppermute(a, self.name, self.turn(k))


def gather(axis, a):
    return jnp.concatenate([a] + [axis.send(a, k) for k in range(1, axis.n)], 0)


def total(parts):
    s = parts[0].astype(F32)
    for p in parts[1:]:
        s = s + p.astype(F32)
    return s.astype(BF16)


def scatter(axis, parts):
    return total([parts[0]] + [axis.send(parts[k], axis.n - k) for k in range(1, axis.n)])


def rows_split(a, n):
    m = a.shape[0] // n
    return [a[i * m : (i + 1) * m] for i in range(n)]


def pieces_of(x):
    out = []
    for _ in range(PIECES):
        hi = lax.reduce_precision(x, 8, 7)
        out.append(hi)
        x = x - hi
    return out


def params(limit=16):
    return pltpu.CompilerParams(vmem_limit_bytes=limit * 2**20)


def prep_kernel(heads, rows, d_ref, run_ref, cols_ref):
    run = d_ref[...]
    lane = lax.broadcasted_iota(jnp.int32, (heads, rows), 1)
    step = 1
    while step < rows:
        run = run + jnp.where(lane >= step, pltpu.roll(run, step, 1), 0.0)
        step *= 2
    enter = jnp.zeros((heads, 1), F32)
    before, after = [], []
    for i in range(rows // CHUNK):
        leave = run[:, (i + 1) * CHUNK - 1 : (i + 1) * CHUNK]
        before.append(jnp.broadcast_to(enter, (heads, CHUNK)))
        after.append(jnp.broadcast_to(leave, (heads, CHUNK)))
        enter = leave
    eq = jnp.exp(run - jnp.concatenate(before, 1))
    ek = jnp.exp(jnp.concatenate(after, 1) - run)
    run_ref[...] = run
    tall = jnp.concatenate([run, eq, ek, jnp.exp(run)], 0)
    if 4 * heads < 128:
        tall = jnp.concatenate([tall, jnp.zeros((128 - 4 * heads, rows), F32)], 0)
    cols_ref[...] = tall.T


def prepare(log_decay):
    rows, heads = log_decay.shape
    return pl.pallas_call(
        functools.partial(prep_kernel, heads, rows),
        out_shape=(
            jax.ShapeDtypeStruct((heads, rows), F32),
            jax.ShapeDtypeStruct((rows, 128), F32),
        ),
        compiler_params=params(),
        name="prepare",
    )(log_decay.T)


def local_kernel(heads, group, base, *refs):
    q_ref, k_ref, v_ref, run_ref, cols_ref = refs[:5]
    mixed_ref, state_ref = refs[-2:]
    rows, width = q_ref.shape[1], q_ref.shape[2] // group
    first = base + pl.program_id(0) * group
    cols = pltpu.roll(cols_ref[...], 128 - first, 1)
    ri = lax.broadcasted_iota(jnp.int32, (CHUNK, CHUNK), 0)
    ci = lax.broadcasted_iota(jnp.int32, (CHUNK, CHUNK), 1)
    causal = ri >= ci
    for g in range(group):
        lanes = slice(g * width, (g + 1) * width)
        run_row = run_ref[pl.ds(first + g, 1), :]
        state = None
        for i in range(rows // CHUNK):
            part = slice(i * CHUNK, (i + 1) * CHUNK)
            q, k, v = q_ref[0, part, lanes], k_ref[0, part, lanes], v_ref[0, part, lanes]
            run_col = cols[part, g : g + 1]
            eq = cols[part, heads + g : heads + g + 1]
            ek = cols[part, 2 * heads + g : 2 * heads + g + 1]
            scores = lax.dot_general(q, k, NT, preferred_element_type=F32)
            decay = jnp.exp(jnp.where(causal, run_col - run_row[:, part], -jnp.inf))
            weights = (scores * decay).astype(BF16)
            out = lax.dot_general(weights, v, NN, preferred_element_type=F32)
            faded = (k.astype(F32) * ek).astype(BF16)
            fresh = lax.dot_general(faded, v, TN, preferred_element_type=F32)
            if state is None:
                state = fresh
            else:
                out = out + eq * lax.dot_general(
                    q, state.astype(BF16), NN, preferred_element_type=F32
                )
                state = eq[CHUNK - 1 :, :] * state + fresh
            mixed_ref[part, lanes] = out.astype(mixed_ref.dtype)
        state_ref[g] = state.astype(BF16)


def local_pass(qkv, run, cols, heads, base, count, behind, group=4):
    rows, width = qkv.shape[1], qkv.shape[2] // heads
    group = min(group, count)
    start = base // group

    def take(which):
        return pl.BlockSpec((1, rows, group * width), lambda h: (which, 0, start + h))

    return pl.pallas_call(
        functools.partial(local_kernel, heads, group, base),
        grid=(count // group,),
        in_specs=[
            take(0),
            take(1),
            take(2),
            pl.BlockSpec(run.shape, lambda h: (0, 0)),
            pl.BlockSpec(cols.shape, lambda h: (0, 0)),
        ]
        + [pl.BlockSpec(memory_space=pl.ANY)] * len(behind),
        out_specs=(
            pl.BlockSpec((rows, group * width), lambda h: (0, h)),
            pl.BlockSpec((group, width, width), lambda h: (h, 0, 0)),
        ),
        out_shape=(
            jax.ShapeDtypeStruct((rows, count * width), BF16),
            jax.ShapeDtypeStruct((count, width, width), BF16),
        ),
        compiler_params=params(56),
        cost_estimate=pl.CostEstimate(
            flops=8 * count * rows * width * CHUNK,
            bytes_accessed=count * rows * width * 8,
            transcendentals=count * rows * CHUNK,
        ),
        name="local_pass",
    )(qkv, qkv, qkv, run, cols, *behind)


def final_kernel(heads, group, base, *refs):
    q_ref, mixed_ref, cols_ref, carried_ref, gain_ref = refs[:5]
    out_ref, mark_ref = refs[-2:]
    mark_ref[...] = jnp.zeros_like(mark_ref)
    width = q_ref.shape[2] // group
    first = base + pl.program_id(0) * group
    cols = pltpu.roll(cols_ref[...], 128 - first, 1)
    for g in range(group):
        lanes = slice(g * width, (g + 1) * width)
        er = cols[:, 3 * heads + g : 3 * heads + g + 1]
        far = lax.dot_general(q_ref[0, :, lanes], carried_ref[g], NN, preferred_element_type=F32)
        mixed = mixed_ref[:, lanes].astype(F32) + er * far
        mean = jnp.mean(mixed * mixed, axis=-1, keepdims=True)
        out_ref[:, lanes] = (mixed * lax.rsqrt(mean + EPS) * gain_ref[:, lanes]).astype(BF16)


def final_pass(qkv, mixed, cols, carried, gain, heads, base, count, done, behind, group=4):
    rows, width = qkv.shape[1], qkv.shape[2] // heads
    group = min(group, count)
    start = base // group
    args = [qkv, mixed, cols, carried, gain]
    specs = [
        pl.BlockSpec((1, rows, group * width), lambda h: (0, 0, start + h)),
        pl.BlockSpec((rows, group * width), lambda h: (0, h)),
        pl.BlockSpec(cols.shape, lambda h: (0, 0)),
        pl.BlockSpec((group, width, width), lambda h: (start + h, 0, 0)),
        pl.BlockSpec((1, group * width), lambda h: (0, start + h)),
    ]
    more = ([] if done is None else [done]) + list(behind)
    args += more
    specs += [pl.BlockSpec(memory_space=pl.ANY)] * len(more)
    return pl.pallas_call(
        functools.partial(final_kernel, heads, group, base),
        grid=(count // group,),
        in_specs=specs,
        out_specs=(
            pl.BlockSpec((rows, group * width), lambda h: (0, start + h)),
            pl.BlockSpec((8, 128), lambda h: (0, 0)),
        ),
        out_shape=(
            jax.ShapeDtypeStruct((rows, heads * width), BF16),
            jax.ShapeDtypeStruct((8, 128), F32),
        ),
        input_output_aliases={} if done is None else {5: 0},
        compiler_params=params(56),
        cost_estimate=pl.CostEstimate(
            flops=2 * count * rows * width * width,
            bytes_accessed=count * rows * width * 6,
            transcendentals=0,
        ),
        name="final_pass",
    )(*args)


def carry_scan(state, last, z_axis, y_axis):
    heads, width = state.shape[0], state.shape[1]
    ny, y = y_axis.n, y_axis.index()
    share = heads // ny
    pad = 16

    def packed(k):
        at = ((y + k) % ny) * share
        body = lax.dynamic_slice_in_dim(state, at, share, 0).reshape(share * width, width)
        fade = jnp.exp(lax.dynamic_slice_in_dim(last, at, share, 0))
        rows = jnp.stack(pieces_of(fade), 0)
        rows = jnp.pad(rows, ((0, pad - PIECES), (0, width - share)))
        return jnp.concatenate([body, rows.astype(BF16)], 0)

    got = [packed(0)] + [y_axis.send(packed(k), k) for k in range(1, ny)]
    states = [g[: share * width].reshape(share, width, width).astype(F32) for g in got]
    fades = [jnp.sum(g[share * width :, :share].astype(F32), 0) for g in got]
    places = [(y - k) % ny for k in range(ny)]

    def reach(k, end):
        r = jnp.where(places[k] < end, 1.0, 0.0) * jnp.ones((share,), F32)
        for m in range(ny):
            if m != k:
                r = r * jnp.where((places[m] > places[k]) & (places[m] < end), fades[m], 1.0)
        return r[:, None, None]

    def whole(end):
        r = jnp.ones((share,), F32)
        for m in range(ny):
            r = r * jnp.where(places[m] < end, fades[m], 1.0)
        return r[:, None, None]

    inner = sum(reach(k, ny) * states[k] for k in range(ny))
    through = whole(ny)
    carried = jnp.zeros((share, width, width), F32)
    for i in range(z_axis.n - 1):
        out = (through * carried + inner).astype(BF16)
        carried = carried + lax.ppermute(out, z_axis.name, z_axis.hop(i)).astype(F32)

    def entering(j):
        end = (y + j) % ny
        return (
            whole(end) * carried + sum(reach(k, end) * states[k] for k in range(ny))
        ).astype(BF16)

    back = [entering(0)] + [y_axis.send(entering(j), j) for j in range(1, ny)]
    both = jnp.stack(back, 0)
    order = [(y - p) % ny for p in range(ny)]
    return jnp.concatenate([lax.dynamic_index_in_dim(both, o, 0, False) for o in order], 0)


def hidden_kernel(steps, split, *refs):
    xs, w_ref, h_ref, gate, up = refs[:4], refs[4], refs[5], refs[6], refs[7]
    step = pl.program_id(0)

    @pl.when(step == 0)
    def _():
        gate[...] = jnp.zeros_like(gate)
        up[...] = jnp.zeros_like(up)

    def add(pair):
        x = jnp.concatenate([pair[0][...], pair[1][...]], 0)
        gate[...] += lax.dot_general(w_ref[0], x, NT, preferred_element_type=F32)
        up[...] += lax.dot_general(w_ref[1], x, NT, preferred_element_type=F32)

    pl.when(step < split)(lambda: add(xs[:2]))
    pl.when(step >= split)(lambda: add(xs[2:]))

    @pl.when(step == steps - 1)
    def _():
        g = gate[...]
        h_ref[...] = (g / (1.0 + jnp.exp(-g)) * up[...]).T.astype(BF16)


def hidden_pass(xs, w_in, block=1024):
    units, wide = w_in.shape[1], w_in.shape[2]
    tokens = xs[0].shape[0] * 2
    steps = wide // block
    split = steps // 2
    half = tokens // 2
    first = pl.BlockSpec((half, block), lambda s: (0, jnp.minimum(s, split - 1)))
    second = pl.BlockSpec((half, block), lambda s: (0, jnp.maximum(s - split, 0)))
    return pl.pallas_call(
        functools.partial(hidden_kernel, steps, split),
        grid=(steps,),
        in_specs=[first, first, second, second]
        + [pl.BlockSpec((2, units, block), lambda s: (0, 0, s))],
        out_specs=pl.BlockSpec((tokens, units), lambda s: (0, 0)),
        out_shape=jax.ShapeDtypeStruct((tokens, units), BF16),
        scratch_shapes=[pltpu.VMEM((units, tokens), F32), pltpu.VMEM((units, tokens), F32)],
        compiler_params=params(56),
        cost_estimate=pl.CostEstimate(
            flops=4 * units * wide * tokens,
            bytes_accessed=4 * units * wide + 2 * tokens * wide,
            transcendentals=units * tokens,
        ),
        name="hidden_pass",
    )(*xs, w_in)


def down_kernel(h_ref, w_ref, p0_ref, p1_ref, o0_ref, o1_ref):
    half = o0_ref.shape[0]
    out = lax.dot_general(h_ref[...], w_ref[...], NN, preferred_element_type=F32)
    o0_ref[...] = (out[:half] * p0_ref[...]).astype(BF16)
    o1_ref[...] = (out[half:] * p1_ref[...]).astype(BF16)


def down_pass(h, w_out, probs, start, width, block=1024):
    tokens, units = h.shape
    half = tokens // 2
    off = start // block
    out = jax.ShapeDtypeStruct((half, width), BF16)
    spec = pl.BlockSpec((half, block), lambda s: (0, s))
    weight = pl.BlockSpec((half, 1), lambda s: (0, 0))
    return pl.pallas_call(
        down_kernel,
        grid=(width // block,),
        in_specs=[
            pl.BlockSpec((tokens, units), lambda s: (0, 0)),
            pl.BlockSpec((units, block), lambda s: (0, off + s)),
            weight,
            weight,
        ],
        out_specs=(spec, spec),
        out_shape=(out, out),
        compiler_params=params(56),
        cost_estimate=pl.CostEstimate(
            flops=2 * units * width * tokens,
            bytes_accessed=2 * units * width + 2 * tokens * width,
            transcendentals=0,
        ),
        name="down_pass",
    )(h, w_out, *probs)


def ordered(ref, lanes, outer, inner):
    m = ref.shape[0] // (outer * inner)
    blocks = [(i * outer + o) * m for o in range(outer) for i in range(inner)]
    return jnp.concatenate([ref[at : at + m, lanes] for at in blocks], 0)


def store_ordered(ref, lanes, value, outer, inner):
    m = ref.shape[0] // (outer * inner)
    for o in range(outer):
        for i in range(inner):
            src, dst = (o * inner + i) * m, (i * outer + o) * m
            ref[dst : dst + m, lanes] = value[src : src + m]


def own_weights(ref, lanes, experts, outer, inner):
    r = ordered(ref, lanes, outer, inner).astype(F32)
    lane = lax.broadcasted_iota(jnp.int32, r.shape, 1)
    mine = (lane % experts == lax.axis_index("exp")) & (lane < PIECES * experts)
    return jnp.sum(jnp.where(mine, r, 0.0), axis=1, keepdims=True)


class Stream:
    def __init__(self, copies, depth):
        self.copies, self.depth, self.at = copies, depth, 0
        for c in copies[:depth]:
            c.start()

    def next(self):
        self.copies[self.at].wait()
        ahead = self.at + self.depth
        if ahead < len(self.copies):
            self.copies[ahead].start()
        self.at += 1


def chunks(w, scratch, sems, start, width, block, first):
    out = []
    for j, at in enumerate(range(0, width, block)):
        src = w.at[(slice(None),) * (len(w.shape) - 1) + (pl.ds(start + at, block),)]
        out.append(pltpu.make_async_copy(src, scratch.at[j], sems.at[first + j]))
    return out


def lead_kernel(experts, nx, ny, block, depth, a, a2, b, b2, w_in, w_out, o, o2, h, flow, acc, wi, wo, sems):
    units, wide = w_in.shape[1], w_in.shape[2]
    half = wide // 2
    rows = a.shape[0]
    copies = chunks(w_in, wi, sems, 0, wide, block, 0)
    copies += chunks(w_out, wo, sems, 0, half, block, len(copies))
    stream = Stream(copies, depth)
    lanes = slice(half, half + 128)
    flow[:rows] = jnp.broadcast_to(own_weights(b, lanes, experts, nx, ny), (rows, 128))
    flow[rows:] = jnp.broadcast_to(own_weights(b2, lanes, experts, nx, ny), (rows, 128))
    for j, at in enumerate(range(0, wide, block)):
        stream.next()
        if at < half:
            x = jnp.concatenate([a[:, at : at + block], a2[:, at : at + block]], 0)
        else:
            lanes = slice(at - half, at - half + block)
            x = jnp.concatenate([ordered(b, lanes, nx, ny), ordered(b2, lanes, nx, ny)], 0)
        w = wi[j].reshape(2 * units, block)
        d = lax.dot_general(w, x, NT, preferred_element_type=F32)
        if at == 0:
            acc[...] = d
        else:
            acc[...] += d
    g = acc[:units]
    h[...] = (g / (1.0 + jnp.exp(-g)) * acc[units:]).T.astype(BF16)
    for j, at in enumerate(range(0, half, block)):
        stream.next()
        lanes = slice(at, at + block)
        d = lax.dot_general(h[...], wo[j], NN, preferred_element_type=F32)
        d = (d * flow[:, :1]).astype(BF16)
        o[:, lanes] = d[:rows]
        o2[:, lanes] = d[rows:]


def rest_kernel(nx, ny, block, depth, h, flow, w_out, o, o2, wo, sems):
    half = w_out.shape[1] // 2
    rows = o.shape[0]
    stream = Stream(chunks(w_out, wo, sems, half, half, block, 0), depth)
    for j, at in enumerate(range(0, half, block)):
        stream.next()
        lanes = slice(at, at + block)
        d = lax.dot_general(h[...], wo[j], NN, preferred_element_type=F32)
        d = (d * flow[:, :1]).astype(BF16)
        store_ordered(o, lanes, d[:rows], nx, ny)
        store_ordered(o2, lanes, d[rows:], nx, ny)


def fitting_experts(a, a2, b, b2, w_in, w_out, experts, nx, ny, block=1024, depth=3):
    units, wide = w_in.shape[1], w_in.shape[2]
    tokens = 2 * a.shape[0]
    n_in, n_out = wide // block, wide // 2 // block
    vmem = pl.BlockSpec(memory_space=pltpu.VMEM)
    hbm = pl.BlockSpec(memory_space=pl.ANY)
    half = jax.ShapeDtypeStruct((tokens // 2, wide // 2), BF16)
    o, o2, h, flow = pl.pallas_call(
        functools.partial(lead_kernel, experts, nx, ny, block, depth),
        in_specs=[vmem] * 4 + [hbm] * 2,
        out_specs=(vmem,) * 4,
        out_shape=(
            half,
            half,
            jax.ShapeDtypeStruct((tokens, units), BF16),
            jax.ShapeDtypeStruct((tokens, 128), F32),
        ),
        scratch_shapes=[
            pltpu.VMEM((2 * units, tokens), F32),
            pltpu.VMEM((n_in, 2, units, block), BF16),
            pltpu.VMEM((n_out, units, block), BF16),
            pltpu.SemaphoreType.DMA((n_in + n_out,)),
        ],
        compiler_params=params(44),
        cost_estimate=pl.CostEstimate(
            flops=5 * units * wide * tokens,
            bytes_accessed=5 * units * wide + 3 * tokens * wide,
            transcendentals=units * tokens,
        ),
        name="lead_pass",
    )(a, a2, b, b2, w_in, w_out)
    p, p2 = pl.pallas_call(
        functools.partial(rest_kernel, nx, ny, block, depth),
        in_specs=[vmem] * 2 + [hbm],
        out_specs=(vmem,) * 2,
        out_shape=(half, half),
        scratch_shapes=[
            pltpu.VMEM((n_out, units, block), BF16),
            pltpu.SemaphoreType.DMA((n_out,)),
        ],
        compiler_params=params(58),
        cost_estimate=pl.CostEstimate(
            flops=units * wide * tokens,
            bytes_accessed=units * wide + tokens * wide,
            transcendentals=0,
        ),
        name="rest_pass",
    )(h, flow, w_out)
    return (o, o2), (p, p2)


def streamed_experts(a, a2, b, b2, w_in, w_out, experts, nx, ny):
    half = a.shape[1]

    def turned(r, m, n):
        return r.reshape(m, n, -1, r.shape[1]).transpose(1, 0, 2, 3).reshape(r.shape)

    b, b2 = turned(b, ny, nx), turned(b2, ny, nx)

    def weights_of(rows):
        r = rows[:, half : half + PIECES * experts].astype(F32).reshape(-1, PIECES, experts)
        mine = jnp.arange(experts)[None, None] == lax.axis_index("exp")
        return jnp.sum(jnp.where(mine, r, 0.0), axis=(1, 2))[:, None]

    flow = (weights_of(b), weights_of(b2))
    h = hidden_pass((a, a2, b, b2), w_in)
    pa = down_pass(h, w_out, flow, 0, half)
    pb = down_pass(h, w_out, flow, half, half)
    return pa, tuple(turned(p, nx, ny) for p in pb)


def route_columns(ids, probs, experts):
    named = ids[:, :, None] == jnp.arange(experts, dtype=jnp.int32)[None, None]
    weight = jnp.sum(jnp.where(named, probs[:, :, None], 0.0), axis=1)
    route = jnp.concatenate(pieces_of(weight), 1)
    return jnp.pad(route, ((0, 0), (0, 128 - route.shape[1]))).astype(BF16)


def nothing(a):
    probe = a[-1, 0].astype(F32)
    return jnp.where(probe != probe, 1.0, 0.0)


def on_device(axes, projected, log_decay, norm_gain, moe_tokens, expert_ids, route_probs, w_in, w_out):
    x_axis, core, z_axis, y_axis = axes
    nx, ny, nz = x_axis.n, y_axis.n, z_axis.n
    heads = log_decay.shape[1]
    half = moe_tokens.shape[1] // 2
    experts = w_in.shape[0] * lax.axis_size("exp")
    count = heads // min(PARTS, heads)
    qkv = projected.transpose(1, 0, 2)
    gain = norm_gain[None]
    route = route_columns(expert_ids, route_probs, experts)

    z = gather(z_axis, jnp.concatenate([moe_tokens, route], 1))
    run, cols = prepare(log_decay)
    local = []

    def local_part(*behind):
        local.append(local_pass(qkv, run, cols, heads, len(local) * count, count, behind))

    while len(local) < heads // count // 2:
        local_part()
    while len(local) < heads // count:
        local_part(z)
    a, b = z[:, :half], z[:, half:]
    a, b = first = gather(y_axis, a), gather(x_axis, b)
    a, b = gather(x_axis, a), gather(y_axis, b)
    last = run[:, -1] + nothing(first[0]) + nothing(first[1])
    a2, b2 = core.send(a, 1), core.send(b, 1)
    state = jnp.concatenate([s for _, s in local], 0)
    carried = carry_scan(state, last, z_axis, y_axis)
    apply = fitting_experts if 2 * a.shape[0] <= 512 else streamed_experts
    pa, pb = apply(a, a2, b, b2, w_in[0].transpose(1, 2, 0), w_out[0], experts, nx, ny)

    a, b = scatter(core, pa), scatter(core, pb)
    attn_out, marks = None, []

    def final_parts(upto, *behind):
        nonlocal attn_out
        for i in range(len(marks), upto):
            attn_out, mark = final_pass(
                qkv, local[i][0], cols, carried, gain, heads, i * count, count, attn_out, behind
            )
            marks.append(mark)
        return marks[-1][0, 0].astype(BF16)

    parts = heads // count
    zero = final_parts(parts // 2, a, b)
    a, b = scatter(x_axis, rows_split(a, nx)), scatter(y_axis, rows_split(b, ny))
    a, b = a + zero, b + zero
    zero = final_parts(3 * parts // 4, a, b)
    a, b = scatter(y_axis, rows_split(a, ny)), scatter(x_axis, rows_split(b, nx))
    both = jnp.concatenate([a, b], 1) + zero
    final_parts(parts, both)
    moe_out = scatter(z_axis, rows_split(both, nz))
    return attn_out, moe_out


def solution(mesh):
    nz, ny = factors(mesh.shape["seq"])
    nx = mesh.shape["exp"] // 2
    axes = (
        Axis("exp", nx, 2, 1),
        Axis("exp", 2, 1, nx),
        Axis("seq", nz, ny, 1),
        Axis("seq", ny, 1, nz),
    )
    in_specs = (
        P("seq", None, "exp"),
        P("seq", "exp"),
        P("exp"),
        P(("seq", "exp"), None),
        P(("seq", "exp"), None),
        P(("seq", "exp"), None),
        P("exp", None, None, "seq"),
        P("exp", "seq", None),
    )
    out_specs = (P("seq", "exp"), P(("seq", "exp"), None))
    return jax.shard_map(
        functools.partial(on_device, axes),
        mesh=mesh,
        in_specs=in_specs,
        out_specs=out_specs,
        check_vma=False,
    )
```

```python
import functools
import jax
import jax.numpy as jnp
from jax import lax
from jax.experimental import pallas as pl
from jax.experimental.pallas import tpu as pltpu
from jax.sharding import PartitionSpec as P

EPS = 1e-06
CHUNK = 256
PARTS = 2
PIECES = 3
F32 = jnp.float32
BF16 = jnp.bfloat16
NT = (((1,), (1,)), ((), ()))
TN = (((0,), (0,)), ((), ()))
NN = (((1,), (0,)), ((), ()))


def factors(size):
    bits = size.bit_length() - 1
    inner = 2 ** (bits // 2)
    return size // inner, inner


class Axis:
    def __init__(self, name, n, inner, outer):
        self.name, self.n, self.inner, self.outer = name, n, inner, outer

    def index(self):
        return (lax.axis_index(self.name) // self.inner) % self.n

    def flat(self, o, i, j):
        return (o * self.n + i) * self.inner + j

    def turn(self, k):
        return [
            (self.flat(o, i, j), self.flat(o, (i + k) % self.n, j))
            for o in range(self.outer)
            for i in range(self.n)
            for j in range(self.inner)
        ]

    def hop(self, i):
        return [
            (self.flat(o, i, j), self.flat(o, i + 1, j))
            for o in range(self.outer)
            for j in range(self.inner)
        ]

    def send(self, a, k):
        return lax.ppermute(a, self.name, self.turn(k))


def gather(axis, a):
    return jnp.concatenate([a] + [axis.send(a, k) for k in range(1, axis.n)], 0)


def total(parts):
    s = parts[0].astype(F32)
    for p in parts[1:]:
        s = s + p.astype(F32)
    return s.astype(BF16)


def scatter(axis, parts):
    return total([parts[0]] + [axis.send(parts[k], axis.n - k) for k in range(1, axis.n)])


def rows_split(a, n):
    m = a.shape[0] // n
    return [a[i * m : (i + 1) * m] for i in range(n)]


def pieces_of(x):
    out = []
    for _ in range(PIECES):
        hi = lax.reduce_precision(x, 8, 7)
        out.append(hi)
        x = x - hi
    return out


def params(limit=16):
    return pltpu.CompilerParams(vmem_limit_bytes=limit * 2**20)


def prep_kernel(heads, rows, d_ref, run_ref, cols_ref, seat_ref):
    seat_ref[...] = jnp.zeros_like(seat_ref) + lax.axis_index("seq")
    run = d_ref[...]
    lane = lax.broadcasted_iota(jnp.int32, (heads, rows), 1)
    step = 1
    while step < rows:
        run = run + jnp.where(lane >= step, pltpu.roll(run, step, 1), 0.0)
        step *= 2
    enter = jnp.zeros((heads, 1), F32)
    before, after = [], []
    for i in range(rows // CHUNK):
        leave = run[:, (i + 1) * CHUNK - 1 : (i + 1) * CHUNK]
        before.append(jnp.broadcast_to(enter, (heads, CHUNK)))
        after.append(jnp.broadcast_to(leave, (heads, CHUNK)))
        enter = leave
    eq = jnp.exp(run - jnp.concatenate(before, 1))
    ek = jnp.exp(jnp.concatenate(after, 1) - run)
    run_ref[...] = run
    tall = jnp.concatenate([run, eq, ek, jnp.exp(run)], 0)
    if 4 * heads < 128:
        tall = jnp.concatenate([tall, jnp.zeros((128 - 4 * heads, rows), F32)], 0)
    cols_ref[...] = tall.T


def prepare(log_decay):
    rows, heads = log_decay.shape
    return pl.pallas_call(
        functools.partial(prep_kernel, heads, rows),
        out_shape=(
            jax.ShapeDtypeStruct((heads, rows), F32),
            jax.ShapeDtypeStruct((rows, 128), F32),
            jax.ShapeDtypeStruct((heads, 128), jnp.int32),
        ),
        compiler_params=params(),
        name="prepare",
    )(log_decay.T)


def local_kernel(heads, group, base, loads, which, *refs):
    q_ref, k_ref, v_ref, run_ref, cols_ref = refs[:5]
    mixed_ref, state_ref, mark_ref = refs[-3 - 2 * loads :][:3]
    if loads:
        w_ref, held_ref, sem = refs[5], refs[-2], refs[-1]
        copy = pltpu.make_async_copy(w_ref.at[which], held_ref, sem)
        pl.when(pl.program_id(0) == 0)(copy.start)
    mark_ref[...] = jnp.zeros_like(mark_ref)
    rows, width = q_ref.shape[1], q_ref.shape[2] // group
    first = base + pl.program_id(0) * group
    cols = pltpu.roll(cols_ref[...], 128 - first, 1)
    ri = lax.broadcasted_iota(jnp.int32, (CHUNK, CHUNK), 0)
    ci = lax.broadcasted_iota(jnp.int32, (CHUNK, CHUNK), 1)
    causal = ri >= ci
    for g in range(group):
        lanes = slice(g * width, (g + 1) * width)
        run_row = run_ref[pl.ds(first + g, 1), :]
        state = None
        for i in range(rows // CHUNK):
            part = slice(i * CHUNK, (i + 1) * CHUNK)
            q, k, v = q_ref[0, part, lanes], k_ref[0, part, lanes], v_ref[0, part, lanes]
            run_col = cols[part, g : g + 1]
            eq = cols[part, heads + g : heads + g + 1]
            ek = cols[part, 2 * heads + g : 2 * heads + g + 1]
            scores = lax.dot_general(q, k, NT, preferred_element_type=F32)
            decay = jnp.exp(jnp.where(causal, run_col - run_row[:, part], -jnp.inf))
            weights = (scores * decay).astype(BF16)
            out = lax.dot_general(weights, v, NN, preferred_element_type=F32)
            faded = (k.astype(F32) * ek).astype(BF16)
            fresh = lax.dot_general(faded, v, TN, preferred_element_type=F32)
            if state is None:
                state = fresh
            else:
                out = out + eq * lax.dot_general(
                    q, state.astype(BF16), NN, preferred_element_type=F32
                )
                state = eq[CHUNK - 1 :, :] * state + fresh
            mixed_ref[part, lanes] = out.astype(mixed_ref.dtype)
        state_ref[g] = state.astype(BF16)
    if loads:
        pl.when(pl.program_id(0) == pl.num_programs(0) - 1)(copy.wait)


def local_pass(qkv, run, cols, heads, base, count, w, done, behind, zeros, group=4):
    rows, width = qkv.shape[1], qkv.shape[2] // heads
    group = min(group, count)
    start = base // group
    loads = 0 if w is None else 1
    hbm = pl.BlockSpec(memory_space=pl.ANY)

    def take(which):
        return pl.BlockSpec((1, rows, group * width), lambda h: (which, 0, start + h))

    more = ([w] if loads else []) + list(done) + list(behind)
    aliases = {5 + loads + i: i for i in range(len(done))}
    out_specs = [
        pl.BlockSpec((rows, group * width), lambda h: (0, start + h)),
        pl.BlockSpec((group, width, width), lambda h: (start + h, 0, 0)),
        pl.BlockSpec((8, zeros), lambda h: (0, 0)),
    ]
    out_shape = [
        jax.ShapeDtypeStruct((rows, heads * width), BF16),
        jax.ShapeDtypeStruct((heads, width, width), BF16),
        jax.ShapeDtypeStruct((8, zeros), BF16),
    ]
    if loads:
        out_specs.append(hbm)
        out_shape.append(pltpu.VMEM(w.shape[1:], w.dtype))
    return pl.pallas_call(
        functools.partial(local_kernel, heads, group, base, loads, base // count),
        grid=(count // group,),
        in_specs=[
            take(0),
            take(1),
            take(2),
            pl.BlockSpec(run.shape, lambda h: (0, 0)),
            pl.BlockSpec(cols.shape, lambda h: (0, 0)),
        ]
        + [hbm] * len(more),
        out_specs=out_specs,
        out_shape=out_shape,
        scratch_shapes=[pltpu.SemaphoreType.DMA] * loads,
        input_output_aliases=aliases,
        compiler_params=params(20),
        cost_estimate=pl.CostEstimate(
            flops=8 * count * rows * width * CHUNK,
            bytes_accessed=count * rows * width * 8,
            transcendentals=count * rows * CHUNK,
        ),
        name="local_pass",
    )(qkv, qkv, qkv, run, cols, *more)


def final_kernel(heads, group, q_ref, mixed_ref, cols_ref, carried_ref, gain_ref, out_ref):
    width = q_ref.shape[2] // group
    first = pl.program_id(0) * group
    cols = pltpu.roll(cols_ref[...], 128 - first, 1)
    for g in range(group):
        lanes = slice(g * width, (g + 1) * width)
        er = cols[:, 3 * heads + g : 3 * heads + g + 1]
        far = lax.dot_general(q_ref[0, :, lanes], carried_ref[g], NN, preferred_element_type=F32)
        mixed = mixed_ref[:, lanes].astype(F32) + er * far
        mean = jnp.mean(mixed * mixed, axis=-1, keepdims=True)
        out_ref[:, lanes] = (mixed * lax.rsqrt(mean + EPS) * gain_ref[:, lanes]).astype(BF16)


def final_pass(qkv, mixed, cols, carried, gain, heads, group=4):
    rows, width = qkv.shape[1], qkv.shape[2] // heads
    group = min(group, heads)
    return pl.pallas_call(
        functools.partial(final_kernel, heads, group),
        grid=(heads // group,),
        in_specs=[
            pl.BlockSpec((1, rows, group * width), lambda h: (0, 0, h)),
            pl.BlockSpec((rows, group * width), lambda h: (0, h)),
            pl.BlockSpec(cols.shape, lambda h: (0, 0)),
            pl.BlockSpec((group, width, width), lambda h: (h, 0, 0)),
            pl.BlockSpec((1, group * width), lambda h: (0, h)),
        ],
        out_specs=pl.BlockSpec((rows, group * width), lambda h: (0, h)),
        out_shape=jax.ShapeDtypeStruct((rows, heads * width), BF16),
        compiler_params=params(20),
        cost_estimate=pl.CostEstimate(
            flops=2 * heads * rows * width * width,
            bytes_accessed=heads * rows * width * 6,
            transcendentals=0,
        ),
        name="final_pass",
    )(qkv, mixed, cols, carried, gain)


def pick(parts, at):
    out = parts[0]
    for p in range(1, len(parts)):
        out = jnp.where((at == p).reshape((-1,) + (1,) * (out.ndim - 1)), parts[p], out)
    return out


def carry_scan(state, last, seat, z_axis, y_axis):
    heads, width = state.shape[0], state.shape[1]
    ny = y_axis.n
    share = heads // ny
    pad = 16
    y = seat[:share]
    turned = [(y + k) & (ny - 1) for k in range(ny)]
    fade = jnp.exp(last)

    def packed(k):
        body = pick(rows_split(state, ny), turned[k]).reshape(share * width, width)
        rows = jnp.stack(pieces_of(pick(rows_split(fade, ny), turned[k])), 0)
        rows = jnp.pad(rows, ((0, pad - PIECES), (0, width - share)))
        return jnp.concatenate([body, rows.astype(BF16)], 0)

    got = [packed(0)] + [y_axis.send(packed(k), k) for k in range(1, ny)]
    states = [g[: share * width].reshape(share, width, width).astype(F32) for g in got]
    fades = [jnp.sum(g[share * width :, :share].astype(F32), 0) for g in got]
    places = [turned[-k % ny] for k in range(ny)]

    def reach(k, end):
        r = jnp.where(places[k] < end, jnp.ones((share,), F32), 0.0)
        for m in range(ny):
            if m != k:
                r = r * jnp.where((places[m] > places[k]) & (places[m] < end), fades[m], 1.0)
        return r[:, None, None]

    def whole(end):
        r = jnp.ones((share,), F32)
        for m in range(ny):
            r = r * jnp.where(places[m] < end, fades[m], 1.0)
        return r[:, None, None]

    inner = sum(reach(k, ny) * states[k] for k in range(ny))
    through = whole(ny)
    carried = jnp.zeros((share, width, width), F32)
    for i in range(z_axis.n - 1):
        out = (through * carried + inner).astype(BF16)
        tie = yield out
        carried = carried + lax.ppermute(out, z_axis.name, z_axis.hop(i)).astype(F32) + tie[:, None]

    def entering(j):
        end = turned[j]
        return (
            whole(end) * carried + sum(reach(k, end) * states[k] for k in range(ny))
        ).astype(BF16)

    tie = yield
    back = [entering(0)] + [y_axis.send(entering(j), j) for j in range(1, ny)]
    back[0] = back[0] + tie.astype(BF16)[:, None]
    yield jnp.concatenate([pick(back, places[p]) for p in range(ny)], 0)


def hidden_kernel(steps, split, *refs):
    xs, w_ref, h_ref, gate, up = refs[:4], refs[4], refs[5], refs[6], refs[7]
    step = pl.program_id(0)

    @pl.when(step == 0)
    def _():
        gate[...] = jnp.zeros_like(gate)
        up[...] = jnp.zeros_like(up)

    def add(pair):
        x = jnp.concatenate([pair[0][...], pair[1][...]], 0)
        gate[...] += lax.dot_general(w_ref[0], x, NT, preferred_element_type=F32)
        up[...] += lax.dot_general(w_ref[1], x, NT, preferred_element_type=F32)

    pl.when(step < split)(lambda: add(xs[:2]))
    pl.when(step >= split)(lambda: add(xs[2:]))

    @pl.when(step == steps - 1)
    def _():
        g = gate[...]
        h_ref[...] = (g / (1.0 + jnp.exp(-g)) * up[...]).T.astype(BF16)


def hidden_pass(xs, w_in, block=1024):
    units, wide = w_in.shape[1], w_in.shape[2]
    tokens = xs[0].shape[0] * 2
    steps = wide // block
    split = steps // 2
    half = tokens // 2
    first = pl.BlockSpec((half, block), lambda s: (0, jnp.minimum(s, split - 1)))
    second = pl.BlockSpec((half, block), lambda s: (0, jnp.maximum(s - split, 0)))
    return pl.pallas_call(
        functools.partial(hidden_kernel, steps, split),
        grid=(steps,),
        in_specs=[first, first, second, second]
        + [pl.BlockSpec((2, units, block), lambda s: (0, 0, s))],
        out_specs=pl.BlockSpec((tokens, units), lambda s: (0, 0)),
        out_shape=jax.ShapeDtypeStruct((tokens, units), BF16),
        scratch_shapes=[pltpu.VMEM((units, tokens), F32), pltpu.VMEM((units, tokens), F32)],
        compiler_params=params(56),
        cost_estimate=pl.CostEstimate(
            flops=4 * units * wide * tokens,
            bytes_accessed=4 * units * wide + 2 * tokens * wide,
            transcendentals=units * tokens,
        ),
        name="hidden_pass",
    )(*xs, w_in)


def down_kernel(h_ref, w_ref, p0_ref, p1_ref, o0_ref, o1_ref):
    half = o0_ref.shape[0]
    out = lax.dot_general(h_ref[...], w_ref[...], NN, preferred_element_type=F32)
    o0_ref[...] = (out[:half] * p0_ref[...]).astype(BF16)
    o1_ref[...] = (out[half:] * p1_ref[...]).astype(BF16)


def down_pass(h, w_out, probs, start, width, block=1024):
    tokens, units = h.shape
    half = tokens // 2
    off = start // block
    out = jax.ShapeDtypeStruct((half, width), BF16)
    spec = pl.BlockSpec((half, block), lambda s: (0, s))
    weight = pl.BlockSpec((half, 1), lambda s: (0, 0))
    return pl.pallas_call(
        down_kernel,
        grid=(width // block,),
        in_specs=[
            pl.BlockSpec((tokens, units), lambda s: (0, 0)),
            pl.BlockSpec((units, block), lambda s: (0, off + s)),
            weight,
            weight,
        ],
        out_specs=(spec, spec),
        out_shape=(out, out),
        compiler_params=params(56),
        cost_estimate=pl.CostEstimate(
            flops=2 * units * width * tokens,
            bytes_accessed=2 * units * width + 2 * tokens * width,
            transcendentals=0,
        ),
        name="down_pass",
    )(h, w_out, *probs)


def ordered(ref, lanes, outer, inner):
    m = ref.shape[0] // (outer * inner)
    blocks = [(i * outer + o) * m for o in range(outer) for i in range(inner)]
    return jnp.concatenate([ref[at : at + m, lanes] for at in blocks], 0)


def store_ordered(ref, lanes, value, outer, inner):
    m = ref.shape[0] // (outer * inner)
    for o in range(outer):
        for i in range(inner):
            src, dst = (o * inner + i) * m, (i * outer + o) * m
            ref[dst : dst + m, lanes] = value[src : src + m]


def own_weights(ref, lanes, experts, outer, inner):
    r = ordered(ref, lanes, outer, inner).astype(F32)
    lane = lax.broadcasted_iota(jnp.int32, r.shape, 1)
    mine = (lane % experts == lax.axis_index("exp")) & (lane < PIECES * experts)
    return jnp.sum(jnp.where(mine, r, 0.0), axis=1, keepdims=True)


def chunks(w, scratch, sems, start, width, block, first):
    out = []
    for j, at in enumerate(range(0, width, block)):
        src = w.at[(slice(None),) * (len(w.shape) - 1) + (pl.ds(start + at, block),)]
        out.append(pltpu.make_async_copy(src, scratch.at[j], sems.at[first + j]))
    return out


def lead_kernel(experts, nx, ny, block, a, a2, b, b2, wg, wu, w_out, o, o2, h, flow, mark, rest, acc, wo, sems):
    units, wide = wg.shape
    half = wide // 2
    rows = a.shape[0]
    copies = chunks(w_out, wo, sems, 0, half, block, 0)
    copies.append(
        pltpu.make_async_copy(w_out.at[:, pl.ds(half, half)], rest, sems.at[len(copies)])
    )
    for c in copies:
        c.start()
    mark[...] = jnp.zeros_like(mark)
    lanes = slice(half, half + 128)
    flow[:rows] = jnp.broadcast_to(own_weights(b, lanes, experts, nx, ny), (rows, 128))
    flow[rows:] = jnp.broadcast_to(own_weights(b2, lanes, experts, nx, ny), (rows, 128))
    for at in range(0, wide, block):
        if at < half:
            x = jnp.concatenate([a[:, at : at + block], a2[:, at : at + block]], 0)
        else:
            lanes = slice(at - half, at - half + block)
            x = jnp.concatenate([ordered(b, lanes, nx, ny), ordered(b2, lanes, nx, ny)], 0)
        for i, w in enumerate((wg, wu)):
            d = lax.dot_general(w[:, at : at + block], x, NT, preferred_element_type=F32)
            if at == 0:
                acc[i] = d
            else:
                acc[i] += d
    g = acc[0]
    h[...] = (g / (1.0 + jnp.exp(-g)) * acc[1]).T.astype(BF16)
    for j, at in enumerate(range(0, half, block)):
        copies[j].wait()
        lanes = slice(at, at + block)
        d = lax.dot_general(h[...], wo[j], NN, preferred_element_type=F32)
        d = (d * flow[:, :1]).astype(BF16)
        o[:, lanes] = d[:rows]
        o2[:, lanes] = d[rows:]
    copies[-1].wait()


def rest_kernel(nx, ny, block, h, flow, w, behind, o, o2):
    rows = o.shape[0]
    for at in range(0, w.shape[1], block):
        lanes = slice(at, at + block)
        d = lax.dot_general(h[...], w[:, lanes], NN, preferred_element_type=F32)
        d = (d * flow[:, :1]).astype(BF16)
        store_ordered(o, lanes, d[:rows], nx, ny)
        store_ordered(o2, lanes, d[rows:], nx, ny)


def lead_pass(a, a2, b, b2, held, w_out, experts, nx, ny, zeros, block=1024):
    units, wide = held[0].shape
    tokens = 2 * a.shape[0]
    n_out = wide // 2 // block
    vmem = pl.BlockSpec(memory_space=pltpu.VMEM)
    hbm = pl.BlockSpec(memory_space=pl.ANY)
    half = pltpu.VMEM((tokens // 2, wide // 2), BF16)
    mark = jax.ShapeDtypeStruct(zeros, F32)
    o, o2, h, flow, mark0, rest = pl.pallas_call(
        functools.partial(lead_kernel, experts, nx, ny, block),
        in_specs=[vmem] * 6 + [hbm],
        out_specs=(vmem,) * 6,
        out_shape=(
            half,
            half,
            pltpu.VMEM((tokens, units), BF16),
            pltpu.VMEM((tokens, 128), F32),
            mark,
            pltpu.VMEM((units, wide // 2), BF16),
        ),
        scratch_shapes=[
            pltpu.VMEM((2, units, tokens), F32),
            pltpu.VMEM((n_out, units, block), BF16),
            pltpu.SemaphoreType.DMA((n_out + 1,)),
        ],
        compiler_params=params(20),
        cost_estimate=pl.CostEstimate(
            flops=5 * units * wide * tokens,
            bytes_accessed=5 * units * wide + 3 * tokens * wide,
            transcendentals=units * tokens,
        ),
        name="lead_pass",
    )(a, a2, b, b2, *held, w_out)
    return (o, o2), (h, flow, rest), mark0


def rest_pass(h, flow, w, behind, nx, ny, block=1024):
    tokens, units = h.shape
    vmem = pl.BlockSpec(memory_space=pltpu.VMEM)
    half = pltpu.VMEM((tokens // 2, w.shape[1]), BF16)
    return pl.pallas_call(
        functools.partial(rest_kernel, nx, ny, block),
        in_specs=[vmem] * 3 + [pl.BlockSpec(memory_space=pl.ANY)],
        out_specs=(vmem,) * 2,
        out_shape=(half, half),
        compiler_params=params(20),
        cost_estimate=pl.CostEstimate(
            flops=2 * units * w.shape[1] * tokens,
            bytes_accessed=2 * units * w.shape[1] + 2 * tokens * w.shape[1],
            transcendentals=0,
        ),
        name="rest_pass",
    )(h, flow, w, behind)


def streamed_experts(a, a2, b, b2, w_in, w_out, experts, nx, ny):
    half = a.shape[1]

    def turned(r, m, n):
        return r.reshape(m, n, -1, r.shape[1]).transpose(1, 0, 2, 3).reshape(r.shape)

    b, b2 = turned(b, ny, nx), turned(b2, ny, nx)

    def weights_of(rows):
        r = rows[:, half : half + PIECES * experts].astype(F32).reshape(-1, PIECES, experts)
        mine = jnp.arange(experts)[None, None] == lax.axis_index("exp")
        return jnp.sum(jnp.where(mine, r, 0.0), axis=(1, 2))[:, None]

    flow = (weights_of(b), weights_of(b2))
    h = hidden_pass((a, a2, b, b2), w_in)
    pa = down_pass(h, w_out, flow, 0, half)
    pb = down_pass(h, w_out, flow, half, half)
    return pa, tuple(turned(p, nx, ny) for p in pb)


def route_columns(ids, probs, experts):
    named = ids[:, :, None] == jnp.arange(experts, dtype=jnp.int32)[None, None]
    weight = jnp.sum(jnp.where(named, probs[:, :, None], 0.0), axis=1)
    route = jnp.concatenate(pieces_of(weight), 1)
    return jnp.pad(route, ((0, 0), (0, 128 - route.shape[1]))).astype(BF16)


def in_hbm(a):
    return pltpu.with_memory_space_constraint(a, pltpu.HBM)


def nothing(a, rows, lanes):
    probe = a[-rows:, :lanes].astype(F32)
    return jnp.where(probe != probe, 1.0, 0.0)


def on_device(axes, projected, log_decay, norm_gain, moe_tokens, expert_ids, route_probs, w_in, w_out):
    x_axis, core, z_axis, y_axis = axes
    nx, ny, nz = x_axis.n, y_axis.n, z_axis.n
    heads = log_decay.shape[1]
    half = moe_tokens.shape[1] // 2
    experts = w_in.shape[0] * lax.axis_size("exp")
    tokens = moe_tokens.shape[0] * lax.axis_size("seq") * lax.axis_size("exp")
    fits = tokens <= 512
    count = heads // PARTS
    qkv = in_hbm(projected.transpose(1, 0, 2))
    w_in = w_in[0].transpose(1, 2, 0)
    w_out = w_out[0]
    route = route_columns(expert_ids, route_probs, experts)

    z = gather(z_axis, jnp.concatenate([moe_tokens, route], 1))
    run, cols, seat = prepare(log_decay)
    made, held = (), []
    for i in range(PARTS):
        w = in_hbm(w_in) if fits else None
        made = local_pass(qkv, run, cols, heads, i * count, count, w, made[:2], (z,) * (i > 0), z.shape[1] - half)
        held += made[3:]
    mixed, state, mark = made[:3]
    a, b = z[:, :half], z[:, half:]
    a, b = gather(y_axis, a), gather(x_axis, b)
    a, b = gather(x_axis, a + mark[:1, :half]), gather(y_axis, b + mark[:1])
    last = run[:, -1]
    zeros = (heads // ny, qkv.shape[2] // heads)
    a2, b2 = core.send(a, 1), core.send(b, 1)
    scan = carry_scan(state, last, seat[:, 0] & (ny - 1), z_axis, y_axis)
    hop = next(scan)
    if fits:
        pa, more, mark = lead_pass(a, a2, b, b2, held, in_hbm(w_out), experts, nx, ny, zeros)
        hop = scan.send(mark)
        pb = rest_pass(*more, hop, nx, ny)
    else:
        pa, pb = streamed_experts(a, a2, b, b2, w_in, w_out, experts, nx, ny)
        scan.send(jnp.zeros(zeros, F32))
    for _ in range(nz - 4):
        scan.send(jnp.zeros(zeros, F32))
    a, b = scatter(core, pa), scatter(core, pb)
    scan.send(nothing(a, *zeros))
    a, b = scatter(x_axis, rows_split(a, nx)), scatter(y_axis, rows_split(b, ny))
    scan.send(nothing(a, *zeros))
    a, b = scatter(y_axis, rows_split(a, ny)), scatter(x_axis, rows_split(b, nx))
    carried = scan.send(nothing(a, *zeros))
    moe_out = scatter(z_axis, rows_split(jnp.concatenate([a, b], 1), nz))
    attn_out = final_pass(qkv, mixed, cols, carried, norm_gain[None], heads)
    return attn_out, moe_out


def solution(mesh):
    nz, ny = factors(mesh.shape["seq"])
    nx = mesh.shape["exp"] // 2
    axes = (
        Axis("exp", nx, 2, 1),
        Axis("exp", 2, 1, nx),
        Axis("seq", nz, ny, 1),
        Axis("seq", ny, 1, nz),
    )
    in_specs = (
        P("seq", None, "exp"),
        P("seq", "exp"),
        P("exp"),
        P(("seq", "exp"), None),
        P(("seq", "exp"), None),
        P(("seq", "exp"), None),
        P("exp", None, None, "seq"),
        P("exp", "seq", None),
    )
    out_specs = (P("seq", "exp"), P(("seq", "exp"), None))
    return jax.shard_map(
        functools.partial(on_device, axes),
        mesh=mesh,
        in_specs=in_specs,
        out_specs=out_specs,
        check_vma=False,
    )
```

```python
import functools
import jax
import jax.numpy as jnp
from jax import lax
from jax.experimental import pallas as pl
from jax.experimental.pallas import tpu as pltpu
from jax.sharding import PartitionSpec as P

EPS = 1e-06
CHUNK = 256
PARTS = 2
PIECES = 3
F32 = jnp.float32
BF16 = jnp.bfloat16
NT = (((1,), (1,)), ((), ()))
TN = (((0,), (0,)), ((), ()))
NN = (((1,), (0,)), ((), ()))


def factors(size):
    bits = size.bit_length() - 1
    inner = 2 ** (bits // 2)
    return size // inner, inner


class Axis:
    def __init__(self, name, n, inner, outer):
        self.name, self.n, self.inner, self.outer = name, n, inner, outer

    def index(self):
        return (lax.axis_index(self.name) // self.inner) % self.n

    def flat(self, o, i, j):
        return (o * self.n + i) * self.inner + j

    def turn(self, k):
        return [
            (self.flat(o, i, j), self.flat(o, (i + k) % self.n, j))
            for o in range(self.outer)
            for i in range(self.n)
            for j in range(self.inner)
        ]

    def hop(self, i):
        return [
            (self.flat(o, i, j), self.flat(o, i + 1, j))
            for o in range(self.outer)
            for j in range(self.inner)
        ]

    def send(self, a, k):
        return lax.ppermute(a, self.name, self.turn(k))


def gather(axis, a):
    return jnp.concatenate([a] + [axis.send(a, k) for k in range(1, axis.n)], 0)


def total(parts):
    s = parts[0].astype(F32)
    for p in parts[1:]:
        s = s + p.astype(F32)
    return s.astype(BF16)


def scatter(axis, parts):
    return total([parts[0]] + [axis.send(parts[k], axis.n - k) for k in range(1, axis.n)])


def rows_split(a, n):
    m = a.shape[0] // n
    return [a[i * m : (i + 1) * m] for i in range(n)]


def pieces_of(x):
    out = []
    for _ in range(PIECES):
        hi = lax.reduce_precision(x, 8, 7)
        out.append(hi)
        x = x - hi
    return out


def params(limit=16):
    return pltpu.CompilerParams(vmem_limit_bytes=limit * 2**20)


def prep_kernel(heads, rows, d_ref, run_ref, cols_ref, seat_ref):
    seat_ref[...] = jnp.zeros_like(seat_ref) + lax.axis_index("seq")
    run = d_ref[...]
    lane = lax.broadcasted_iota(jnp.int32, (heads, rows), 1)
    step = 1
    while step < rows:
        run = run + jnp.where(lane >= step, pltpu.roll(run, step, 1), 0.0)
        step *= 2
    enter = jnp.zeros((heads, 1), F32)
    before, after = [], []
    for i in range(rows // CHUNK):
        leave = run[:, (i + 1) * CHUNK - 1 : (i + 1) * CHUNK]
        before.append(jnp.broadcast_to(enter, (heads, CHUNK)))
        after.append(jnp.broadcast_to(leave, (heads, CHUNK)))
        enter = leave
    eq = jnp.exp(run - jnp.concatenate(before, 1))
    ek = jnp.exp(jnp.concatenate(after, 1) - run)
    run_ref[...] = run
    tall = jnp.concatenate([run, eq, ek, jnp.exp(run)], 0)
    if 4 * heads < 128:
        tall = jnp.concatenate([tall, jnp.zeros((128 - 4 * heads, rows), F32)], 0)
    cols_ref[...] = tall.T


def prepare(log_decay):
    rows, heads = log_decay.shape
    return pl.pallas_call(
        functools.partial(prep_kernel, heads, rows),
        out_shape=(
            jax.ShapeDtypeStruct((heads, rows), F32),
            jax.ShapeDtypeStruct((rows, 128), F32),
            jax.ShapeDtypeStruct((heads, 128), jnp.int32),
        ),
        compiler_params=params(),
        name="prepare",
    )(log_decay.T)


def local_kernel(heads, group, base, loads, which, *refs):
    q_ref, k_ref, v_ref, run_ref, cols_ref = refs[:5]
    mixed_ref, state_ref, mark_ref = refs[-3 - 2 * loads :][:3]
    if loads:
        w_ref, held_ref, sem = refs[5], refs[-2], refs[-1]
        copy = pltpu.make_async_copy(w_ref.at[which], held_ref, sem)
        pl.when(pl.program_id(0) == 0)(copy.start)
    mark_ref[...] = jnp.zeros_like(mark_ref)
    rows, width = q_ref.shape[1], q_ref.shape[2] // group
    first = base + pl.program_id(0) * group
    cols = pltpu.roll(cols_ref[...], 128 - first, 1)
    ri = lax.broadcasted_iota(jnp.int32, (CHUNK, CHUNK), 0)
    ci = lax.broadcasted_iota(jnp.int32, (CHUNK, CHUNK), 1)
    causal = ri >= ci
    for g in range(group):
        lanes = slice(g * width, (g + 1) * width)
        run_row = run_ref[pl.ds(first + g, 1), :]
        state = None
        for i in range(rows // CHUNK):
            part = slice(i * CHUNK, (i + 1) * CHUNK)
            q, k, v = q_ref[0, part, lanes], k_ref[0, part, lanes], v_ref[0, part, lanes]
            run_col = cols[part, g : g + 1]
            eq = cols[part, heads + g : heads + g + 1]
            ek = cols[part, 2 * heads + g : 2 * heads + g + 1]
            scores = lax.dot_general(q, k, NT, preferred_element_type=F32)
            decay = jnp.exp(jnp.where(causal, run_col - run_row[:, part], -jnp.inf))
            weights = (scores * decay).astype(BF16)
            out = lax.dot_general(weights, v, NN, preferred_element_type=F32)
            faded = (k.astype(F32) * ek).astype(BF16)
            fresh = lax.dot_general(faded, v, TN, preferred_element_type=F32)
            if state is None:
                state = fresh
            else:
                out = out + eq * lax.dot_general(
                    q, state.astype(BF16), NN, preferred_element_type=F32
                )
                state = eq[CHUNK - 1 :, :] * state + fresh
            mixed_ref[part, lanes] = out.astype(mixed_ref.dtype)
        state_ref[g] = state.astype(BF16)
    if loads:
        pl.when(pl.program_id(0) == pl.num_programs(0) - 1)(copy.wait)


def local_pass(qkv, run, cols, heads, base, count, w, done, behind, zeros, group=4):
    rows, width = qkv.shape[1], qkv.shape[2] // heads
    group = min(group, count)
    start = base // group
    loads = 0 if w is None else 1
    hbm = pl.BlockSpec(memory_space=pl.ANY)

    def take(which):
        return pl.BlockSpec((1, rows, group * width), lambda h: (which, 0, start + h))

    more = ([w] if loads else []) + list(done) + list(behind)
    aliases = {5 + loads + i: i for i in range(len(done))}
    out_specs = [
        pl.BlockSpec((rows, group * width), lambda h: (0, start + h)),
        pl.BlockSpec((group, width, width), lambda h: (start + h, 0, 0)),
        pl.BlockSpec((8, zeros), lambda h: (0, 0)),
    ]
    out_shape = [
        jax.ShapeDtypeStruct((rows, heads * width), BF16),
        jax.ShapeDtypeStruct((heads, width, width), BF16),
        jax.ShapeDtypeStruct((8, zeros), BF16),
    ]
    if loads:
        out_specs.append(hbm)
        out_shape.append(pltpu.VMEM(w.shape[1:], w.dtype))
    return pl.pallas_call(
        functools.partial(local_kernel, heads, group, base, loads, base // count),
        grid=(count // group,),
        in_specs=[
            take(0),
            take(1),
            take(2),
            pl.BlockSpec(run.shape, lambda h: (0, 0)),
            pl.BlockSpec(cols.shape, lambda h: (0, 0)),
        ]
        + [hbm] * len(more),
        out_specs=out_specs,
        out_shape=out_shape,
        scratch_shapes=[pltpu.SemaphoreType.DMA] * loads,
        input_output_aliases=aliases,
        compiler_params=params(20),
        cost_estimate=pl.CostEstimate(
            flops=8 * count * rows * width * CHUNK,
            bytes_accessed=count * rows * width * 8,
            transcendentals=count * rows * CHUNK,
        ),
        name="local_pass",
    )(qkv, qkv, qkv, run, cols, *more)


def final_kernel(heads, group, first_of, *refs):
    q_ref, mixed_ref, cols_ref, carried_ref, gain_ref = refs[:5]
    out_ref = refs[-1]
    width = q_ref.shape[2] // group
    first = first_of(pl.program_id(0)) * group
    cols = pltpu.roll(cols_ref[...], 128 - first, 1)
    for g in range(group):
        lanes = slice(g * width, (g + 1) * width)
        er = cols[:, 3 * heads + g : 3 * heads + g + 1]
        far = lax.dot_general(q_ref[0, :, lanes], carried_ref[g], NN, preferred_element_type=F32)
        mixed = mixed_ref[:, lanes].astype(F32) + er * far
        mean = jnp.mean(mixed * mixed, axis=-1, keepdims=True)
        out_ref[:, lanes] = (mixed * lax.rsqrt(mean + EPS) * gain_ref[:, lanes]).astype(BF16)


def final_pass(qkv, mixed, cols, carried, gain, heads, y_axis, back, done, behind, group=4):
    rows, width = qkv.shape[1], qkv.shape[2] // heads
    share = carried.shape[0]
    group = min(group, share)

    def block(h):
        place = (y_axis.index() + y_axis.n - back) % y_axis.n
        return place * (share // group) + h

    more = [a for a in (done, behind) if a is not None]
    return pl.pallas_call(
        functools.partial(final_kernel, heads, group, block),
        grid=(share // group,),
        in_specs=[
            pl.BlockSpec((1, rows, group * width), lambda h: (0, 0, block(h))),
            pl.BlockSpec((rows, group * width), lambda h: (0, block(h))),
            pl.BlockSpec(cols.shape, lambda h: (0, 0)),
            pl.BlockSpec((group, width, width), lambda h: (h, 0, 0)),
            pl.BlockSpec((1, group * width), lambda h: (0, block(h))),
        ]
        + [pl.BlockSpec(memory_space=pl.ANY)] * len(more),
        out_specs=pl.BlockSpec((rows, group * width), lambda h: (0, block(h))),
        out_shape=jax.ShapeDtypeStruct((rows, heads * width), BF16),
        input_output_aliases={} if done is None else {5: 0},
        compiler_params=params(20),
        cost_estimate=pl.CostEstimate(
            flops=2 * share * rows * width * width,
            bytes_accessed=share * rows * width * 6,
            transcendentals=0,
        ),
        name="final_pass",
    )(qkv, mixed, cols, carried, gain, *more)


def pick(parts, at):
    out = parts[0]
    for p in range(1, len(parts)):
        out = jnp.where((at == p).reshape((-1,) + (1,) * (out.ndim - 1)), parts[p], out)
    return out


def carry_scan(state, last, seat, z_axis, y_axis):
    heads, width = state.shape[0], state.shape[1]
    ny = y_axis.n
    share = heads // ny
    pad = 16
    y = seat[:share]
    turned = [(y + k) & (ny - 1) for k in range(ny)]
    fade = jnp.exp(last)
    tie = yield

    def packed(k):
        body = pick(rows_split(state, ny), turned[k]) + tie[:, None].astype(BF16)
        body = body.reshape(share * width, width)
        rows = jnp.stack(pieces_of(pick(rows_split(fade, ny), turned[k])), 0)
        rows = jnp.pad(rows, ((0, pad - PIECES), (0, width - share)))
        return jnp.concatenate([body, rows.astype(BF16)], 0)

    got = [packed(0)] + [y_axis.send(packed(k), k) for k in range(1, ny)]
    states = [g[: share * width].reshape(share, width, width).astype(F32) for g in got]
    fades = [jnp.sum(g[share * width :, :share].astype(F32), 0) for g in got]
    places = [turned[-k % ny] for k in range(ny)]

    def reach(k, end):
        r = jnp.where(places[k] < end, jnp.ones((share,), F32), 0.0)
        for m in range(ny):
            if m != k:
                r = r * jnp.where((places[m] > places[k]) & (places[m] < end), fades[m], 1.0)
        return r[:, None, None]

    def whole(end):
        r = jnp.ones((share,), F32)
        for m in range(ny):
            r = r * jnp.where(places[m] < end, fades[m], 1.0)
        return r[:, None, None]

    tie = yield
    inner = sum(reach(k, ny) * states[k] for k in range(ny)) + tie[:, None]
    through = whole(ny)
    carried = jnp.zeros((share, width, width), F32)
    for i in range(z_axis.n - 1):
        out = (through * carried + inner).astype(BF16)
        tie = yield out
        carried = carried + lax.ppermute(out, z_axis.name, z_axis.hop(i)).astype(F32) + tie[:, None]

    def entering(j):
        end = turned[j]
        return (
            whole(end) * carried + sum(reach(k, end) * states[k] for k in range(ny))
        ).astype(BF16)

    yield [entering(0)] + [y_axis.send(entering(j), j) for j in range(1, ny)]


def hidden_kernel(steps, split, *refs):
    xs, w_ref, h_ref, gate, up = refs[:4], refs[4], refs[5], refs[6], refs[7]
    step = pl.program_id(0)

    @pl.when(step == 0)
    def _():
        gate[...] = jnp.zeros_like(gate)
        up[...] = jnp.zeros_like(up)

    def add(pair):
        x = jnp.concatenate([pair[0][...], pair[1][...]], 0)
        gate[...] += lax.dot_general(w_ref[0], x, NT, preferred_element_type=F32)
        up[...] += lax.dot_general(w_ref[1], x, NT, preferred_element_type=F32)

    pl.when(step < split)(lambda: add(xs[:2]))
    pl.when(step >= split)(lambda: add(xs[2:]))

    @pl.when(step == steps - 1)
    def _():
        g = gate[...]
        h_ref[...] = (g / (1.0 + jnp.exp(-g)) * up[...]).T.astype(BF16)


def hidden_pass(xs, w_in, block=1024):
    units, wide = w_in.shape[1], w_in.shape[2]
    tokens = xs[0].shape[0] * 2
    steps = wide // block
    split = steps // 2
    half = tokens // 2
    first = pl.BlockSpec((half, block), lambda s: (0, jnp.minimum(s, split - 1)))
    second = pl.BlockSpec((half, block), lambda s: (0, jnp.maximum(s - split, 0)))
    return pl.pallas_call(
        functools.partial(hidden_kernel, steps, split),
        grid=(steps,),
        in_specs=[first, first, second, second]
        + [pl.BlockSpec((2, units, block), lambda s: (0, 0, s))],
        out_specs=pl.BlockSpec((tokens, units), lambda s: (0, 0)),
        out_shape=jax.ShapeDtypeStruct((tokens, units), BF16),
        scratch_shapes=[pltpu.VMEM((units, tokens), F32), pltpu.VMEM((units, tokens), F32)],
        compiler_params=params(56),
        cost_estimate=pl.CostEstimate(
            flops=4 * units * wide * tokens,
            bytes_accessed=4 * units * wide + 2 * tokens * wide,
            transcendentals=units * tokens,
        ),
        name="hidden_pass",
    )(*xs, w_in)


def down_kernel(h_ref, w_ref, p0_ref, p1_ref, o0_ref, o1_ref):
    half = o0_ref.shape[0]
    out = lax.dot_general(h_ref[...], w_ref[...], NN, preferred_element_type=F32)
    o0_ref[...] = (out[:half] * p0_ref[...]).astype(BF16)
    o1_ref[...] = (out[half:] * p1_ref[...]).astype(BF16)


def down_pass(h, w_out, probs, start, width, block=1024):
    tokens, units = h.shape
    half = tokens // 2
    off = start // block
    out = jax.ShapeDtypeStruct((half, width), BF16)
    spec = pl.BlockSpec((half, block), lambda s: (0, s))
    weight = pl.BlockSpec((half, 1), lambda s: (0, 0))
    return pl.pallas_call(
        down_kernel,
        grid=(width // block,),
        in_specs=[
            pl.BlockSpec((tokens, units), lambda s: (0, 0)),
            pl.BlockSpec((units, block), lambda s: (0, off + s)),
            weight,
            weight,
        ],
        out_specs=(spec, spec),
        out_shape=(out, out),
        compiler_params=params(56),
        cost_estimate=pl.CostEstimate(
            flops=2 * units * width * tokens,
            bytes_accessed=2 * units * width + 2 * tokens * width,
            transcendentals=0,
        ),
        name="down_pass",
    )(h, w_out, *probs)


def ordered(ref, lanes, outer, inner):
    m = ref.shape[0] // (outer * inner)
    blocks = [(i * outer + o) * m for o in range(outer) for i in range(inner)]
    return jnp.concatenate([ref[at : at + m, lanes] for at in blocks], 0)


def store_ordered(ref, lanes, value, outer, inner):
    m = ref.shape[0] // (outer * inner)
    for o in range(outer):
        for i in range(inner):
            src, dst = (o * inner + i) * m, (i * outer + o) * m
            ref[dst : dst + m, lanes] = value[src : src + m]


def own_weights(ref, lanes, experts, outer, inner):
    r = ordered(ref, lanes, outer, inner).astype(F32)
    lane = lax.broadcasted_iota(jnp.int32, r.shape, 1)
    mine = (lane % experts == lax.axis_index("exp")) & (lane < PIECES * experts)
    return jnp.sum(jnp.where(mine, r, 0.0), axis=1, keepdims=True)


def chunks(w, scratch, sems, start, width, block, first):
    out = []
    for j, at in enumerate(range(0, width, block)):
        src = w.at[(slice(None),) * (len(w.shape) - 1) + (pl.ds(start + at, block),)]
        out.append(pltpu.make_async_copy(src, scratch.at[j], sems.at[first + j]))
    return out


def lead_kernel(experts, nx, ny, block, a, a2, b, b2, wg, wu, w_out, o, o2, h, flow, mark, rest, acc, wo, sems):
    units, wide = wg.shape
    half = wide // 2
    rows = a.shape[0]
    copies = chunks(w_out, wo, sems, 0, half, block, 0)
    copies.append(
        pltpu.make_async_copy(w_out.at[:, pl.ds(half, half)], rest, sems.at[len(copies)])
    )
    for c in copies:
        c.start()
    mark[...] = jnp.zeros_like(mark)
    lanes = slice(half, half + 128)
    flow[:rows] = jnp.broadcast_to(own_weights(b, lanes, experts, nx, ny), (rows, 128))
    flow[rows:] = jnp.broadcast_to(own_weights(b2, lanes, experts, nx, ny), (rows, 128))
    for at in range(0, wide, block):
        if at < half:
            x = jnp.concatenate([a[:, at : at + block], a2[:, at : at + block]], 0)
        else:
            lanes = slice(at - half, at - half + block)
            x = jnp.concatenate([ordered(b, lanes, nx, ny), ordered(b2, lanes, nx, ny)], 0)
        for i, w in enumerate((wg, wu)):
            d = lax.dot_general(w[:, at : at + block], x, NT, preferred_element_type=F32)
            if at == 0:
                acc[i] = d
            else:
                acc[i] += d
    g = acc[0]
    h[...] = (g / (1.0 + jnp.exp(-g)) * acc[1]).T.astype(BF16)
    for j, at in enumerate(range(0, half, block)):
        copies[j].wait()
        lanes = slice(at, at + block)
        d = lax.dot_general(h[...], wo[j], NN, preferred_element_type=F32)
        d = (d * flow[:, :1]).astype(BF16)
        o[:, lanes] = d[:rows]
        o2[:, lanes] = d[rows:]
    copies[-1].wait()


def rest_kernel(nx, ny, block, h, flow, w, behind, o, o2):
    rows = o.shape[0]
    for at in range(0, w.shape[1], block):
        lanes = slice(at, at + block)
        d = lax.dot_general(h[...], w[:, lanes], NN, preferred_element_type=F32)
        d = (d * flow[:, :1]).astype(BF16)
        store_ordered(o, lanes, d[:rows], nx, ny)
        store_ordered(o2, lanes, d[rows:], nx, ny)


def lead_pass(a, a2, b, b2, held, w_out, experts, nx, ny, zeros, block=1024):
    units, wide = held[0].shape
    tokens = 2 * a.shape[0]
    n_out = wide // 2 // block
    vmem = pl.BlockSpec(memory_space=pltpu.VMEM)
    hbm = pl.BlockSpec(memory_space=pl.ANY)
    half = pltpu.VMEM((tokens // 2, wide // 2), BF16)
    mark = jax.ShapeDtypeStruct(zeros, F32)
    o, o2, h, flow, mark0, rest = pl.pallas_call(
        functools.partial(lead_kernel, experts, nx, ny, block),
        in_specs=[vmem] * 6 + [hbm],
        out_specs=(vmem,) * 6,
        out_shape=(
            half,
            half,
            pltpu.VMEM((tokens, units), BF16),
            pltpu.VMEM((tokens, 128), F32),
            mark,
            pltpu.VMEM((units, wide // 2), BF16),
        ),
        scratch_shapes=[
            pltpu.VMEM((2, units, tokens), F32),
            pltpu.VMEM((n_out, units, block), BF16),
            pltpu.SemaphoreType.DMA((n_out + 1,)),
        ],
        compiler_params=params(20),
        cost_estimate=pl.CostEstimate(
            flops=5 * units * wide * tokens,
            bytes_accessed=5 * units * wide + 3 * tokens * wide,
            transcendentals=units * tokens,
        ),
        name="lead_pass",
    )(a, a2, b, b2, *held, w_out)
    return (o, o2), (h, flow, rest), mark0


def rest_pass(h, flow, w, behind, nx, ny, block=1024):
    tokens, units = h.shape
    vmem = pl.BlockSpec(memory_space=pltpu.VMEM)
    half = pltpu.VMEM((tokens // 2, w.shape[1]), BF16)
    return pl.pallas_call(
        functools.partial(rest_kernel, nx, ny, block),
        in_specs=[vmem] * 3 + [pl.BlockSpec(memory_space=pl.ANY)],
        out_specs=(vmem,) * 2,
        out_shape=(half, half),
        compiler_params=params(20),
        cost_estimate=pl.CostEstimate(
            flops=2 * units * w.shape[1] * tokens,
            bytes_accessed=2 * units * w.shape[1] + 2 * tokens * w.shape[1],
            transcendentals=0,
        ),
        name="rest_pass",
    )(h, flow, w, behind)


def streamed_experts(a, a2, b, b2, w_in, w_out, experts, nx, ny):
    half = a.shape[1]

    def turned(r, m, n):
        return r.reshape(m, n, -1, r.shape[1]).transpose(1, 0, 2, 3).reshape(r.shape)

    b, b2 = turned(b, ny, nx), turned(b2, ny, nx)

    def weights_of(rows):
        r = rows[:, half : half + PIECES * experts].astype(F32).reshape(-1, PIECES, experts)
        mine = jnp.arange(experts)[None, None] == lax.axis_index("exp")
        return jnp.sum(jnp.where(mine, r, 0.0), axis=(1, 2))[:, None]

    flow = (weights_of(b), weights_of(b2))
    h = hidden_pass((a, a2, b, b2), w_in)
    pa = down_pass(h, w_out, flow, 0, half)
    pb = down_pass(h, w_out, flow, half, half)
    return pa, tuple(turned(p, nx, ny) for p in pb)


def route_columns(ids, probs, experts):
    named = ids[:, :, None] == jnp.arange(experts, dtype=jnp.int32)[None, None]
    weight = jnp.sum(jnp.where(named, probs[:, :, None], 0.0), axis=1)
    route = jnp.concatenate(pieces_of(weight), 1)
    return jnp.pad(route, ((0, 0), (0, 128 - route.shape[1]))).astype(BF16)


def in_hbm(a):
    return pltpu.with_memory_space_constraint(a, pltpu.HBM)


def nothing(a, rows, lanes):
    probe = a[-rows:, :lanes].astype(F32)
    return jnp.where(probe != probe, 1.0, 0.0)


def on_device(axes, projected, log_decay, norm_gain, moe_tokens, expert_ids, route_probs, w_in, w_out):
    x_axis, core, z_axis, y_axis = axes
    nx, ny, nz = x_axis.n, y_axis.n, z_axis.n
    heads = log_decay.shape[1]
    half = moe_tokens.shape[1] // 2
    experts = w_in.shape[0] * lax.axis_size("exp")
    tokens = moe_tokens.shape[0] * lax.axis_size("seq") * lax.axis_size("exp")
    fits = tokens <= 512
    count = heads // PARTS
    qkv = in_hbm(projected.transpose(1, 0, 2))
    w_in = w_in[0].transpose(1, 2, 0)
    w_out = w_out[0]
    route = route_columns(expert_ids, route_probs, experts)

    z = gather(z_axis, jnp.concatenate([moe_tokens, route], 1))
    run, cols, seat = prepare(log_decay)
    made, held = (), []
    for i in range(PARTS):
        w = in_hbm(w_in) if fits else None
        made = local_pass(qkv, run, cols, heads, i * count, count, w, made[:2], (z,) * (i > 0), z.shape[1] - half)
        held += made[3:]
    mixed, state, mark = made[:3]
    a, b = z[:, :half], z[:, half:]
    a, b = gather(y_axis, a), gather(x_axis, b)
    a, b = gather(x_axis, a + mark[:1, :half]), gather(y_axis, b + mark[:1])
    last = run[:, -1]
    zeros = (heads // ny, qkv.shape[2] // heads)
    a2, b2 = core.send(a, 1), core.send(b, 1)
    scan = carry_scan(state, last, seat[:, 0] & (ny - 1), z_axis, y_axis)
    next(scan)
    scan.send(nothing(b, *zeros))
    if fits:
        pa, more, mark = lead_pass(a, a2, b, b2, held, in_hbm(w_out), experts, nx, ny, zeros)
        hop = scan.send(mark)
        pb = rest_pass(*more, hop, nx, ny)
    else:
        pa, pb = streamed_experts(a, a2, b, b2, w_in, w_out, experts, nx, ny)
        scan.send(jnp.zeros(zeros, F32))
    for _ in range(nz - 4):
        scan.send(jnp.zeros(zeros, F32))
    a, b = scatter(core, pa), scatter(core, pb)
    scan.send(nothing(a, *zeros))
    a, b = scatter(x_axis, rows_split(a, nx)), scatter(y_axis, rows_split(b, ny))
    scan.send(nothing(a, *zeros))
    a, b = scatter(y_axis, rows_split(a, ny)), scatter(x_axis, rows_split(b, nx))
    carried = scan.send(nothing(a, *zeros))
    both = jnp.concatenate([a, b], 1)
    moe_out = scatter(z_axis, rows_split(both, nz))
    attn_out = None
    for k in range(ny):
        attn_out = final_pass(
            qkv,
            mixed,
            cols,
            carried[k],
            norm_gain[None],
            heads,
            y_axis,
            k,
            attn_out,
            both if k == 0 else None,
        )
    return attn_out, moe_out


def solution(mesh):
    nz, ny = factors(mesh.shape["seq"])
    nx = mesh.shape["exp"] // 2
    axes = (
        Axis("exp", nx, 2, 1),
        Axis("exp", 2, 1, nx),
        Axis("seq", nz, ny, 1),
        Axis("seq", ny, 1, nz),
    )
    in_specs = (
        P("seq", None, "exp"),
        P("seq", "exp"),
        P("exp"),
        P(("seq", "exp"), None),
        P(("seq", "exp"), None),
        P(("seq", "exp"), None),
        P("exp", None, None, "seq"),
        P("exp", "seq", None),
    )
    out_specs = (P("seq", "exp"), P(("seq", "exp"), None))
    return jax.shard_map(
        functools.partial(on_device, axes),
        mesh=mesh,
        in_specs=in_specs,
        out_specs=out_specs,
        check_vma=False,
    )
```

```python
import functools
import jax
import jax.numpy as jnp
from jax import lax
from jax.experimental import pallas as pl
from jax.experimental.pallas import tpu as pltpu
from jax.sharding import PartitionSpec as P

EPS = 1e-06
CHUNK = 256
PIECES = 3
F32 = jnp.float32
BF16 = jnp.bfloat16
NT = (((1,), (1,)), ((), ()))
TN = (((0,), (0,)), ((), ()))
NN = (((1,), (0,)), ((), ()))


def factors(size):
    bits = size.bit_length() - 1
    inner = 2 ** (bits // 2)
    return size // inner, inner


class Axis:
    def __init__(self, name, n, inner, outer):
        self.name, self.n, self.inner, self.outer = name, n, inner, outer

    def index(self):
        return (lax.axis_index(self.name) // self.inner) % self.n

    def flat(self, o, i, j):
        return (o * self.n + i) * self.inner + j

    def turn(self, k):
        return [
            (self.flat(o, i, j), self.flat(o, (i + k) % self.n, j))
            for o in range(self.outer)
            for i in range(self.n)
            for j in range(self.inner)
        ]

    def jump(self, k):
        return [
            (self.flat(o, i, j), self.flat(o, i + k, j))
            for o in range(self.outer)
            for i in range(self.n - k)
            for j in range(self.inner)
        ]

    def send(self, a, k):
        return lax.ppermute(a, self.name, self.turn(k))


def gather(axis, a):
    return jnp.concatenate([a] + [axis.send(a, k) for k in range(1, axis.n)], 0)


def total(parts):
    s = parts[0].astype(F32)
    for p in parts[1:]:
        s = s + p.astype(F32)
    return s.astype(BF16)


def scatter(axis, parts):
    return total([parts[0]] + [axis.send(parts[k], axis.n - k) for k in range(1, axis.n)])


def rows_split(a, n):
    m = a.shape[0] // n
    return [a[i * m : (i + 1) * m] for i in range(n)]


def pieces_of(x):
    out = []
    for _ in range(PIECES):
        hi = lax.reduce_precision(x, 8, 7)
        out.append(hi)
        x = x - hi
    return out


def params(limit=16):
    return pltpu.CompilerParams(vmem_limit_bytes=limit * 2**20)


def prep_kernel(heads, rows, d_ref, run_ref, cols_ref, seat_ref):
    seat_ref[...] = jnp.zeros_like(seat_ref) + lax.axis_index("seq")
    run = d_ref[...]
    lane = lax.broadcasted_iota(jnp.int32, (heads, rows), 1)
    step = 1
    while step < rows:
        run = run + jnp.where(lane >= step, pltpu.roll(run, step, 1), 0.0)
        step *= 2
    enter = jnp.zeros((heads, 1), F32)
    before, after = [], []
    for i in range(rows // CHUNK):
        leave = run[:, (i + 1) * CHUNK - 1 : (i + 1) * CHUNK]
        before.append(jnp.broadcast_to(enter, (heads, CHUNK)))
        after.append(jnp.broadcast_to(leave, (heads, CHUNK)))
        enter = leave
    eq = jnp.exp(run - jnp.concatenate(before, 1))
    ek = jnp.exp(jnp.concatenate(after, 1) - run)
    run_ref[...] = run
    tall = jnp.concatenate([run, eq, ek, jnp.exp(run)], 0)
    if 4 * heads < 128:
        tall = jnp.concatenate([tall, jnp.zeros((128 - 4 * heads, rows), F32)], 0)
    cols_ref[...] = tall.T


def prepare(log_decay):
    rows, heads = log_decay.shape
    return pl.pallas_call(
        functools.partial(prep_kernel, heads, rows),
        out_shape=(
            jax.ShapeDtypeStruct((heads, rows), F32),
            jax.ShapeDtypeStruct((rows, 128), F32),
            jax.ShapeDtypeStruct((heads, 128), jnp.int32),
        ),
        compiler_params=params(),
        name="prepare",
    )(log_decay.T)


def local_kernel(heads, group, first_of, loads, which, *refs):
    q_ref, k_ref, v_ref, run_ref, cols_ref = refs[:5]
    mixed_ref, state_ref, mark_ref = refs[-3 - 2 * loads :][:3]
    if loads:
        w_ref, held_ref, sem = refs[5], refs[-2], refs[-1]
        copy = pltpu.make_async_copy(w_ref.at[which], held_ref, sem)
        pl.when(pl.program_id(0) == 0)(copy.start)
    mark_ref[...] = jnp.zeros_like(mark_ref)
    rows, width = q_ref.shape[1], q_ref.shape[2] // group
    first = first_of(pl.program_id(0)) * group
    cols = pltpu.roll(cols_ref[...], 128 - first, 1)
    ri = lax.broadcasted_iota(jnp.int32, (CHUNK, CHUNK), 0)
    ci = lax.broadcasted_iota(jnp.int32, (CHUNK, CHUNK), 1)
    causal = ri >= ci
    for g in range(group):
        lanes = slice(g * width, (g + 1) * width)
        run_row = run_ref[pl.ds(first + g, 1), :]
        state = None
        for i in range(rows // CHUNK):
            part = slice(i * CHUNK, (i + 1) * CHUNK)
            q, k, v = q_ref[0, part, lanes], k_ref[0, part, lanes], v_ref[0, part, lanes]
            run_col = cols[part, g : g + 1]
            eq = cols[part, heads + g : heads + g + 1]
            ek = cols[part, 2 * heads + g : 2 * heads + g + 1]
            scores = lax.dot_general(q, k, NT, preferred_element_type=F32)
            decay = jnp.exp(jnp.where(causal, run_col - run_row[:, part], -jnp.inf))
            weights = (scores * decay).astype(BF16)
            out = lax.dot_general(weights, v, NN, preferred_element_type=F32)
            faded = (k.astype(F32) * ek).astype(BF16)
            fresh = lax.dot_general(faded, v, TN, preferred_element_type=F32)
            if state is None:
                state = fresh
            else:
                out = out + eq * lax.dot_general(
                    q, state.astype(BF16), NN, preferred_element_type=F32
                )
                state = eq[CHUNK - 1 :, :] * state + fresh
            mixed_ref[part, lanes] = out.astype(mixed_ref.dtype)
        state_ref[g] = state.astype(BF16)
    if loads:
        pl.when(pl.program_id(0) == pl.num_programs(0) - 1)(copy.wait)


def place_block(axis, turn, per):
    return lambda h: ((axis.index() + axis.n + turn) % axis.n) * per + h


def local_pass(qkv, run, cols, heads, y_axis, turn, w, which, done, behind, zeros, group=4):
    rows, width = qkv.shape[1], qkv.shape[2] // heads
    share = heads // y_axis.n
    group = min(group, share)
    block = place_block(y_axis, turn, share // group)
    loads = 0 if w is None else 1
    hbm = pl.BlockSpec(memory_space=pl.ANY)

    def take(part):
        return pl.BlockSpec((1, rows, group * width), lambda h: (part, 0, block(h)))

    more = ([w] if loads else []) + list(done) + list(behind)
    aliases = {5 + loads + i: i for i in range(len(done))}
    out_specs = [
        pl.BlockSpec((rows, group * width), lambda h: (0, block(h))),
        pl.BlockSpec((group, width, width), lambda h: (h, 0, 0)),
        pl.BlockSpec((8, zeros), lambda h: (0, 0)),
    ]
    out_shape = [
        jax.ShapeDtypeStruct((rows, heads * width), BF16),
        jax.ShapeDtypeStruct((share, width, width), BF16),
        jax.ShapeDtypeStruct((8, zeros), BF16),
    ]
    if loads:
        out_specs.append(hbm)
        out_shape.append(pltpu.VMEM(w.shape[1:], w.dtype))
    return pl.pallas_call(
        functools.partial(local_kernel, heads, group, block, loads, which),
        grid=(share // group,),
        in_specs=[
            take(0),
            take(1),
            take(2),
            pl.BlockSpec(run.shape, lambda h: (0, 0)),
            pl.BlockSpec(cols.shape, lambda h: (0, 0)),
        ]
        + [hbm] * len(more),
        out_specs=out_specs,
        out_shape=out_shape,
        scratch_shapes=[pltpu.SemaphoreType.DMA] * loads,
        input_output_aliases=aliases,
        compiler_params=params(20),
        cost_estimate=pl.CostEstimate(flops=1, bytes_accessed=1, transcendentals=0),
        name="local_pass",
    )(qkv, qkv, qkv, run, cols, *more)


def final_kernel(heads, group, first_of, *refs):
    q_ref, mixed_ref, cols_ref, carried_ref, gain_ref = refs[:5]
    out_ref = refs[-1]
    width = q_ref.shape[2] // group
    first = first_of(pl.program_id(0)) * group
    cols = pltpu.roll(cols_ref[...], 128 - first, 1)
    for g in range(group):
        lanes = slice(g * width, (g + 1) * width)
        er = cols[:, 3 * heads + g : 3 * heads + g + 1]
        far = lax.dot_general(q_ref[0, :, lanes], carried_ref[g], NN, preferred_element_type=F32)
        mixed = mixed_ref[:, lanes].astype(F32) + er * far
        mean = jnp.mean(mixed * mixed, axis=-1, keepdims=True)
        out_ref[:, lanes] = (mixed * lax.rsqrt(mean + EPS) * gain_ref[:, lanes]).astype(BF16)


def final_pass(qkv, mixed, cols, carried, gain, heads, y_axis, back, done, behind, group=4):
    rows, width = qkv.shape[1], qkv.shape[2] // heads
    share = carried.shape[0]
    group = min(group, share)

    block = place_block(y_axis, -back, share // group)
    more = [a for a in (done, behind) if a is not None]
    return pl.pallas_call(
        functools.partial(final_kernel, heads, group, block),
        grid=(share // group,),
        in_specs=[
            pl.BlockSpec((1, rows, group * width), lambda h: (0, 0, block(h))),
            pl.BlockSpec((rows, group * width), lambda h: (0, block(h))),
            pl.BlockSpec(cols.shape, lambda h: (0, 0)),
            pl.BlockSpec((group, width, width), lambda h: (h, 0, 0)),
            pl.BlockSpec((1, group * width), lambda h: (0, block(h))),
        ]
        + [pl.BlockSpec(memory_space=pl.ANY)] * len(more),
        out_specs=pl.BlockSpec((rows, group * width), lambda h: (0, block(h))),
        out_shape=jax.ShapeDtypeStruct((rows, heads * width), BF16),
        input_output_aliases={} if done is None else {5: 0},
        compiler_params=params(20),
        cost_estimate=pl.CostEstimate(flops=1, bytes_accessed=1, transcendentals=0),
        name="final_pass",
    )(qkv, mixed, cols, carried, gain, *more)


def pick(parts, at):
    out = parts[0]
    for p in range(1, len(parts)):
        out = jnp.where((at == p).reshape((-1,) + (1,) * (out.ndim - 1)), parts[p], out)
    return out


def carry_scan(shares, last, seat, z_axis, y_axis):
    share, width = shares[0].shape[:2]
    ny = y_axis.n
    pad = 16
    y = seat[:share]
    turned = [(y + k) & (ny - 1) for k in range(ny)]
    fade = jnp.exp(last)
    mine = [pick(rows_split(fade, ny), turned[k]) for k in range(ny)]

    def packed(body, fade):
        rows = jnp.stack(pieces_of(fade), 0)
        rows = jnp.pad(rows, ((0, pad - PIECES), (0, width - share)))
        body = body.reshape(share * width, width)
        return jnp.concatenate([body.astype(BF16), rows.astype(BF16)], 0)

    def unpacked(g):
        body = g[: share * width].reshape(share, width, width).astype(F32)
        return body, jnp.sum(g[share * width :, :share].astype(F32), 0)

    got = [y_axis.send(packed(shares[k], mine[k]), k) for k in range(1, ny)]
    tie = yield
    states, fades = zip((shares[0].astype(F32), mine[0]), *[unpacked(g) for g in got])
    places = [turned[-k % ny] for k in range(ny)]

    def reach(k, end):
        r = jnp.where(places[k] < end, jnp.ones((share,), F32), 0.0)
        for m in range(ny):
            if m != k:
                r = r * jnp.where((places[m] > places[k]) & (places[m] < end), fades[m], 1.0)
        return r[:, None, None]

    def whole(end):
        r = jnp.ones((share,), F32)
        for m in range(ny):
            r = r * jnp.where(places[m] < end, fades[m], 1.0)
        return r[:, None, None]

    inner = sum(reach(k, ny) * states[k] for k in range(ny))
    through = whole(ny)
    carried, behind = jnp.zeros((share, width, width), F32), jnp.ones((share,), F32)
    first = tie[:, None]
    far = 1
    while far < z_axis.n:
        out = through * carried + inner + first
        if 2 * far < z_axis.n:
            out = packed(out, through[:, 0, 0] * behind)
        else:
            out = out.astype(BF16)
        tie = yield out
        came = lax.ppermute(out, z_axis.name, z_axis.jump(far))
        if 2 * far < z_axis.n:
            came, more = unpacked(came + tie[:1].astype(BF16))
            carried = carried + behind[:, None, None] * came
            behind = behind * more
        else:
            carried = carried + behind[:, None, None] * came.astype(F32) + tie[:, None]
        first = 0.0
        far *= 2

    def entering(j):
        end = turned[j]
        return (
            whole(end) * carried + sum(reach(k, end) * states[k] for k in range(ny))
        ).astype(BF16)

    yield [entering(0)] + [y_axis.send(entering(j), j) for j in range(1, ny)]


def hidden_kernel(steps, split, *refs):
    xs, w_ref, h_ref, gate, up = refs[:4], refs[4], refs[5], refs[6], refs[7]
    step = pl.program_id(0)

    @pl.when(step == 0)
    def _():
        gate[...] = jnp.zeros_like(gate)
        up[...] = jnp.zeros_like(up)

    def add(pair):
        x = jnp.concatenate([pair[0][...], pair[1][...]], 0)
        gate[...] += lax.dot_general(w_ref[0], x, NT, preferred_element_type=F32)
        up[...] += lax.dot_general(w_ref[1], x, NT, preferred_element_type=F32)

    pl.when(step < split)(lambda: add(xs[:2]))
    pl.when(step >= split)(lambda: add(xs[2:]))

    @pl.when(step == steps - 1)
    def _():
        g = gate[...]
        h_ref[...] = (g / (1.0 + jnp.exp(-g)) * up[...]).T.astype(BF16)


def hidden_pass(xs, w_in, block=1024):
    units, wide = w_in.shape[1], w_in.shape[2]
    tokens = xs[0].shape[0] * 2
    steps = wide // block
    split = steps // 2
    half = tokens // 2
    first = pl.BlockSpec((half, block), lambda s: (0, jnp.minimum(s, split - 1)))
    second = pl.BlockSpec((half, block), lambda s: (0, jnp.maximum(s - split, 0)))
    return pl.pallas_call(
        functools.partial(hidden_kernel, steps, split),
        grid=(steps,),
        in_specs=[first, first, second, second]
        + [pl.BlockSpec((2, units, block), lambda s: (0, 0, s))],
        out_specs=pl.BlockSpec((tokens, units), lambda s: (0, 0)),
        out_shape=jax.ShapeDtypeStruct((tokens, units), BF16),
        scratch_shapes=[pltpu.VMEM((units, tokens), F32), pltpu.VMEM((units, tokens), F32)],
        compiler_params=params(56),
        cost_estimate=pl.CostEstimate(flops=1, bytes_accessed=1, transcendentals=0),
        name="hidden_pass",
    )(*xs, w_in)


def down_kernel(h_ref, w_ref, p0_ref, p1_ref, o0_ref, o1_ref):
    half = o0_ref.shape[0]
    out = lax.dot_general(h_ref[...], w_ref[...], NN, preferred_element_type=F32)
    o0_ref[...] = (out[:half] * p0_ref[...]).astype(BF16)
    o1_ref[...] = (out[half:] * p1_ref[...]).astype(BF16)


def down_pass(h, w_out, probs, start, width, block=1024):
    tokens, units = h.shape
    half = tokens // 2
    off = start // block
    out = jax.ShapeDtypeStruct((half, width), BF16)
    spec = pl.BlockSpec((half, block), lambda s: (0, s))
    weight = pl.BlockSpec((half, 1), lambda s: (0, 0))
    return pl.pallas_call(
        down_kernel,
        grid=(width // block,),
        in_specs=[
            pl.BlockSpec((tokens, units), lambda s: (0, 0)),
            pl.BlockSpec((units, block), lambda s: (0, off + s)),
            weight,
            weight,
        ],
        out_specs=(spec, spec),
        out_shape=(out, out),
        compiler_params=params(56),
        cost_estimate=pl.CostEstimate(flops=1, bytes_accessed=1, transcendentals=0),
        name="down_pass",
    )(h, w_out, *probs)


def ordered(ref, lanes, outer, inner):
    m = ref.shape[0] // (outer * inner)
    blocks = [(i * outer + o) * m for o in range(outer) for i in range(inner)]
    return jnp.concatenate([ref[at : at + m, lanes] for at in blocks], 0)


def store_ordered(ref, lanes, value, outer, inner):
    m = ref.shape[0] // (outer * inner)
    for o in range(outer):
        for i in range(inner):
            src, dst = (o * inner + i) * m, (i * outer + o) * m
            ref[dst : dst + m, lanes] = value[src : src + m]


def own_weights(ref, lanes, experts, outer, inner):
    r = ordered(ref, lanes, outer, inner).astype(F32)
    lane = lax.broadcasted_iota(jnp.int32, r.shape, 1)
    mine = (lane % experts == lax.axis_index("exp")) & (lane < PIECES * experts)
    return jnp.sum(jnp.where(mine, r, 0.0), axis=1, keepdims=True)


def chunks(w, scratch, sems, start, width, block, first):
    out = []
    for j, at in enumerate(range(0, width, block)):
        src = w.at[(slice(None),) * (len(w.shape) - 1) + (pl.ds(start + at, block),)]
        out.append(pltpu.make_async_copy(src, scratch.at[j], sems.at[first + j]))
    return out


def lead_kernel(experts, nx, ny, block, a, a2, b, b2, wg, wu, w_out, o, o2, h, flow, mark, rest, acc, wo, sems):
    units, wide = wg.shape
    half = wide // 2
    rows = a.shape[0]
    copies = chunks(w_out, wo, sems, 0, half, block, 0)
    copies.append(
        pltpu.make_async_copy(w_out.at[:, pl.ds(half, half)], rest, sems.at[len(copies)])
    )
    for c in copies:
        c.start()
    mark[...] = jnp.zeros_like(mark)
    lanes = slice(half, half + 128)
    flow[:rows] = jnp.broadcast_to(own_weights(b, lanes, experts, nx, ny), (rows, 128))
    flow[rows:] = jnp.broadcast_to(own_weights(b2, lanes, experts, nx, ny), (rows, 128))
    for at in range(0, wide, block):
        if at < half:
            x = jnp.concatenate([a[:, at : at + block], a2[:, at : at + block]], 0)
        else:
            lanes = slice(at - half, at - half + block)
            x = jnp.concatenate([ordered(b, lanes, nx, ny), ordered(b2, lanes, nx, ny)], 0)
        for i, w in enumerate((wg, wu)):
            d = lax.dot_general(w[:, at : at + block], x, NT, preferred_element_type=F32)
            if at == 0:
                acc[i] = d
            else:
                acc[i] += d
    g = acc[0]
    h[...] = (g / (1.0 + jnp.exp(-g)) * acc[1]).T.astype(BF16)
    for j, at in enumerate(range(0, half, block)):
        copies[j].wait()
        lanes = slice(at, at + block)
        d = lax.dot_general(h[...], wo[j], NN, preferred_element_type=F32)
        d = (d * flow[:, :1]).astype(BF16)
        o[:, lanes] = d[:rows]
        o2[:, lanes] = d[rows:]
    copies[-1].wait()


def rest_kernel(nx, ny, block, h, flow, w, behind, o, o2):
    rows = o.shape[0]
    for at in range(0, w.shape[1], block):
        lanes = slice(at, at + block)
        d = lax.dot_general(h[...], w[:, lanes], NN, preferred_element_type=F32)
        d = (d * flow[:, :1]).astype(BF16)
        store_ordered(o, lanes, d[:rows], nx, ny)
        store_ordered(o2, lanes, d[rows:], nx, ny)


def lead_pass(a, a2, b, b2, held, w_out, experts, nx, ny, zeros, block=1024):
    units, wide = held[0].shape
    tokens = 2 * a.shape[0]
    n_out = wide // 2 // block
    vmem = pl.BlockSpec(memory_space=pltpu.VMEM)
    hbm = pl.BlockSpec(memory_space=pl.ANY)
    half = pltpu.VMEM((tokens // 2, wide // 2), BF16)
    mark = jax.ShapeDtypeStruct(zeros, F32)
    o, o2, h, flow, mark0, rest = pl.pallas_call(
        functools.partial(lead_kernel, experts, nx, ny, block),
        in_specs=[vmem] * 6 + [hbm],
        out_specs=(vmem,) * 6,
        out_shape=(
            half,
            half,
            pltpu.VMEM((tokens, units), BF16),
            pltpu.VMEM((tokens, 128), F32),
            mark,
            pltpu.VMEM((units, wide // 2), BF16),
        ),
        scratch_shapes=[
            pltpu.VMEM((2, units, tokens), F32),
            pltpu.VMEM((n_out, units, block), BF16),
            pltpu.SemaphoreType.DMA((n_out + 1,)),
        ],
        compiler_params=params(20),
        cost_estimate=pl.CostEstimate(flops=1, bytes_accessed=1, transcendentals=0),
        name="lead_pass",
    )(a, a2, b, b2, *held, w_out)
    return (o, o2), (h, flow, rest), mark0


def rest_pass(h, flow, w, behind, nx, ny, block=1024):
    tokens, units = h.shape
    vmem = pl.BlockSpec(memory_space=pltpu.VMEM)
    half = pltpu.VMEM((tokens // 2, w.shape[1]), BF16)
    return pl.pallas_call(
        functools.partial(rest_kernel, nx, ny, block),
        in_specs=[vmem] * 3 + [pl.BlockSpec(memory_space=pl.ANY)],
        out_specs=(vmem,) * 2,
        out_shape=(half, half),
        compiler_params=params(20),
        cost_estimate=pl.CostEstimate(flops=1, bytes_accessed=1, transcendentals=0),
        name="rest_pass",
    )(h, flow, w, behind)


def streamed_experts(a, a2, b, b2, w_in, w_out, experts, nx, ny):
    half = a.shape[1]

    def turned(r, m, n):
        return r.reshape(m, n, -1, r.shape[1]).transpose(1, 0, 2, 3).reshape(r.shape)

    b, b2 = turned(b, ny, nx), turned(b2, ny, nx)

    def weights_of(rows):
        r = rows[:, half : half + PIECES * experts].astype(F32).reshape(-1, PIECES, experts)
        mine = jnp.arange(experts)[None, None] == lax.axis_index("exp")
        return jnp.sum(jnp.where(mine, r, 0.0), axis=(1, 2))[:, None]

    flow = (weights_of(b), weights_of(b2))
    h = hidden_pass((a, a2, b, b2), w_in)
    pa = down_pass(h, w_out, flow, 0, half)
    pb = down_pass(h, w_out, flow, half, half)
    return pa, tuple(turned(p, nx, ny) for p in pb)


def route_columns(ids, probs, experts):
    named = ids[:, :, None] == jnp.arange(experts, dtype=jnp.int32)[None, None]
    weight = jnp.sum(jnp.where(named, probs[:, :, None], 0.0), axis=1)
    route = jnp.concatenate(pieces_of(weight), 1)
    return jnp.pad(route, ((0, 0), (0, 128 - route.shape[1]))).astype(BF16)


def in_hbm(a):
    return pltpu.with_memory_space_constraint(a, pltpu.HBM)


def nothing(a, rows, lanes):
    probe = a[-rows:, :lanes].astype(F32)
    return jnp.where(probe != probe, 1.0, 0.0)


def on_device(axes, projected, log_decay, norm_gain, moe_tokens, expert_ids, route_probs, w_in, w_out):
    x_axis, core, z_axis, y_axis = axes
    nx, ny, nz = x_axis.n, y_axis.n, z_axis.n
    heads = log_decay.shape[1]
    half = moe_tokens.shape[1] // 2
    experts = w_in.shape[0] * lax.axis_size("exp")
    tokens = moe_tokens.shape[0] * lax.axis_size("seq") * lax.axis_size("exp")
    fits = tokens <= 512 and ny == 2
    zeros = (heads // ny, projected.shape[2] // heads)
    qkv = in_hbm(projected.transpose(1, 0, 2))
    w_in = w_in[0].transpose(1, 2, 0)
    w_out = w_out[0]
    route = route_columns(expert_ids, route_probs, experts)

    z = gather(z_axis, jnp.concatenate([moe_tokens, route], 1))
    run, cols, seat = prepare(log_decay)
    done, held, shares = (), [], {}
    for i in range(ny):
        turn = (i + 1) % ny
        w = in_hbm(w_in) if fits else None
        behind = (z,) * (i == ny - 1)
        made = local_pass(
            qkv, run, cols, heads, y_axis, turn, w, i, done, behind, z.shape[1] - half
        )
        done, shares[turn], mark = made[:1], made[1], made[2]
        held += made[3:]
    mixed = done[0]
    scan = carry_scan(shares, run[:, -1], seat[:, 0] & (ny - 1), z_axis, y_axis)
    next(scan)
    a, b = z[:, :half], z[:, half:]
    a, b = gather(y_axis, a), gather(x_axis, b)
    a, b = gather(x_axis, a + mark[:1, :half]), gather(y_axis, b + mark[:1])
    scan.send(nothing(a, *zeros))
    a2, b2 = core.send(a, 1), core.send(b, 1)
    if fits:
        pa, more, mark = lead_pass(
            a, a2, b, b2, held, in_hbm(w_out), experts, nx, ny, zeros
        )
        hop = scan.send(mark)
        pb = rest_pass(*more, hop, nx, ny)
    else:
        pa, pb = streamed_experts(a, a2, b, b2, w_in, w_out, experts, nx, ny)
        scan.send(jnp.zeros(zeros, F32))
    for _ in range((nz - 1).bit_length() - 2):
        scan.send(jnp.zeros(zeros, F32))
    a, b = scatter(core, pa), scatter(core, pb)
    a, b = scatter(x_axis, rows_split(a, nx)), scatter(y_axis, rows_split(b, ny))
    carried = scan.send(nothing(a, *zeros))
    a, b = scatter(y_axis, rows_split(a, ny)), scatter(x_axis, rows_split(b, nx))
    both = jnp.concatenate([a, b], 1)
    moe_out = scatter(z_axis, rows_split(both, nz))
    attn_out = None
    for k in range(ny):
        attn_out = final_pass(
            qkv,
            mixed,
            cols,
            carried[k],
            norm_gain[None],
            heads,
            y_axis,
            k,
            attn_out,
            both if k == 0 else None,
        )
    return attn_out, moe_out


def solution(mesh):
    nz, ny = factors(mesh.shape["seq"])
    nx = mesh.shape["exp"] // 2
    axes = (
        Axis("exp", nx, 2, 1),
        Axis("exp", 2, 1, nx),
        Axis("seq", nz, ny, 1),
        Axis("seq", ny, 1, nz),
    )
    in_specs = (
        P("seq", None, "exp"),
        P("seq", "exp"),
        P("exp"),
        P(("seq", "exp"), None),
        P(("seq", "exp"), None),
        P(("seq", "exp"), None),
        P("exp", None, None, "seq"),
        P("exp", "seq", None),
    )
    out_specs = (P("seq", "exp"), P(("seq", "exp"), None))
    return jax.shard_map(
        functools.partial(on_device, axes),
        mesh=mesh,
        in_specs=in_specs,
        out_specs=out_specs,
        check_vma=False,
    )
```

```python
import functools
import jax
import jax.numpy as jnp
from jax import lax
from jax.experimental import pallas as pl
from jax.experimental.pallas import tpu as pltpu
from jax.sharding import PartitionSpec as P

EPS = 1e-06
CHUNK = 256
PIECES = 3
F32 = jnp.float32
BF16 = jnp.bfloat16
NT = (((1,), (1,)), ((), ()))
TN = (((0,), (0,)), ((), ()))
NN = (((1,), (0,)), ((), ()))


def factors(size):
    bits = size.bit_length() - 1
    inner = 2 ** (bits // 2)
    return size // inner, inner


class Axis:
    def __init__(self, name, n, inner, outer):
        self.name, self.n, self.inner, self.outer = name, n, inner, outer

    def index(self):
        return (lax.axis_index(self.name) // self.inner) % self.n

    def flat(self, o, i, j):
        return (o * self.n + i) * self.inner + j

    def turn(self, k):
        return [
            (self.flat(o, i, j), self.flat(o, (i + k) % self.n, j))
            for o in range(self.outer)
            for i in range(self.n)
            for j in range(self.inner)
        ]

    def jump(self, k):
        return [
            (self.flat(o, i, j), self.flat(o, i + k, j))
            for o in range(self.outer)
            for i in range(self.n - k)
            for j in range(self.inner)
        ]

    def send(self, a, k):
        return lax.ppermute(a, self.name, self.turn(k))


def gather(axis, a):
    return jnp.concatenate([a] + [axis.send(a, k) for k in range(1, axis.n)], 0)


def total(parts):
    s = parts[0].astype(F32)
    for p in parts[1:]:
        s = s + p.astype(F32)
    return s.astype(BF16)


def scatter(axis, parts):
    return total([parts[0]] + [axis.send(parts[k], axis.n - k) for k in range(1, axis.n)])


def rows_split(a, n):
    m = a.shape[0] // n
    return [a[i * m : (i + 1) * m] for i in range(n)]


def pieces_of(x):
    out = []
    for _ in range(PIECES):
        hi = lax.reduce_precision(x, 8, 7)
        out.append(hi)
        x = x - hi
    return out


def params(limit=16):
    return pltpu.CompilerParams(vmem_limit_bytes=limit * 2**20)


def prep_kernel(heads, rows, d_ref, run_ref, cols_ref, seat_ref):
    seat_ref[...] = jnp.zeros_like(seat_ref) + lax.axis_index("seq")
    run = d_ref[...]
    lane = lax.broadcasted_iota(jnp.int32, (heads, rows), 1)
    step = 1
    while step < rows:
        run = run + jnp.where(lane >= step, pltpu.roll(run, step, 1), 0.0)
        step *= 2
    enter = jnp.zeros((heads, 1), F32)
    before, after = [], []
    for i in range(rows // CHUNK):
        leave = run[:, (i + 1) * CHUNK - 1 : (i + 1) * CHUNK]
        before.append(jnp.broadcast_to(enter, (heads, CHUNK)))
        after.append(jnp.broadcast_to(leave, (heads, CHUNK)))
        enter = leave
    eq = jnp.exp(run - jnp.concatenate(before, 1))
    ek = jnp.exp(jnp.concatenate(after, 1) - run)
    run_ref[...] = run
    tall = jnp.concatenate([run, eq, ek, jnp.exp(run)], 0)
    if 4 * heads < 128:
        tall = jnp.concatenate([tall, jnp.zeros((128 - 4 * heads, rows), F32)], 0)
    cols_ref[...] = tall.T


def prepare(log_decay):
    rows, heads = log_decay.shape
    return pl.pallas_call(
        functools.partial(prep_kernel, heads, rows),
        out_shape=(
            jax.ShapeDtypeStruct((heads, rows), F32),
            jax.ShapeDtypeStruct((rows, 128), F32),
            jax.ShapeDtypeStruct((heads, 128), jnp.int32),
        ),
        compiler_params=params(),
        name="prepare",
    )(log_decay.T)


def local_kernel(heads, group, first_of, loads, which, *refs):
    q_ref, k_ref, v_ref, run_ref, cols_ref = refs[:5]
    mixed_ref, state_ref, mark_ref = refs[-3 - 2 * loads :][:3]
    if loads:
        w_ref, held_ref, sem = refs[5], refs[-2], refs[-1]
        copy = pltpu.make_async_copy(w_ref.at[which], held_ref, sem)
        pl.when(pl.program_id(0) == 0)(copy.start)
    mark_ref[...] = jnp.zeros_like(mark_ref)
    rows, width = q_ref.shape[1], q_ref.shape[2] // group
    first = first_of(pl.program_id(0)) * group
    cols = pltpu.roll(cols_ref[...], 128 - first, 1)
    ri = lax.broadcasted_iota(jnp.int32, (CHUNK, CHUNK), 0)
    ci = lax.broadcasted_iota(jnp.int32, (CHUNK, CHUNK), 1)
    causal = ri >= ci
    for g in range(group):
        lanes = slice(g * width, (g + 1) * width)
        run_row = run_ref[pl.ds(first + g, 1), :]
        state = None
        for i in range(rows // CHUNK):
            part = slice(i * CHUNK, (i + 1) * CHUNK)
            q, k, v = q_ref[0, part, lanes], k_ref[0, part, lanes], v_ref[0, part, lanes]
            run_col = cols[part, g : g + 1]
            eq = cols[part, heads + g : heads + g + 1]
            ek = cols[part, 2 * heads + g : 2 * heads + g + 1]
            scores = lax.dot_general(q, k, NT, preferred_element_type=F32)
            decay = jnp.exp(jnp.where(causal, run_col - run_row[:, part], -jnp.inf))
            weights = (scores * decay).astype(BF16)
            out = lax.dot_general(weights, v, NN, preferred_element_type=F32)
            faded = (k.astype(F32) * ek).astype(BF16)
            fresh = lax.dot_general(faded, v, TN, preferred_element_type=F32)
            if state is None:
                state = fresh
            else:
                out = out + eq * lax.dot_general(
                    q, state.astype(BF16), NN, preferred_element_type=F32
                )
                state = eq[CHUNK - 1 :, :] * state + fresh
            mixed_ref[part, lanes] = out.astype(mixed_ref.dtype)
        state_ref[g] = state.astype(BF16)
    if loads:
        pl.when(pl.program_id(0) == pl.num_programs(0) - 1)(copy.wait)


def place_block(axis, turn, per):
    return lambda h: ((axis.index() + axis.n + turn) % axis.n) * per + h


def local_pass(qkv, run, cols, heads, y_axis, turn, w, which, done, behind, zeros, group=4):
    rows, width = qkv.shape[1], qkv.shape[2] // heads
    share = heads // y_axis.n
    group = min(group, share)
    block = place_block(y_axis, turn, share // group)
    loads = 0 if w is None else 1
    hbm = pl.BlockSpec(memory_space=pl.ANY)

    def take(part):
        return pl.BlockSpec((1, rows, group * width), lambda h: (part, 0, block(h)))

    more = ([w] if loads else []) + list(done) + list(behind)
    aliases = {5 + loads + i: i for i in range(len(done))}
    out_specs = [
        pl.BlockSpec((rows, group * width), lambda h: (0, block(h))),
        pl.BlockSpec((group, width, width), lambda h: (h, 0, 0)),
        pl.BlockSpec((8, zeros), lambda h: (0, 0)),
    ]
    out_shape = [
        jax.ShapeDtypeStruct((rows, heads * width), BF16),
        jax.ShapeDtypeStruct((share, width, width), BF16),
        jax.ShapeDtypeStruct((8, zeros), BF16),
    ]
    if loads:
        out_specs.append(hbm)
        out_shape.append(pltpu.VMEM(w.shape[1:], w.dtype))
    return pl.pallas_call(
        functools.partial(local_kernel, heads, group, block, loads, which),
        grid=(share // group,),
        in_specs=[
            take(0),
            take(1),
            take(2),
            pl.BlockSpec(run.shape, lambda h: (0, 0)),
            pl.BlockSpec(cols.shape, lambda h: (0, 0)),
        ]
        + [hbm] * len(more),
        out_specs=out_specs,
        out_shape=out_shape,
        scratch_shapes=[pltpu.SemaphoreType.DMA] * loads,
        input_output_aliases=aliases,
        compiler_params=params(20),
        cost_estimate=pl.CostEstimate(flops=1, bytes_accessed=1, transcendentals=0),
        name="local_pass",
    )(qkv, qkv, qkv, run, cols, *more)


def final_kernel(heads, group, first_of, *refs):
    q_ref, mixed_ref, cols_ref, carried_ref, gain_ref = refs[:5]
    out_ref, mark_ref = refs[-2:]
    mark_ref[...] = jnp.zeros_like(mark_ref)
    width = q_ref.shape[2] // group
    first = first_of(pl.program_id(0)) * group
    cols = pltpu.roll(cols_ref[...], 128 - first, 1)
    for g in range(group):
        lanes = slice(g * width, (g + 1) * width)
        er = cols[:, 3 * heads + g : 3 * heads + g + 1]
        far = lax.dot_general(q_ref[0, :, lanes], carried_ref[g], NN, preferred_element_type=F32)
        mixed = mixed_ref[:, lanes].astype(F32) + er * far
        mean = jnp.mean(mixed * mixed, axis=-1, keepdims=True)
        out_ref[:, lanes] = (mixed * lax.rsqrt(mean + EPS) * gain_ref[:, lanes]).astype(BF16)


def final_pass(qkv, mixed, cols, carried, gain, heads, y_axis, back, done, behind, zeros, group=4):
    rows, width = qkv.shape[1], qkv.shape[2] // heads
    share = carried.shape[0]
    group = min(group, share)

    block = place_block(y_axis, -back, share // group)
    more = [a for a in (done, behind) if a is not None]
    return pl.pallas_call(
        functools.partial(final_kernel, heads, group, block),
        grid=(share // group,),
        in_specs=[
            pl.BlockSpec((1, rows, group * width), lambda h: (0, 0, block(h))),
            pl.BlockSpec((rows, group * width), lambda h: (0, block(h))),
            pl.BlockSpec(cols.shape, lambda h: (0, 0)),
            pl.BlockSpec((group, width, width), lambda h: (h, 0, 0)),
            pl.BlockSpec((1, group * width), lambda h: (0, block(h))),
        ]
        + [pl.BlockSpec(memory_space=pl.ANY)] * len(more),
        out_specs=(
            pl.BlockSpec((rows, group * width), lambda h: (0, block(h))),
            pl.BlockSpec((8, zeros), lambda h: (0, 0)),
        ),
        out_shape=(
            jax.ShapeDtypeStruct((rows, heads * width), BF16),
            jax.ShapeDtypeStruct((8, zeros), BF16),
        ),
        input_output_aliases={} if done is None else {5: 0},
        compiler_params=params(20),
        cost_estimate=pl.CostEstimate(flops=1, bytes_accessed=1, transcendentals=0),
        name="final_pass",
    )(qkv, mixed, cols, carried, gain, *more)


def pick(parts, at):
    out = parts[0]
    for p in range(1, len(parts)):
        out = jnp.where((at == p).reshape((-1,) + (1,) * (out.ndim - 1)), parts[p], out)
    return out


def carry_scan(shares, last, seat, z_axis, y_axis):
    share, width = shares[0].shape[:2]
    ny = y_axis.n
    pad = 16
    y = seat[:share]
    turned = [(y + k) & (ny - 1) for k in range(ny)]
    fade = jnp.exp(last)
    mine = [pick(rows_split(fade, ny), turned[k]) for k in range(ny)]

    def packed(body, fade):
        rows = jnp.stack(pieces_of(fade), 0)
        rows = jnp.pad(rows, ((0, pad - PIECES), (0, width - share)))
        body = body.reshape(share * width, width)
        return jnp.concatenate([body.astype(BF16), rows.astype(BF16)], 0)

    def unpacked(g):
        body = g[: share * width].reshape(share, width, width).astype(F32)
        return body, jnp.sum(g[share * width :, :share].astype(F32), 0)

    got = [y_axis.send(packed(shares[k], mine[k]), k) for k in range(1, ny)]
    tie = yield
    states, fades = zip((shares[0].astype(F32), mine[0]), *[unpacked(g) for g in got])
    places = [turned[-k % ny] for k in range(ny)]

    def reach(k, end):
        r = jnp.where(places[k] < end, jnp.ones((share,), F32), 0.0)
        for m in range(ny):
            if m != k:
                r = r * jnp.where((places[m] > places[k]) & (places[m] < end), fades[m], 1.0)
        return r[:, None, None]

    def whole(end):
        r = jnp.ones((share,), F32)
        for m in range(ny):
            r = r * jnp.where(places[m] < end, fades[m], 1.0)
        return r[:, None, None]

    inner = sum(reach(k, ny) * states[k] for k in range(ny))
    through = whole(ny)
    carried, behind = jnp.zeros((share, width, width), F32), jnp.ones((share,), F32)
    first = tie[:, None]
    far = 1
    while far < z_axis.n:
        out = through * carried + inner + first
        if 2 * far < z_axis.n:
            out = packed(out, through[:, 0, 0] * behind)
        else:
            out = out.astype(BF16)
        tie = yield out
        came = lax.ppermute(out, z_axis.name, z_axis.jump(far))
        if 2 * far < z_axis.n:
            came, more = unpacked(came + tie[:1].astype(BF16))
            carried = carried + behind[:, None, None] * came
            behind = behind * more
        else:
            carried = carried + behind[:, None, None] * came.astype(F32) + tie[:, None]
        first = 0.0
        far *= 2

    def entering(j):
        end = turned[j]
        return (
            whole(end) * carried + sum(reach(k, end) * states[k] for k in range(ny))
        ).astype(BF16)

    yield [entering(0)] + [y_axis.send(entering(j), j) for j in range(1, ny)]


def hidden_kernel(steps, split, *refs):
    xs, w_ref, h_ref, gate, up = refs[:4], refs[4], refs[5], refs[6], refs[7]
    step = pl.program_id(0)

    @pl.when(step == 0)
    def _():
        gate[...] = jnp.zeros_like(gate)
        up[...] = jnp.zeros_like(up)

    def add(pair):
        x = jnp.concatenate([pair[0][...], pair[1][...]], 0)
        gate[...] += lax.dot_general(w_ref[0], x, NT, preferred_element_type=F32)
        up[...] += lax.dot_general(w_ref[1], x, NT, preferred_element_type=F32)

    pl.when(step < split)(lambda: add(xs[:2]))
    pl.when(step >= split)(lambda: add(xs[2:]))

    @pl.when(step == steps - 1)
    def _():
        g = gate[...]
        h_ref[...] = (g / (1.0 + jnp.exp(-g)) * up[...]).T.astype(BF16)


def hidden_pass(xs, w_in, block=1024):
    units, wide = w_in.shape[1], w_in.shape[2]
    tokens = xs[0].shape[0] * 2
    steps = wide // block
    split = steps // 2
    half = tokens // 2
    first = pl.BlockSpec((half, block), lambda s: (0, jnp.minimum(s, split - 1)))
    second = pl.BlockSpec((half, block), lambda s: (0, jnp.maximum(s - split, 0)))
    return pl.pallas_call(
        functools.partial(hidden_kernel, steps, split),
        grid=(steps,),
        in_specs=[first, first, second, second]
        + [pl.BlockSpec((2, units, block), lambda s: (0, 0, s))],
        out_specs=pl.BlockSpec((tokens, units), lambda s: (0, 0)),
        out_shape=jax.ShapeDtypeStruct((tokens, units), BF16),
        scratch_shapes=[pltpu.VMEM((units, tokens), F32), pltpu.VMEM((units, tokens), F32)],
        compiler_params=params(56),
        cost_estimate=pl.CostEstimate(flops=1, bytes_accessed=1, transcendentals=0),
        name="hidden_pass",
    )(*xs, w_in)


def down_kernel(h_ref, w_ref, p0_ref, p1_ref, o0_ref, o1_ref):
    half = o0_ref.shape[0]
    out = lax.dot_general(h_ref[...], w_ref[...], NN, preferred_element_type=F32)
    o0_ref[...] = (out[:half] * p0_ref[...]).astype(BF16)
    o1_ref[...] = (out[half:] * p1_ref[...]).astype(BF16)


def down_pass(h, w_out, probs, start, width, block=1024):
    tokens, units = h.shape
    half = tokens // 2
    off = start // block
    out = jax.ShapeDtypeStruct((half, width), BF16)
    spec = pl.BlockSpec((half, block), lambda s: (0, s))
    weight = pl.BlockSpec((half, 1), lambda s: (0, 0))
    return pl.pallas_call(
        down_kernel,
        grid=(width // block,),
        in_specs=[
            pl.BlockSpec((tokens, units), lambda s: (0, 0)),
            pl.BlockSpec((units, block), lambda s: (0, off + s)),
            weight,
            weight,
        ],
        out_specs=(spec, spec),
        out_shape=(out, out),
        compiler_params=params(56),
        cost_estimate=pl.CostEstimate(flops=1, bytes_accessed=1, transcendentals=0),
        name="down_pass",
    )(h, w_out, *probs)


def ordered(ref, lanes, outer, inner):
    m = ref.shape[0] // (outer * inner)
    blocks = [(i * outer + o) * m for o in range(outer) for i in range(inner)]
    return jnp.concatenate([ref[at : at + m, lanes] for at in blocks], 0)


def store_ordered(ref, lanes, value, outer, inner):
    m = ref.shape[0] // (outer * inner)
    for o in range(outer):
        for i in range(inner):
            src, dst = (o * inner + i) * m, (i * outer + o) * m
            ref[dst : dst + m, lanes] = value[src : src + m]


def own_weights(ref, lanes, experts, outer, inner):
    r = ordered(ref, lanes, outer, inner).astype(F32)
    lane = lax.broadcasted_iota(jnp.int32, r.shape, 1)
    mine = (lane % experts == lax.axis_index("exp")) & (lane < PIECES * experts)
    return jnp.sum(jnp.where(mine, r, 0.0), axis=1, keepdims=True)


def chunks(w, scratch, sems, start, width, block, first):
    out = []
    for j, at in enumerate(range(0, width, block)):
        src = w.at[(slice(None),) * (len(w.shape) - 1) + (pl.ds(start + at, block),)]
        out.append(pltpu.make_async_copy(src, scratch.at[j], sems.at[first + j]))
    return out


def lead_kernel(experts, nx, ny, block, a, a2, b, b2, wg, wu, w_out, o, o2, h, flow, mark, rest, acc, wo, sems):
    units, wide = wg.shape
    half = wide // 2
    rows = a.shape[0]
    copies = chunks(w_out, wo, sems, 0, half, block, 0)
    copies.append(
        pltpu.make_async_copy(w_out.at[:, pl.ds(half, half)], rest, sems.at[len(copies)])
    )
    for c in copies:
        c.start()
    mark[...] = jnp.zeros_like(mark)
    lanes = slice(half, half + 128)
    flow[:rows] = jnp.broadcast_to(own_weights(b, lanes, experts, nx, ny), (rows, 128))
    flow[rows:] = jnp.broadcast_to(own_weights(b2, lanes, experts, nx, ny), (rows, 128))
    for at in range(0, wide, block):
        if at < half:
            x = jnp.concatenate([a[:, at : at + block], a2[:, at : at + block]], 0)
        else:
            lanes = slice(at - half, at - half + block)
            x = jnp.concatenate([ordered(b, lanes, nx, ny), ordered(b2, lanes, nx, ny)], 0)
        for i, w in enumerate((wg, wu)):
            d = lax.dot_general(w[:, at : at + block], x, NT, preferred_element_type=F32)
            if at == 0:
                acc[i] = d
            else:
                acc[i] += d
    g = acc[0]
    h[...] = (g / (1.0 + jnp.exp(-g)) * acc[1]).T.astype(BF16)
    for j, at in enumerate(range(0, half, block)):
        copies[j].wait()
        lanes = slice(at, at + block)
        d = lax.dot_general(h[...], wo[j], NN, preferred_element_type=F32)
        d = (d * flow[:, :1]).astype(BF16)
        o[:, lanes] = d[:rows]
        o2[:, lanes] = d[rows:]
    copies[-1].wait()


def rest_kernel(nx, ny, block, h, flow, w, behind, o, o2):
    rows = o.shape[0]
    for at in range(0, w.shape[1], block):
        lanes = slice(at, at + block)
        d = lax.dot_general(h[...], w[:, lanes], NN, preferred_element_type=F32)
        d = (d * flow[:, :1]).astype(BF16)
        store_ordered(o, lanes, d[:rows], nx, ny)
        store_ordered(o2, lanes, d[rows:], nx, ny)


def lead_pass(a, a2, b, b2, held, w_out, experts, nx, ny, zeros, block=1024):
    units, wide = held[0].shape
    tokens = 2 * a.shape[0]
    n_out = wide // 2 // block
    vmem = pl.BlockSpec(memory_space=pltpu.VMEM)
    hbm = pl.BlockSpec(memory_space=pl.ANY)
    half = pltpu.VMEM((tokens // 2, wide // 2), BF16)
    mark = jax.ShapeDtypeStruct(zeros, F32)
    o, o2, h, flow, mark0, rest = pl.pallas_call(
        functools.partial(lead_kernel, experts, nx, ny, block),
        in_specs=[vmem] * 6 + [hbm],
        out_specs=(vmem,) * 6,
        out_shape=(
            half,
            half,
            pltpu.VMEM((tokens, units), BF16),
            pltpu.VMEM((tokens, 128), F32),
            mark,
            pltpu.VMEM((units, wide // 2), BF16),
        ),
        scratch_shapes=[
            pltpu.VMEM((2, units, tokens), F32),
            pltpu.VMEM((n_out, units, block), BF16),
            pltpu.SemaphoreType.DMA((n_out + 1,)),
        ],
        compiler_params=params(20),
        cost_estimate=pl.CostEstimate(flops=1, bytes_accessed=1, transcendentals=0),
        name="lead_pass",
    )(a, a2, b, b2, *held, w_out)
    return (o, o2), (h, flow, rest), mark0


def rest_pass(h, flow, w, behind, nx, ny, block=1024):
    tokens, units = h.shape
    vmem = pl.BlockSpec(memory_space=pltpu.VMEM)
    half = pltpu.VMEM((tokens // 2, w.shape[1]), BF16)
    return pl.pallas_call(
        functools.partial(rest_kernel, nx, ny, block),
        in_specs=[vmem] * 3 + [pl.BlockSpec(memory_space=pl.ANY)],
        out_specs=(vmem,) * 2,
        out_shape=(half, half),
        compiler_params=params(20),
        cost_estimate=pl.CostEstimate(flops=1, bytes_accessed=1, transcendentals=0),
        name="rest_pass",
    )(h, flow, w, behind)


def streamed_experts(a, a2, b, b2, w_in, w_out, experts, nx, ny):
    half = a.shape[1]

    def turned(r, m, n):
        return r.reshape(m, n, -1, r.shape[1]).transpose(1, 0, 2, 3).reshape(r.shape)

    b, b2 = turned(b, ny, nx), turned(b2, ny, nx)

    def weights_of(rows):
        r = rows[:, half : half + PIECES * experts].astype(F32).reshape(-1, PIECES, experts)
        mine = jnp.arange(experts)[None, None] == lax.axis_index("exp")
        return jnp.sum(jnp.where(mine, r, 0.0), axis=(1, 2))[:, None]

    flow = (weights_of(b), weights_of(b2))
    h = hidden_pass((a, a2, b, b2), w_in)
    pa = down_pass(h, w_out, flow, 0, half)
    pb = down_pass(h, w_out, flow, half, half)
    return pa, tuple(turned(p, nx, ny) for p in pb)


def route_columns(ids, probs, experts):
    named = ids[:, :, None] == jnp.arange(experts, dtype=jnp.int32)[None, None]
    weight = jnp.sum(jnp.where(named, probs[:, :, None], 0.0), axis=1)
    route = jnp.concatenate(pieces_of(weight), 1)
    return jnp.pad(route, ((0, 0), (0, 128 - route.shape[1]))).astype(BF16)


def in_hbm(a):
    return pltpu.with_memory_space_constraint(a, pltpu.HBM)


def nothing(a, rows, lanes):
    probe = a[-rows:, :lanes].astype(F32)
    return jnp.where(probe != probe, 1.0, 0.0)


def on_device(axes, projected, log_decay, norm_gain, moe_tokens, expert_ids, route_probs, w_in, w_out):
    x_axis, core, z_axis, y_axis = axes
    nx, ny, nz = x_axis.n, y_axis.n, z_axis.n
    heads = log_decay.shape[1]
    half = moe_tokens.shape[1] // 2
    experts = w_in.shape[0] * lax.axis_size("exp")
    tokens = moe_tokens.shape[0] * lax.axis_size("seq") * lax.axis_size("exp")
    fits = tokens <= 512 and ny == 2
    zeros = (heads // ny, projected.shape[2] // heads)
    qkv = in_hbm(projected.transpose(1, 0, 2))
    w_in = w_in[0].transpose(1, 2, 0)
    w_out = w_out[0]
    route = route_columns(expert_ids, route_probs, experts)

    z = gather(z_axis, jnp.concatenate([moe_tokens, route], 1))
    run, cols, seat = prepare(log_decay)
    done, held, shares = (), [], {}
    for i in range(ny):
        turn = (i + 1) % ny
        w = in_hbm(w_in) if fits else None
        behind = (z,) * (i == ny - 1)
        made = local_pass(
            qkv, run, cols, heads, y_axis, turn, w, i, done, behind, z.shape[1] - half
        )
        done, shares[turn], mark = made[:1], made[1], made[2]
        held += made[3:]
    mixed = done[0]
    scan = carry_scan(shares, run[:, -1], seat[:, 0] & (ny - 1), z_axis, y_axis)
    next(scan)
    a, b = z[:, :half], z[:, half:]
    a, b = gather(y_axis, a), gather(x_axis, b)
    a, b = gather(x_axis, a + mark[:1, :half]), gather(y_axis, b + mark[:1])
    scan.send(nothing(a, *zeros))
    a2, b2 = core.send(a, 1), core.send(b, 1)
    if fits:
        pa, more, mark = lead_pass(
            a, a2, b, b2, held, in_hbm(w_out), experts, nx, ny, zeros
        )
        hop = scan.send(mark)
        pb = rest_pass(*more, hop, nx, ny)
    else:
        pa, pb = streamed_experts(a, a2, b, b2, w_in, w_out, experts, nx, ny)
        scan.send(jnp.zeros(zeros, F32))
    for _ in range((nz - 1).bit_length() - 2):
        scan.send(jnp.zeros(zeros, F32))
    a, b = scatter(core, pa), scatter(core, pb)
    a, b = scatter(x_axis, rows_split(a, nx)), scatter(y_axis, rows_split(b, ny))
    carried = scan.send(nothing(a, *zeros))
    attn_out = None

    def final(k, behind):
        gain = norm_gain[None]
        return final_pass(
            qkv, mixed, cols, carried[k], gain, heads, y_axis, k, attn_out, behind, 2 * half
        )

    attn_out, mark = final(0, a)
    a, b = scatter(y_axis, rows_split(a, ny)), scatter(x_axis, rows_split(b, nx))
    both = jnp.concatenate([a, b], 1) + mark[:1]
    for k in range(1, ny):
        attn_out, _ = final(k, both)
    moe_out = scatter(z_axis, rows_split(both, nz))
    return attn_out, moe_out


def solution(mesh):
    nz, ny = factors(mesh.shape["seq"])
    nx = mesh.shape["exp"] // 2
    axes = (
        Axis("exp", nx, 2, 1),
        Axis("exp", 2, 1, nx),
        Axis("seq", nz, ny, 1),
        Axis("seq", ny, 1, nz),
    )
    in_specs = (
        P("seq", None, "exp"),
        P("seq", "exp"),
        P("exp"),
        P(("seq", "exp"), None),
        P(("seq", "exp"), None),
        P(("seq", "exp"), None),
        P("exp", None, None, "seq"),
        P("exp", "seq", None),
    )
    out_specs = (P("seq", "exp"), P(("seq", "exp"), None))
    return jax.shard_map(
        functools.partial(on_device, axes),
        mesh=mesh,
        in_specs=in_specs,
        out_specs=out_specs,
        check_vma=False,
    )
```

```python
import functools
import jax
import jax.numpy as jnp
from jax import lax
from jax.experimental import pallas as pl
from jax.experimental.pallas import tpu as pltpu
from jax.sharding import PartitionSpec as P

EPS = 1e-06
CHUNK = 256
PIECES = 3
F32 = jnp.float32
BF16 = jnp.bfloat16
NT = (((1,), (1,)), ((), ()))
TN = (((0,), (0,)), ((), ()))
NN = (((1,), (0,)), ((), ()))


def factors(size):
    bits = size.bit_length() - 1
    inner = 2 ** (bits // 2)
    return size // inner, inner


class Axis:
    def __init__(self, name, n, inner, outer):
        self.name, self.n, self.inner, self.outer = name, n, inner, outer

    def index(self):
        return (lax.axis_index(self.name) // self.inner) % self.n

    def flat(self, o, i, j):
        return (o * self.n + i) * self.inner + j

    def turn(self, k):
        return [
            (self.flat(o, i, j), self.flat(o, (i + k) % self.n, j))
            for o in range(self.outer)
            for i in range(self.n)
            for j in range(self.inner)
        ]

    def pairs(self, step, upwards):
        return [
            (self.flat(o, i, j), self.flat(o, i ^ step, j))
            for o in range(self.outer)
            for i in range(self.n)
            for j in range(self.inner)
            if not (upwards and i & step)
        ]

    def send(self, a, k):
        return lax.ppermute(a, self.name, self.turn(k))


def gather(axis, a):
    return jnp.concatenate([a] + [axis.send(a, k) for k in range(1, axis.n)], 0)


def total(parts):
    s = parts[0].astype(F32)
    for p in parts[1:]:
        s = s + p.astype(F32)
    return s.astype(BF16)


def scatter(axis, parts):
    return total([parts[0]] + [axis.send(parts[k], axis.n - k) for k in range(1, axis.n)])


def rows_split(a, n):
    m = a.shape[0] // n
    return [a[i * m : (i + 1) * m] for i in range(n)]


def pieces_of(x):
    out = []
    for _ in range(PIECES):
        hi = lax.reduce_precision(x, 8, 7)
        out.append(hi)
        x = x - hi
    return out


def params(limit=16):
    return pltpu.CompilerParams(vmem_limit_bytes=limit * 2**20)


def prep_kernel(heads, rows, d_ref, run_ref, cols_ref, seat_ref):
    seat_ref[...] = jnp.zeros_like(seat_ref) + lax.axis_index("seq")
    run = d_ref[...]
    lane = lax.broadcasted_iota(jnp.int32, (heads, rows), 1)
    step = 1
    while step < rows:
        run = run + jnp.where(lane >= step, pltpu.roll(run, step, 1), 0.0)
        step *= 2
    enter = jnp.zeros((heads, 1), F32)
    before, after = [], []
    for i in range(rows // CHUNK):
        leave = run[:, (i + 1) * CHUNK - 1 : (i + 1) * CHUNK]
        before.append(jnp.broadcast_to(enter, (heads, CHUNK)))
        after.append(jnp.broadcast_to(leave, (heads, CHUNK)))
        enter = leave
    eq = jnp.exp(run - jnp.concatenate(before, 1))
    ek = jnp.exp(jnp.concatenate(after, 1) - run)
    run_ref[...] = run
    tall = jnp.concatenate([run, eq, ek, jnp.exp(run)], 0)
    if 4 * heads < 128:
        tall = jnp.concatenate([tall, jnp.zeros((128 - 4 * heads, rows), F32)], 0)
    cols_ref[...] = tall.T


def prepare(log_decay):
    rows, heads = log_decay.shape
    return pl.pallas_call(
        functools.partial(prep_kernel, heads, rows),
        out_shape=(
            jax.ShapeDtypeStruct((heads, rows), F32),
            jax.ShapeDtypeStruct((rows, 128), F32),
            jax.ShapeDtypeStruct((heads, 128), jnp.int32),
        ),
        compiler_params=params(),
        name="prepare",
    )(log_decay.T)


def local_kernel(heads, group, first_of, loads, which, *refs):
    q_ref, k_ref, v_ref, run_ref, cols_ref = refs[:5]
    mixed_ref, state_ref, mark_ref = refs[-3 - 2 * loads :][:3]
    if loads:
        w_ref, held_ref, sem = refs[5], refs[-2], refs[-1]
        copy = pltpu.make_async_copy(w_ref.at[which], held_ref, sem)
        pl.when(pl.program_id(0) == 0)(copy.start)
    mark_ref[...] = jnp.zeros_like(mark_ref)
    rows, width = q_ref.shape[1], q_ref.shape[2] // group
    first = first_of(pl.program_id(0)) * group
    cols = pltpu.roll(cols_ref[...], 128 - first, 1)
    ri = lax.broadcasted_iota(jnp.int32, (CHUNK, CHUNK), 0)
    ci = lax.broadcasted_iota(jnp.int32, (CHUNK, CHUNK), 1)
    causal = ri >= ci
    for g in range(group):
        lanes = slice(g * width, (g + 1) * width)
        run_row = run_ref[pl.ds(first + g, 1), :]
        state = None
        for i in range(rows // CHUNK):
            part = slice(i * CHUNK, (i + 1) * CHUNK)
            q, k, v = q_ref[0, part, lanes], k_ref[0, part, lanes], v_ref[0, part, lanes]
            run_col = cols[part, g : g + 1]
            eq = cols[part, heads + g : heads + g + 1]
            ek = cols[part, 2 * heads + g : 2 * heads + g + 1]
            scores = lax.dot_general(q, k, NT, preferred_element_type=F32)
            decay = jnp.exp(jnp.where(causal, run_col - run_row[:, part], -jnp.inf))
            weights = (scores * decay).astype(BF16)
            out = lax.dot_general(weights, v, NN, preferred_element_type=F32)
            faded = (k.astype(F32) * ek).astype(BF16)
            fresh = lax.dot_general(faded, v, TN, preferred_element_type=F32)
            if state is None:
                state = fresh
            else:
                out = out + eq * lax.dot_general(
                    q, state.astype(BF16), NN, preferred_element_type=F32
                )
                state = eq[CHUNK - 1 :, :] * state + fresh
            mixed_ref[part, lanes] = out.astype(mixed_ref.dtype)
        state_ref[g] = state.astype(BF16)
    if loads:
        pl.when(pl.program_id(0) == pl.num_programs(0) - 1)(copy.wait)


def place_block(axis, turn, per):
    return lambda h: ((axis.index() + axis.n + turn) % axis.n) * per + h


def local_pass(qkv, run, cols, heads, y_axis, turn, w, which, done, behind, zeros, group=4):
    rows, width = qkv.shape[1], qkv.shape[2] // heads
    share = heads // y_axis.n
    group = min(group, share)
    block = place_block(y_axis, turn, share // group)
    loads = 0 if w is None else 1
    hbm = pl.BlockSpec(memory_space=pl.ANY)

    def take(part):
        return pl.BlockSpec((1, rows, group * width), lambda h: (part, 0, block(h)))

    more = ([w] if loads else []) + list(done) + list(behind)
    aliases = {5 + loads + i: i for i in range(len(done))}
    out_specs = [
        pl.BlockSpec((rows, group * width), lambda h: (0, block(h))),
        pl.BlockSpec((group, width, width), lambda h: (h, 0, 0)),
        pl.BlockSpec((8, zeros), lambda h: (0, 0)),
    ]
    out_shape = [
        jax.ShapeDtypeStruct((rows, heads * width), BF16),
        jax.ShapeDtypeStruct((share, width, width), BF16),
        jax.ShapeDtypeStruct((8, zeros), BF16),
    ]
    if loads:
        out_specs.append(hbm)
        out_shape.append(pltpu.VMEM(w.shape[1:], w.dtype))
    return pl.pallas_call(
        functools.partial(local_kernel, heads, group, block, loads, which),
        grid=(share // group,),
        in_specs=[
            take(0),
            take(1),
            take(2),
            pl.BlockSpec(run.shape, lambda h: (0, 0)),
            pl.BlockSpec(cols.shape, lambda h: (0, 0)),
        ]
        + [hbm] * len(more),
        out_specs=out_specs,
        out_shape=out_shape,
        scratch_shapes=[pltpu.SemaphoreType.DMA] * loads,
        input_output_aliases=aliases,
        compiler_params=params(20),
        cost_estimate=pl.CostEstimate(flops=1, bytes_accessed=1, transcendentals=0),
        name="local_pass",
    )(qkv, qkv, qkv, run, cols, *more)


def final_kernel(heads, group, first_of, *refs):
    q_ref, mixed_ref, cols_ref, carried_ref, gain_ref = refs[:5]
    out_ref, mark_ref = refs[-2:]
    mark_ref[...] = jnp.zeros_like(mark_ref)
    width = q_ref.shape[2] // group
    first = first_of(pl.program_id(0)) * group
    cols = pltpu.roll(cols_ref[...], 128 - first, 1)
    for g in range(group):
        lanes = slice(g * width, (g + 1) * width)
        er = cols[:, 3 * heads + g : 3 * heads + g + 1]
        far = lax.dot_general(q_ref[0, :, lanes], carried_ref[g], NN, preferred_element_type=F32)
        mixed = mixed_ref[:, lanes].astype(F32) + er * far
        mean = jnp.mean(mixed * mixed, axis=-1, keepdims=True)
        out_ref[:, lanes] = (mixed * lax.rsqrt(mean + EPS) * gain_ref[:, lanes]).astype(BF16)


def final_pass(qkv, mixed, cols, carried, gain, heads, y_axis, back, done, behind, zeros, group=4):
    rows, width = qkv.shape[1], qkv.shape[2] // heads
    share = carried.shape[0]
    group = min(group, share)

    block = place_block(y_axis, -back, share // group)
    more = [a for a in (done, behind) if a is not None]
    return pl.pallas_call(
        functools.partial(final_kernel, heads, group, block),
        grid=(share // group,),
        in_specs=[
            pl.BlockSpec((1, rows, group * width), lambda h: (0, 0, block(h))),
            pl.BlockSpec((rows, group * width), lambda h: (0, block(h))),
            pl.BlockSpec(cols.shape, lambda h: (0, 0)),
            pl.BlockSpec((group, width, width), lambda h: (h, 0, 0)),
            pl.BlockSpec((1, group * width), lambda h: (0, block(h))),
        ]
        + [pl.BlockSpec(memory_space=pl.ANY)] * len(more),
        out_specs=(
            pl.BlockSpec((rows, group * width), lambda h: (0, block(h))),
            pl.BlockSpec((8, zeros), lambda h: (0, 0)),
        ),
        out_shape=(
            jax.ShapeDtypeStruct((rows, heads * width), BF16),
            jax.ShapeDtypeStruct((8, zeros), BF16),
        ),
        input_output_aliases={} if done is None else {5: 0},
        compiler_params=params(20),
        cost_estimate=pl.CostEstimate(flops=1, bytes_accessed=1, transcendentals=0),
        name="final_pass",
    )(qkv, mixed, cols, carried, gain, *more)


def pick(parts, at):
    out = parts[0]
    for p in range(1, len(parts)):
        out = jnp.where((at == p).reshape((-1,) + (1,) * (out.ndim - 1)), parts[p], out)
    return out


def carry_scan(shares, last, seat, z_axis, y_axis):
    share, width = shares[0].shape[:2]
    ny = y_axis.n
    pad = 16
    y = seat[:share] & (ny - 1)
    turned = [(y + k) & (ny - 1) for k in range(ny)]
    fade = jnp.exp(last)
    mine = [pick(rows_split(fade, ny), turned[k]) for k in range(ny)]

    def packed(body, fade):
        rows = jnp.stack(pieces_of(fade), 0)
        rows = jnp.pad(rows, ((0, pad - PIECES), (0, width - share)))
        body = body.reshape(share * width, width)
        return jnp.concatenate([body.astype(BF16), rows.astype(BF16)], 0)

    def unpacked(g):
        body = g[: share * width].reshape(share, width, width).astype(F32)
        return body, jnp.sum(g[share * width :, :share].astype(F32), 0)

    got = [y_axis.send(packed(shares[k], mine[k]), k) for k in range(1, ny)]
    tie = yield
    states, fades = zip((shares[0].astype(F32), mine[0]), *[unpacked(g) for g in got])
    places = [turned[-k % ny] for k in range(ny)]

    def reach(k, end):
        r = jnp.where(places[k] < end, jnp.ones((share,), F32), 0.0)
        for m in range(ny):
            if m != k:
                r = r * jnp.where((places[m] > places[k]) & (places[m] < end), fades[m], 1.0)
        return r[:, None, None]

    def whole(end):
        r = jnp.ones((share,), F32)
        for m in range(ny):
            r = r * jnp.where(places[m] < end, fades[m], 1.0)
        return r[:, None, None]

    inner = sum(reach(k, ny) * states[k] for k in range(ny))
    through = whole(ny)
    carried, behind = jnp.zeros((share, width, width), F32), jnp.ones((share,), F32)
    group, fall = inner + tie[:, None], through[:, 0, 0]
    z = seat[:share] >> (ny.bit_length() - 1)
    step = 1
    while step < z_axis.n:
        upper = (z & step) != 0
        last_step = 2 * step == z_axis.n
        out = group.astype(BF16) if last_step else packed(group, fall)
        tie = yield out
        came = lax.ppermute(out, z_axis.name, z_axis.pairs(step, last_step))
        if last_step:
            came = came.astype(F32) + tie[:, None]
        else:
            came, more = unpacked(came + tie[:1].astype(BF16))
            group = (
                jnp.where(upper, 1.0, more)[:, None, None] * group
                + jnp.where(upper, fall, 1.0)[:, None, None] * came
            )
        carried = carried + jnp.where(upper, behind, 0.0)[:, None, None] * came
        if not last_step:
            behind, fall = jnp.where(upper, behind * more, behind), fall * more
        step *= 2

    def entering(j):
        end = turned[j]
        return (
            whole(end) * carried + sum(reach(k, end) * states[k] for k in range(ny))
        ).astype(BF16)

    yield [entering(0)] + [y_axis.send(entering(j), j) for j in range(1, ny)]


def hidden_kernel(steps, split, *refs):
    xs, w_ref, h_ref, gate, up = refs[:4], refs[4], refs[5], refs[6], refs[7]
    step = pl.program_id(0)

    @pl.when(step == 0)
    def _():
        gate[...] = jnp.zeros_like(gate)
        up[...] = jnp.zeros_like(up)

    def add(pair):
        x = jnp.concatenate([pair[0][...], pair[1][...]], 0)
        gate[...] += lax.dot_general(w_ref[0], x, NT, preferred_element_type=F32)
        up[...] += lax.dot_general(w_ref[1], x, NT, preferred_element_type=F32)

    pl.when(step < split)(lambda: add(xs[:2]))
    pl.when(step >= split)(lambda: add(xs[2:]))

    @pl.when(step == steps - 1)
    def _():
        g = gate[...]
        h_ref[...] = (g / (1.0 + jnp.exp(-g)) * up[...]).T.astype(BF16)


def hidden_pass(xs, w_in, block=1024):
    units, wide = w_in.shape[1], w_in.shape[2]
    tokens = xs[0].shape[0] * 2
    steps = wide // block
    split = steps // 2
    half = tokens // 2
    first = pl.BlockSpec((half, block), lambda s: (0, jnp.minimum(s, split - 1)))
    second = pl.BlockSpec((half, block), lambda s: (0, jnp.maximum(s - split, 0)))
    return pl.pallas_call(
        functools.partial(hidden_kernel, steps, split),
        grid=(steps,),
        in_specs=[first, first, second, second]
        + [pl.BlockSpec((2, units, block), lambda s: (0, 0, s))],
        out_specs=pl.BlockSpec((tokens, units), lambda s: (0, 0)),
        out_shape=jax.ShapeDtypeStruct((tokens, units), BF16),
        scratch_shapes=[pltpu.VMEM((units, tokens), F32), pltpu.VMEM((units, tokens), F32)],
        compiler_params=params(56),
        cost_estimate=pl.CostEstimate(flops=1, bytes_accessed=1, transcendentals=0),
        name="hidden_pass",
    )(*xs, w_in)


def down_kernel(h_ref, w_ref, p0_ref, p1_ref, o0_ref, o1_ref):
    half = o0_ref.shape[0]
    out = lax.dot_general(h_ref[...], w_ref[...], NN, preferred_element_type=F32)
    o0_ref[...] = (out[:half] * p0_ref[...]).astype(BF16)
    o1_ref[...] = (out[half:] * p1_ref[...]).astype(BF16)


def down_pass(h, w_out, probs, start, width, block=1024):
    tokens, units = h.shape
    half = tokens // 2
    off = start // block
    out = jax.ShapeDtypeStruct((half, width), BF16)
    spec = pl.BlockSpec((half, block), lambda s: (0, s))
    weight = pl.BlockSpec((half, 1), lambda s: (0, 0))
    return pl.pallas_call(
        down_kernel,
        grid=(width // block,),
        in_specs=[
            pl.BlockSpec((tokens, units), lambda s: (0, 0)),
            pl.BlockSpec((units, block), lambda s: (0, off + s)),
            weight,
            weight,
        ],
        out_specs=(spec, spec),
        out_shape=(out, out),
        compiler_params=params(56),
        cost_estimate=pl.CostEstimate(flops=1, bytes_accessed=1, transcendentals=0),
        name="down_pass",
    )(h, w_out, *probs)


def ordered(ref, lanes, outer, inner):
    m = ref.shape[0] // (outer * inner)
    blocks = [(i * outer + o) * m for o in range(outer) for i in range(inner)]
    return jnp.concatenate([ref[at : at + m, lanes] for at in blocks], 0)


def store_ordered(ref, lanes, value, outer, inner):
    m = ref.shape[0] // (outer * inner)
    for o in range(outer):
        for i in range(inner):
            src, dst = (o * inner + i) * m, (i * outer + o) * m
            ref[dst : dst + m, lanes] = value[src : src + m]


def own_weights(ref, lanes, experts, outer, inner):
    r = ordered(ref, lanes, outer, inner).astype(F32)
    lane = lax.broadcasted_iota(jnp.int32, r.shape, 1)
    mine = (lane % experts == lax.axis_index("exp")) & (lane < PIECES * experts)
    return jnp.sum(jnp.where(mine, r, 0.0), axis=1, keepdims=True)


def chunks(w, scratch, sems, start, width, block, first):
    out = []
    for j, at in enumerate(range(0, width, block)):
        src = w.at[(slice(None),) * (len(w.shape) - 1) + (pl.ds(start + at, block),)]
        out.append(pltpu.make_async_copy(src, scratch.at[j], sems.at[first + j]))
    return out


def lead_kernel(experts, nx, ny, block, a, a2, b, b2, wg, wu, w_out, o, o2, h, flow, mark, rest, acc, wo, sems):
    units, wide = wg.shape
    half = wide // 2
    rows = a.shape[0]
    copies = chunks(w_out, wo, sems, 0, half, block, 0)
    copies.append(
        pltpu.make_async_copy(w_out.at[:, pl.ds(half, half)], rest, sems.at[len(copies)])
    )
    for c in copies:
        c.start()
    mark[...] = jnp.zeros_like(mark)
    lanes = slice(half, half + 128)
    flow[:rows] = jnp.broadcast_to(own_weights(b, lanes, experts, nx, ny), (rows, 128))
    flow[rows:] = jnp.broadcast_to(own_weights(b2, lanes, experts, nx, ny), (rows, 128))
    for at in range(0, wide, block):
        if at < half:
            x = jnp.concatenate([a[:, at : at + block], a2[:, at : at + block]], 0)
        else:
            lanes = slice(at - half, at - half + block)
            x = jnp.concatenate([ordered(b, lanes, nx, ny), ordered(b2, lanes, nx, ny)], 0)
        for i, w in enumerate((wg, wu)):
            d = lax.dot_general(w[:, at : at + block], x, NT, preferred_element_type=F32)
            if at == 0:
                acc[i] = d
            else:
                acc[i] += d
    g = acc[0]
    h[...] = (g / (1.0 + jnp.exp(-g)) * acc[1]).T.astype(BF16)
    for j, at in enumerate(range(0, half, block)):
        copies[j].wait()
        lanes = slice(at, at + block)
        d = lax.dot_general(h[...], wo[j], NN, preferred_element_type=F32)
        d = (d * flow[:, :1]).astype(BF16)
        o[:, lanes] = d[:rows]
        o2[:, lanes] = d[rows:]
    copies[-1].wait()


def rest_kernel(nx, ny, block, h, flow, w, behind, o, o2):
    rows = o.shape[0]
    for at in range(0, w.shape[1], block):
        lanes = slice(at, at + block)
        d = lax.dot_general(h[...], w[:, lanes], NN, preferred_element_type=F32)
        d = (d * flow[:, :1]).astype(BF16)
        store_ordered(o, lanes, d[:rows], nx, ny)
        store_ordered(o2, lanes, d[rows:], nx, ny)


def lead_pass(a, a2, b, b2, held, w_out, experts, nx, ny, zeros, block=1024):
    units, wide = held[0].shape
    tokens = 2 * a.shape[0]
    n_out = wide // 2 // block
    vmem = pl.BlockSpec(memory_space=pltpu.VMEM)
    hbm = pl.BlockSpec(memory_space=pl.ANY)
    half = pltpu.VMEM((tokens // 2, wide // 2), BF16)
    mark = jax.ShapeDtypeStruct(zeros, F32)
    o, o2, h, flow, mark0, rest = pl.pallas_call(
        functools.partial(lead_kernel, experts, nx, ny, block),
        in_specs=[vmem] * 6 + [hbm],
        out_specs=(vmem,) * 6,
        out_shape=(
            half,
            half,
            pltpu.VMEM((tokens, units), BF16),
            pltpu.VMEM((tokens, 128), F32),
            mark,
            pltpu.VMEM((units, wide // 2), BF16),
        ),
        scratch_shapes=[
            pltpu.VMEM((2, units, tokens), F32),
            pltpu.VMEM((n_out, units, block), BF16),
            pltpu.SemaphoreType.DMA((n_out + 1,)),
        ],
        compiler_params=params(20),
        cost_estimate=pl.CostEstimate(flops=1, bytes_accessed=1, transcendentals=0),
        name="lead_pass",
    )(a, a2, b, b2, *held, w_out)
    return (o, o2), (h, flow, rest), mark0


def rest_pass(h, flow, w, behind, nx, ny, block=1024):
    tokens, units = h.shape
    vmem = pl.BlockSpec(memory_space=pltpu.VMEM)
    half = pltpu.VMEM((tokens // 2, w.shape[1]), BF16)
    return pl.pallas_call(
        functools.partial(rest_kernel, nx, ny, block),
        in_specs=[vmem] * 3 + [pl.BlockSpec(memory_space=pl.ANY)],
        out_specs=(vmem,) * 2,
        out_shape=(half, half),
        compiler_params=params(20),
        cost_estimate=pl.CostEstimate(flops=1, bytes_accessed=1, transcendentals=0),
        name="rest_pass",
    )(h, flow, w, behind)


def streamed_experts(a, a2, b, b2, w_in, w_out, experts, nx, ny):
    half = a.shape[1]

    def turned(r, m, n):
        return r.reshape(m, n, -1, r.shape[1]).transpose(1, 0, 2, 3).reshape(r.shape)

    b, b2 = turned(b, ny, nx), turned(b2, ny, nx)

    def weights_of(rows):
        r = rows[:, half : half + PIECES * experts].astype(F32).reshape(-1, PIECES, experts)
        mine = jnp.arange(experts)[None, None] == lax.axis_index("exp")
        return jnp.sum(jnp.where(mine, r, 0.0), axis=(1, 2))[:, None]

    flow = (weights_of(b), weights_of(b2))
    h = hidden_pass((a, a2, b, b2), w_in)
    pa = down_pass(h, w_out, flow, 0, half)
    pb = down_pass(h, w_out, flow, half, half)
    return pa, tuple(turned(p, nx, ny) for p in pb)


def route_columns(ids, probs, experts):
    named = ids[:, :, None] == jnp.arange(experts, dtype=jnp.int32)[None, None]
    weight = jnp.sum(jnp.where(named, probs[:, :, None], 0.0), axis=1)
    route = jnp.concatenate(pieces_of(weight), 1)
    return jnp.pad(route, ((0, 0), (0, 128 - route.shape[1]))).astype(BF16)


def in_hbm(a):
    return pltpu.with_memory_space_constraint(a, pltpu.HBM)


def nothing(a, rows, lanes):
    probe = a[-rows:, :lanes].astype(F32)
    return jnp.where(probe != probe, 1.0, 0.0)


def on_device(axes, projected, log_decay, norm_gain, moe_tokens, expert_ids, route_probs, w_in, w_out):
    x_axis, core, z_axis, y_axis = axes
    nx, ny, nz = x_axis.n, y_axis.n, z_axis.n
    heads = log_decay.shape[1]
    half = moe_tokens.shape[1] // 2
    experts = w_in.shape[0] * lax.axis_size("exp")
    tokens = moe_tokens.shape[0] * lax.axis_size("seq") * lax.axis_size("exp")
    fits = tokens <= 512 and ny == 2
    zeros = (heads // ny, projected.shape[2] // heads)
    qkv = in_hbm(projected.transpose(1, 0, 2))
    w_in = w_in[0].transpose(1, 2, 0)
    w_out = w_out[0]
    route = route_columns(expert_ids, route_probs, experts)

    z = gather(z_axis, jnp.concatenate([moe_tokens, route], 1))
    run, cols, seat = prepare(log_decay)
    done, held, shares = (), [], {}
    for i in range(ny):
        turn = (i + 1) % ny
        w = in_hbm(w_in) if fits else None
        behind = (z,) * (i == ny - 1)
        made = local_pass(
            qkv, run, cols, heads, y_axis, turn, w, i, done, behind, z.shape[1] - half
        )
        done, shares[turn], mark = made[:1], made[1], made[2]
        held += made[3:]
    mixed = done[0]
    scan = carry_scan(shares, run[:, -1], seat[:, 0], z_axis, y_axis)
    next(scan)
    a, b = z[:, :half], z[:, half:]
    a, b = gather(y_axis, a), gather(x_axis, b)
    a, b = gather(x_axis, a + mark[:1, :half]), gather(y_axis, b + mark[:1])
    scan.send(nothing(a, *zeros))
    a2, b2 = core.send(a, 1), core.send(b, 1)
    if fits:
        pa, more, mark = lead_pass(
            a, a2, b, b2, held, in_hbm(w_out), experts, nx, ny, zeros
        )
        hop = scan.send(mark)
        pb = rest_pass(*more, hop, nx, ny)
    else:
        pa, pb = streamed_experts(a, a2, b, b2, w_in, w_out, experts, nx, ny)
        scan.send(jnp.zeros(zeros, F32))
    for _ in range((nz - 1).bit_length() - 2):
        scan.send(jnp.zeros(zeros, F32))
    a, b = scatter(core, pa), scatter(core, pb)
    a, b = scatter(x_axis, rows_split(a, nx)), scatter(y_axis, rows_split(b, ny))
    carried = scan.send(nothing(a, *zeros))
    attn_out = None

    def final(k, behind):
        gain = norm_gain[None]
        return final_pass(
            qkv, mixed, cols, carried[k], gain, heads, y_axis, k, attn_out, behind, 2 * half
        )

    attn_out, mark = final(0, a)
    a, b = scatter(y_axis, rows_split(a, ny)), scatter(x_axis, rows_split(b, nx))
    both = jnp.concatenate([a, b], 1) + mark[:1]
    for k in range(1, ny):
        attn_out, _ = final(k, both)
    moe_out = scatter(z_axis, rows_split(both, nz))
    return attn_out, moe_out


def solution(mesh):
    nz, ny = factors(mesh.shape["seq"])
    nx = mesh.shape["exp"] // 2
    axes = (
        Axis("exp", nx, 2, 1),
        Axis("exp", 2, 1, nx),
        Axis("seq", nz, ny, 1),
        Axis("seq", ny, 1, nz),
    )
    in_specs = (
        P("seq", None, "exp"),
        P("seq", "exp"),
        P("exp"),
        P(("seq", "exp"), None),
        P(("seq", "exp"), None),
        P(("seq", "exp"), None),
        P("exp", None, None, "seq"),
        P("exp", "seq", None),
    )
    out_specs = (P("seq", "exp"), P(("seq", "exp"), None))
    return jax.shard_map(
        functools.partial(on_device, axes),
        mesh=mesh,
        in_specs=in_specs,
        out_specs=out_specs,
        check_vma=False,
    )
```

```python
import functools
import jax
import jax.numpy as jnp
from jax import lax
from jax.experimental import pallas as pl
from jax.experimental.pallas import tpu as pltpu
from jax.sharding import PartitionSpec as P

EPS = 1e-06
CHUNK = 256
PIECES = 3
F32 = jnp.float32
BF16 = jnp.bfloat16
NT = (((1,), (1,)), ((), ()))
TN = (((0,), (0,)), ((), ()))
NN = (((1,), (0,)), ((), ()))


def factors(size):
    bits = size.bit_length() - 1
    inner = 2 ** (bits // 2)
    return size // inner, inner


class Axis:
    def __init__(self, name, n, inner, outer):
        self.name, self.n, self.inner, self.outer = name, n, inner, outer

    def index(self):
        return (lax.axis_index(self.name) // self.inner) % self.n

    def flat(self, o, i, j):
        return (o * self.n + i) * self.inner + j

    def turn(self, k):
        return [
            (self.flat(o, i, j), self.flat(o, (i + k) % self.n, j))
            for o in range(self.outer)
            for i in range(self.n)
            for j in range(self.inner)
        ]

    def pairs(self, step, upwards):
        return [
            (self.flat(o, i, j), self.flat(o, i ^ step, j))
            for o in range(self.outer)
            for i in range(self.n)
            for j in range(self.inner)
            if not (upwards and i & step)
        ]

    def send(self, a, k):
        return lax.ppermute(a, self.name, self.turn(k))


def parts_of(axis, a):
    return [a] + [axis.send(a, k) for k in range(1, axis.n)]


def gather(axis, a):
    return jnp.concatenate(parts_of(axis, a), 0)


def total(parts):
    s = parts[0].astype(F32)
    for p in parts[1:]:
        s = s + p.astype(F32)
    return s.astype(BF16)


def scatter(axis, parts):
    return total([parts[0]] + [axis.send(parts[k], axis.n - k) for k in range(1, axis.n)])


def rows_split(a, n):
    m = a.shape[0] // n
    return [a[i * m : (i + 1) * m] for i in range(n)]


def pieces_of(x):
    out = []
    for _ in range(PIECES):
        hi = lax.reduce_precision(x, 8, 7)
        out.append(hi)
        x = x - hi
    return out


def params(limit=16):
    return pltpu.CompilerParams(vmem_limit_bytes=limit * 2**20)


def prep_kernel(heads, rows, d_ref, run_ref, cols_ref, seat_ref):
    seat_ref[...] = jnp.zeros_like(seat_ref) + lax.axis_index("seq")
    run = d_ref[...]
    lane = lax.broadcasted_iota(jnp.int32, (heads, rows), 1)
    step = 1
    while step < rows:
        run = run + jnp.where(lane >= step, pltpu.roll(run, step, 1), 0.0)
        step *= 2
    enter = jnp.zeros((heads, 1), F32)
    before, after = [], []
    for i in range(rows // CHUNK):
        leave = run[:, (i + 1) * CHUNK - 1 : (i + 1) * CHUNK]
        before.append(jnp.broadcast_to(enter, (heads, CHUNK)))
        after.append(jnp.broadcast_to(leave, (heads, CHUNK)))
        enter = leave
    eq = jnp.exp(run - jnp.concatenate(before, 1))
    ek = jnp.exp(jnp.concatenate(after, 1) - run)
    run_ref[...] = run
    tall = jnp.concatenate([run, eq, ek, jnp.exp(run)], 0)
    if 4 * heads < 128:
        tall = jnp.concatenate([tall, jnp.zeros((128 - 4 * heads, rows), F32)], 0)
    cols_ref[...] = tall.T


def prepare(log_decay):
    rows, heads = log_decay.shape
    return pl.pallas_call(
        functools.partial(prep_kernel, heads, rows),
        out_shape=(
            jax.ShapeDtypeStruct((heads, rows), F32),
            jax.ShapeDtypeStruct((rows, 128), F32),
            jax.ShapeDtypeStruct((heads, 128), jnp.int32),
        ),
        compiler_params=params(),
        name="prepare",
    )(log_decay.T)


def local_kernel(heads, group, first_of, loads, which, *refs):
    q_ref, k_ref, v_ref, run_ref, cols_ref = refs[:5]
    mixed_ref, state_ref, mark_ref = refs[-3 - 2 * loads :][:3]
    if loads:
        w_ref, held_ref, sem = refs[5], refs[-2], refs[-1]
        copy = pltpu.make_async_copy(w_ref.at[which], held_ref, sem)
        pl.when(pl.program_id(0) == 0)(copy.start)
    mark_ref[...] = jnp.zeros_like(mark_ref)
    rows, width = q_ref.shape[1], q_ref.shape[2] // group
    first = first_of(pl.program_id(0)) * group
    cols = pltpu.roll(cols_ref[...], 128 - first, 1)
    ri = lax.broadcasted_iota(jnp.int32, (CHUNK, CHUNK), 0)
    ci = lax.broadcasted_iota(jnp.int32, (CHUNK, CHUNK), 1)
    causal = ri >= ci
    for g in range(group):
        lanes = slice(g * width, (g + 1) * width)
        run_row = run_ref[pl.ds(first + g, 1), :]
        state = None
        for i in range(rows // CHUNK):
            part = slice(i * CHUNK, (i + 1) * CHUNK)
            q, k, v = q_ref[0, part, lanes], k_ref[0, part, lanes], v_ref[0, part, lanes]
            run_col = cols[part, g : g + 1]
            eq = cols[part, heads + g : heads + g + 1]
            ek = cols[part, 2 * heads + g : 2 * heads + g + 1]
            scores = lax.dot_general(q, k, NT, preferred_element_type=F32)
            decay = jnp.exp(jnp.where(causal, run_col - run_row[:, part], -jnp.inf))
            weights = (scores * decay).astype(BF16)
            out = lax.dot_general(weights, v, NN, preferred_element_type=F32)
            faded = (k.astype(F32) * ek).astype(BF16)
            fresh = lax.dot_general(faded, v, TN, preferred_element_type=F32)
            if state is None:
                state = fresh
            else:
                out = out + eq * lax.dot_general(
                    q, state.astype(BF16), NN, preferred_element_type=F32
                )
                state = eq[CHUNK - 1 :, :] * state + fresh
            mixed_ref[part, lanes] = out.astype(mixed_ref.dtype)
        state_ref[g] = state.astype(BF16)
    if loads:
        pl.when(pl.program_id(0) == pl.num_programs(0) - 1)(copy.wait)


def place_block(axis, turn, per):
    return lambda h: ((axis.index() + axis.n + turn) % axis.n) * per + h


def local_pass(qkv, run, cols, heads, y_axis, turn, w, which, done, behind, zeros, group=4):
    rows, width = qkv.shape[1], qkv.shape[2] // heads
    share = heads // y_axis.n
    group = min(group, share)
    block = place_block(y_axis, turn, share // group)
    loads = 0 if w is None else 1
    hbm = pl.BlockSpec(memory_space=pl.ANY)

    def take(part):
        return pl.BlockSpec((1, rows, group * width), lambda h: (part, 0, block(h)))

    more = ([w] if loads else []) + list(done) + list(behind)
    aliases = {5 + loads + i: i for i in range(len(done))}
    out_specs = [
        pl.BlockSpec((rows, group * width), lambda h: (0, block(h))),
        pl.BlockSpec((group, width, width), lambda h: (h, 0, 0)),
        pl.BlockSpec((8, zeros), lambda h: (0, 0)),
    ]
    out_shape = [
        jax.ShapeDtypeStruct((rows, heads * width), BF16),
        jax.ShapeDtypeStruct((share, width, width), BF16),
        jax.ShapeDtypeStruct((8, zeros), BF16),
    ]
    if loads:
        out_specs.append(hbm)
        out_shape.append(pltpu.VMEM(w.shape[1:], w.dtype))
    return pl.pallas_call(
        functools.partial(local_kernel, heads, group, block, loads, which),
        grid=(share // group,),
        in_specs=[
            take(0),
            take(1),
            take(2),
            pl.BlockSpec(run.shape, lambda h: (0, 0)),
            pl.BlockSpec(cols.shape, lambda h: (0, 0)),
        ]
        + [hbm] * len(more),
        out_specs=out_specs,
        out_shape=out_shape,
        scratch_shapes=[pltpu.SemaphoreType.DMA] * loads,
        input_output_aliases=aliases,
        compiler_params=params(20),
        cost_estimate=pl.CostEstimate(flops=1, bytes_accessed=1, transcendentals=0),
        name="local_pass",
    )(qkv, qkv, qkv, run, cols, *more)


def final_kernel(heads, group, first_of, *refs):
    q_ref, mixed_ref, cols_ref, carried_ref, gain_ref = refs[:5]
    out_ref, mark_ref = refs[-2:]
    mark_ref[...] = jnp.zeros_like(mark_ref)
    width = q_ref.shape[2] // group
    first = first_of(pl.program_id(0)) * group
    cols = pltpu.roll(cols_ref[...], 128 - first, 1)
    for g in range(group):
        lanes = slice(g * width, (g + 1) * width)
        er = cols[:, 3 * heads + g : 3 * heads + g + 1]
        far = lax.dot_general(q_ref[0, :, lanes], carried_ref[g], NN, preferred_element_type=F32)
        mixed = mixed_ref[:, lanes].astype(F32) + er * far
        mean = jnp.mean(mixed * mixed, axis=-1, keepdims=True)
        out_ref[:, lanes] = (mixed * lax.rsqrt(mean + EPS) * gain_ref[:, lanes]).astype(BF16)


def final_pass(qkv, mixed, cols, carried, gain, heads, y_axis, back, done, behind, zeros, group=4):
    rows, width = qkv.shape[1], qkv.shape[2] // heads
    share = carried.shape[0]
    group = min(group, share)

    block = place_block(y_axis, -back, share // group)
    more = [a for a in (done, behind) if a is not None]
    return pl.pallas_call(
        functools.partial(final_kernel, heads, group, block),
        grid=(share // group,),
        in_specs=[
            pl.BlockSpec((1, rows, group * width), lambda h: (0, 0, block(h))),
            pl.BlockSpec((rows, group * width), lambda h: (0, block(h))),
            pl.BlockSpec(cols.shape, lambda h: (0, 0)),
            pl.BlockSpec((group, width, width), lambda h: (h, 0, 0)),
            pl.BlockSpec((1, group * width), lambda h: (0, block(h))),
        ]
        + [pl.BlockSpec(memory_space=pl.ANY)] * len(more),
        out_specs=(
            pl.BlockSpec((rows, group * width), lambda h: (0, block(h))),
            pl.BlockSpec((8, zeros), lambda h: (0, 0)),
        ),
        out_shape=(
            jax.ShapeDtypeStruct((rows, heads * width), BF16),
            jax.ShapeDtypeStruct((8, zeros), BF16),
        ),
        input_output_aliases={} if done is None else {5: 0},
        compiler_params=params(20),
        cost_estimate=pl.CostEstimate(flops=1, bytes_accessed=1, transcendentals=0),
        name="final_pass",
    )(qkv, mixed, cols, carried, gain, *more)


def pick(parts, at):
    out = parts[0]
    for p in range(1, len(parts)):
        out = jnp.where((at == p).reshape((-1,) + (1,) * (out.ndim - 1)), parts[p], out)
    return out


def carry_scan(shares, last, seat, z_axis, y_axis):
    share, width = shares[0].shape[:2]
    ny = y_axis.n
    pad = 16
    y = seat[:share] & (ny - 1)
    turned = [(y + k) & (ny - 1) for k in range(ny)]
    fade = jnp.exp(last)
    mine = [pick(rows_split(fade, ny), turned[k]) for k in range(ny)]

    def packed(body, fade):
        rows = jnp.stack(pieces_of(fade), 0)
        rows = jnp.pad(rows, ((0, pad - PIECES), (0, width - share)))
        body = body.reshape(share * width, width)
        return jnp.concatenate([body.astype(BF16), rows.astype(BF16)], 0)

    def unpacked(g):
        body = g[: share * width].reshape(share, width, width).astype(F32)
        return body, jnp.sum(g[share * width :, :share].astype(F32), 0)

    got = [y_axis.send(packed(shares[k], mine[k]), k) for k in range(1, ny)]
    tie = yield
    states, fades = zip((shares[0].astype(F32), mine[0]), *[unpacked(g) for g in got])
    places = [turned[-k % ny] for k in range(ny)]

    def reach(k, end):
        r = jnp.where(places[k] < end, jnp.ones((share,), F32), 0.0)
        for m in range(ny):
            if m != k:
                r = r * jnp.where((places[m] > places[k]) & (places[m] < end), fades[m], 1.0)
        return r[:, None, None]

    def whole(end):
        r = jnp.ones((share,), F32)
        for m in range(ny):
            r = r * jnp.where(places[m] < end, fades[m], 1.0)
        return r[:, None, None]

    inner = sum(reach(k, ny) * states[k] for k in range(ny))
    through = whole(ny)
    carried, behind = jnp.zeros((share, width, width), F32), jnp.ones((share,), F32)
    group, fall = inner + tie[:, None], through[:, 0, 0]
    z = seat[:share] >> (ny.bit_length() - 1)
    step = 1
    while step < z_axis.n:
        upper = (z & step) != 0
        last_step = 2 * step == z_axis.n
        out = group.astype(BF16) if last_step else packed(group, fall)
        tie = yield out
        came = lax.ppermute(out, z_axis.name, z_axis.pairs(step, last_step))
        if last_step:
            came = came.astype(F32) + tie[:, None]
        else:
            came, more = unpacked(came + tie[:1].astype(BF16))
            group = (
                jnp.where(upper, 1.0, more)[:, None, None] * group
                + jnp.where(upper, fall, 1.0)[:, None, None] * came
            )
        carried = carried + jnp.where(upper, behind, 0.0)[:, None, None] * came
        if not last_step:
            behind, fall = jnp.where(upper, behind * more, behind), fall * more
        step *= 2

    def entering(j):
        end = turned[j]
        return (
            whole(end) * carried + sum(reach(k, end) * states[k] for k in range(ny))
        ).astype(BF16)

    yield [entering(0)] + [y_axis.send(entering(j), j) for j in range(1, ny)]


def hidden_kernel(steps, split, *refs):
    xs, w_ref, h_ref, gate, up = refs[:4], refs[4], refs[5], refs[6], refs[7]
    step = pl.program_id(0)

    @pl.when(step == 0)
    def _():
        gate[...] = jnp.zeros_like(gate)
        up[...] = jnp.zeros_like(up)

    def add(pair):
        x = jnp.concatenate([pair[0][...], pair[1][...]], 0)
        gate[...] += lax.dot_general(w_ref[0], x, NT, preferred_element_type=F32)
        up[...] += lax.dot_general(w_ref[1], x, NT, preferred_element_type=F32)

    pl.when(step < split)(lambda: add(xs[:2]))
    pl.when(step >= split)(lambda: add(xs[2:]))

    @pl.when(step == steps - 1)
    def _():
        g = gate[...]
        h_ref[...] = (g / (1.0 + jnp.exp(-g)) * up[...]).T.astype(BF16)


def hidden_pass(xs, w_in, block=1024):
    units, wide = w_in.shape[1], w_in.shape[2]
    tokens = xs[0].shape[0] * 2
    steps = wide // block
    split = steps // 2
    half = tokens // 2
    first = pl.BlockSpec((half, block), lambda s: (0, jnp.minimum(s, split - 1)))
    second = pl.BlockSpec((half, block), lambda s: (0, jnp.maximum(s - split, 0)))
    return pl.pallas_call(
        functools.partial(hidden_kernel, steps, split),
        grid=(steps,),
        in_specs=[first, first, second, second]
        + [pl.BlockSpec((2, units, block), lambda s: (0, 0, s))],
        out_specs=pl.BlockSpec((tokens, units), lambda s: (0, 0)),
        out_shape=jax.ShapeDtypeStruct((tokens, units), BF16),
        scratch_shapes=[pltpu.VMEM((units, tokens), F32), pltpu.VMEM((units, tokens), F32)],
        compiler_params=params(56),
        cost_estimate=pl.CostEstimate(flops=1, bytes_accessed=1, transcendentals=0),
        name="hidden_pass",
    )(*xs, w_in)


def down_kernel(h_ref, w_ref, p0_ref, p1_ref, o0_ref, o1_ref):
    half = o0_ref.shape[0]
    out = lax.dot_general(h_ref[...], w_ref[...], NN, preferred_element_type=F32)
    o0_ref[...] = (out[:half] * p0_ref[...]).astype(BF16)
    o1_ref[...] = (out[half:] * p1_ref[...]).astype(BF16)


def down_pass(h, w_out, probs, start, width, block=1024):
    tokens, units = h.shape
    half = tokens // 2
    off = start // block
    out = jax.ShapeDtypeStruct((half, width), BF16)
    spec = pl.BlockSpec((half, block), lambda s: (0, s))
    weight = pl.BlockSpec((half, 1), lambda s: (0, 0))
    return pl.pallas_call(
        down_kernel,
        grid=(width // block,),
        in_specs=[
            pl.BlockSpec((tokens, units), lambda s: (0, 0)),
            pl.BlockSpec((units, block), lambda s: (0, off + s)),
            weight,
            weight,
        ],
        out_specs=(spec, spec),
        out_shape=(out, out),
        compiler_params=params(56),
        cost_estimate=pl.CostEstimate(flops=1, bytes_accessed=1, transcendentals=0),
        name="down_pass",
    )(h, w_out, *probs)


def across(pieces, lanes, outer):
    m = pieces[0].shape[0] // outer
    return [p[o * m : (o + 1) * m, lanes] for o in range(outer) for p in pieces]


def store_ordered(ref, lanes, value, outer, inner):
    m = ref.shape[0] // (outer * inner)
    for o in range(outer):
        for i in range(inner):
            src, dst = (o * inner + i) * m, (i * outer + o) * m
            ref[dst : dst + m, lanes] = value[src : src + m]


def own_weights(pieces, lanes, experts, outer):
    r = jnp.concatenate(across(pieces, lanes, outer), 0).astype(F32)
    lane = lax.broadcasted_iota(jnp.int32, r.shape, 1)
    mine = (lane % experts == lax.axis_index("exp")) & (lane < PIECES * experts)
    return jnp.sum(jnp.where(mine, r, 0.0), axis=1, keepdims=True)


def chunks(w, scratch, sems, start, width, block, first):
    out = []
    for j, at in enumerate(range(0, width, block)):
        src = w.at[(slice(None),) * (len(w.shape) - 1) + (pl.ds(start + at, block),)]
        out.append(pltpu.make_async_copy(src, scratch.at[j], sems.at[first + j]))
    return out


def lead_kernel(experts, nx, ny, block, *refs):
    a, a2, refs = refs[:nx], refs[nx : 2 * nx], refs[2 * nx :]
    b, b2, refs = refs[:ny], refs[ny : 2 * ny], refs[2 * ny :]
    wg, wu, w_out, o, o2, h, flow, mark, rest, acc, wo, sems = refs
    units, wide = wg.shape
    half = wide // 2
    rows = nx * a[0].shape[0]
    copies = chunks(w_out, wo, sems, 0, half, block, 0)
    copies.append(
        pltpu.make_async_copy(w_out.at[:, pl.ds(half, half)], rest, sems.at[len(copies)])
    )
    for c in copies:
        c.start()
    mark[...] = jnp.zeros_like(mark)
    lanes = slice(half, half + 128)
    flow[:rows] = jnp.broadcast_to(own_weights(b, lanes, experts, nx), (rows, 128))
    flow[rows:] = jnp.broadcast_to(own_weights(b2, lanes, experts, nx), (rows, 128))
    for at in range(0, wide, block):
        if at < half:
            lanes = slice(at, at + block)
            x = jnp.concatenate([p[:, lanes] for p in (*a, *a2)], 0)
        else:
            lanes = slice(at - half, at - half + block)
            x = jnp.concatenate(across(b, lanes, nx) + across(b2, lanes, nx), 0)
        for i, w in enumerate((wg, wu)):
            d = lax.dot_general(w[:, at : at + block], x, NT, preferred_element_type=F32)
            if at == 0:
                acc[i] = d
            else:
                acc[i] += d
    g = acc[0]
    h[...] = (g / (1.0 + jnp.exp(-g)) * acc[1]).T.astype(BF16)
    for j, at in enumerate(range(0, half, block)):
        copies[j].wait()
        lanes = slice(at, at + block)
        d = lax.dot_general(h[...], wo[j], NN, preferred_element_type=F32)
        d = (d * flow[:, :1]).astype(BF16)
        o[:, lanes] = d[:rows]
        o2[:, lanes] = d[rows:]
    copies[-1].wait()


def rest_kernel(nx, ny, block, h, flow, w, behind, o, o2):
    rows = o.shape[0]
    for at in range(0, w.shape[1], block):
        lanes = slice(at, at + block)
        d = lax.dot_general(h[...], w[:, lanes], NN, preferred_element_type=F32)
        d = (d * flow[:, :1]).astype(BF16)
        store_ordered(o, lanes, d[:rows], nx, ny)
        store_ordered(o2, lanes, d[rows:], nx, ny)


def lead_pass(a, a2, b, b2, held, w_out, experts, nx, ny, zeros, block=1024):
    units, wide = held[0].shape
    tokens = 2 * nx * a[0].shape[0]
    n_out = wide // 2 // block
    vmem = pl.BlockSpec(memory_space=pltpu.VMEM)
    hbm = pl.BlockSpec(memory_space=pl.ANY)
    half = pltpu.VMEM((tokens // 2, wide // 2), BF16)
    mark = jax.ShapeDtypeStruct(zeros, F32)
    o, o2, h, flow, mark0, rest = pl.pallas_call(
        functools.partial(lead_kernel, experts, nx, ny, block),
        in_specs=[vmem] * (2 * (nx + ny) + 2) + [hbm],
        out_specs=(vmem,) * 6,
        out_shape=(
            half,
            half,
            pltpu.VMEM((tokens, units), BF16),
            pltpu.VMEM((tokens, 128), F32),
            mark,
            pltpu.VMEM((units, wide // 2), BF16),
        ),
        scratch_shapes=[
            pltpu.VMEM((2, units, tokens), F32),
            pltpu.VMEM((n_out, units, block), BF16),
            pltpu.SemaphoreType.DMA((n_out + 1,)),
        ],
        compiler_params=params(20),
        cost_estimate=pl.CostEstimate(flops=1, bytes_accessed=1, transcendentals=0),
        name="lead_pass",
    )(*a, *a2, *b, *b2, *held, w_out)
    return (o, o2), (h, flow, rest), mark0


def rest_pass(h, flow, w, behind, nx, ny, block=1024):
    tokens, units = h.shape
    vmem = pl.BlockSpec(memory_space=pltpu.VMEM)
    half = pltpu.VMEM((tokens // 2, w.shape[1]), BF16)
    return pl.pallas_call(
        functools.partial(rest_kernel, nx, ny, block),
        in_specs=[vmem] * 3 + [pl.BlockSpec(memory_space=pl.ANY)],
        out_specs=(vmem,) * 2,
        out_shape=(half, half),
        compiler_params=params(20),
        cost_estimate=pl.CostEstimate(flops=1, bytes_accessed=1, transcendentals=0),
        name="rest_pass",
    )(h, flow, w, behind)


def streamed_experts(a, a2, b, b2, w_in, w_out, experts, nx, ny):
    a, a2, b, b2 = [jnp.concatenate(p, 0) for p in (a, a2, b, b2)]
    half = a.shape[1]

    def turned(r, m, n):
        return r.reshape(m, n, -1, r.shape[1]).transpose(1, 0, 2, 3).reshape(r.shape)

    b, b2 = turned(b, ny, nx), turned(b2, ny, nx)

    def weights_of(rows):
        r = rows[:, half : half + PIECES * experts].astype(F32).reshape(-1, PIECES, experts)
        mine = jnp.arange(experts)[None, None] == lax.axis_index("exp")
        return jnp.sum(jnp.where(mine, r, 0.0), axis=(1, 2))[:, None]

    flow = (weights_of(b), weights_of(b2))
    h = hidden_pass((a, a2, b, b2), w_in)
    pa = down_pass(h, w_out, flow, 0, half)
    pb = down_pass(h, w_out, flow, half, half)
    return pa, tuple(turned(p, nx, ny) for p in pb)


def route_columns(ids, probs, experts):
    named = ids[:, :, None] == jnp.arange(experts, dtype=jnp.int32)[None, None]
    weight = jnp.sum(jnp.where(named, probs[:, :, None], 0.0), axis=1)
    route = jnp.concatenate(pieces_of(weight), 1)
    return jnp.pad(route, ((0, 0), (0, 128 - route.shape[1]))).astype(BF16)


def in_hbm(a):
    return pltpu.with_memory_space_constraint(a, pltpu.HBM)


def nothing(a, rows, lanes):
    probe = a[-rows:, :lanes].astype(F32)
    return jnp.where(probe != probe, 1.0, 0.0)


def on_device(axes, projected, log_decay, norm_gain, moe_tokens, expert_ids, route_probs, w_in, w_out):
    x_axis, core, z_axis, y_axis = axes
    nx, ny, nz = x_axis.n, y_axis.n, z_axis.n
    heads = log_decay.shape[1]
    half = moe_tokens.shape[1] // 2
    experts = w_in.shape[0] * lax.axis_size("exp")
    tokens = moe_tokens.shape[0] * lax.axis_size("seq") * lax.axis_size("exp")
    fits = tokens <= 512 and ny == 2
    zeros = (heads // ny, projected.shape[2] // heads)
    qkv = in_hbm(projected.transpose(1, 0, 2))
    w_in = w_in[0].transpose(1, 2, 0)
    w_out = w_out[0]
    route = route_columns(expert_ids, route_probs, experts)

    z = gather(z_axis, jnp.concatenate([moe_tokens, route], 1))
    run, cols, seat = prepare(log_decay)
    done, held, shares = (), [], {}
    for i in range(ny):
        turn = (i + 1) % ny
        w = in_hbm(w_in) if fits else None
        behind = (z,) * (i == ny - 1)
        made = local_pass(
            qkv, run, cols, heads, y_axis, turn, w, i, done, behind, z.shape[1] - half
        )
        done, shares[turn], mark = made[:1], made[1], made[2]
        held += made[3:]
    mixed = done[0]
    scan = carry_scan(shares, run[:, -1], seat[:, 0], z_axis, y_axis)
    next(scan)
    a, b = z[:, :half], z[:, half:]
    a, b = gather(y_axis, a), gather(x_axis, b)
    a, b = parts_of(x_axis, a + mark[:1, :half]), parts_of(y_axis, b + mark[:1])
    scan.send(nothing(a[-1], *zeros))
    a2, b2 = [core.send(p, 1) for p in a], [core.send(p, 1) for p in b]
    if fits:
        pa, more, mark = lead_pass(
            a, a2, b, b2, held, in_hbm(w_out), experts, nx, ny, zeros
        )
        hop = scan.send(mark)
        pb = rest_pass(*more, hop, nx, ny)
    else:
        pa, pb = streamed_experts(a, a2, b, b2, w_in, w_out, experts, nx, ny)
        scan.send(jnp.zeros(zeros, F32))
    for _ in range((nz - 1).bit_length() - 2):
        scan.send(jnp.zeros(zeros, F32))
    a, b = scatter(core, pa), scatter(core, pb)
    a, b = scatter(x_axis, rows_split(a, nx)), scatter(y_axis, rows_split(b, ny))
    carried = scan.send(nothing(a, *zeros))
    attn_out = None

    def final(k, behind):
        gain = norm_gain[None]
        return final_pass(
            qkv, mixed, cols, carried[k], gain, heads, y_axis, k, attn_out, behind, 2 * half
        )

    attn_out, mark = final(0, a)
    a, b = scatter(y_axis, rows_split(a, ny)), scatter(x_axis, rows_split(b, nx))
    both = jnp.concatenate([a, b], 1) + mark[:1]
    for k in range(1, ny):
        attn_out, _ = final(k, both)
    moe_out = scatter(z_axis, rows_split(both, nz))
    return attn_out, moe_out


def solution(mesh):
    nz, ny = factors(mesh.shape["seq"])
    nx = mesh.shape["exp"] // 2
    axes = (
        Axis("exp", nx, 2, 1),
        Axis("exp", 2, 1, nx),
        Axis("seq", nz, ny, 1),
        Axis("seq", ny, 1, nz),
    )
    in_specs = (
        P("seq", None, "exp"),
        P("seq", "exp"),
        P("exp"),
        P(("seq", "exp"), None),
        P(("seq", "exp"), None),
        P(("seq", "exp"), None),
        P("exp", None, None, "seq"),
        P("exp", "seq", None),
    )
    out_specs = (P("seq", "exp"), P(("seq", "exp"), None))
    return jax.shard_map(
        functools.partial(on_device, axes),
        mesh=mesh,
        in_specs=in_specs,
        out_specs=out_specs,
        check_vma=False,
    )
```

```python
import functools
import jax
import jax.numpy as jnp
from jax import lax
from jax.experimental import pallas as pl
from jax.experimental.pallas import tpu as pltpu
from jax.sharding import PartitionSpec as P

EPS = 1e-06
CHUNK = 256
PIECES = 3
F32 = jnp.float32
BF16 = jnp.bfloat16
NT = (((1,), (1,)), ((), ()))
TN = (((0,), (0,)), ((), ()))
NN = (((1,), (0,)), ((), ()))


def factors(size):
    bits = size.bit_length() - 1
    inner = 2 ** (bits // 2)
    return size // inner, inner


class Axis:
    def __init__(self, name, n, inner, outer):
        self.name, self.n, self.inner, self.outer = name, n, inner, outer

    def index(self):
        return (lax.axis_index(self.name) // self.inner) % self.n

    def flat(self, o, i, j):
        return (o * self.n + i) * self.inner + j

    def turn(self, k):
        return [
            (self.flat(o, i, j), self.flat(o, (i + k) % self.n, j))
            for o in range(self.outer)
            for i in range(self.n)
            for j in range(self.inner)
        ]

    def pairs(self, step, upwards):
        return [
            (self.flat(o, i, j), self.flat(o, i ^ step, j))
            for o in range(self.outer)
            for i in range(self.n)
            for j in range(self.inner)
            if not (upwards and i & step)
        ]

    def send(self, a, k):
        return lax.ppermute(a, self.name, self.turn(k))


def parts_of(axis, a):
    return [a] + [axis.send(a, k) for k in range(1, axis.n)]


def gather(axis, a):
    return jnp.concatenate(parts_of(axis, a), 0)


def total(parts):
    s = parts[0].astype(F32)
    for p in parts[1:]:
        s = s + p.astype(F32)
    return s.astype(BF16)


def scatter(axis, parts):
    return total([parts[0]] + [axis.send(parts[k], axis.n - k) for k in range(1, axis.n)])


def rows_split(a, n):
    m = a.shape[0] // n
    return [a[i * m : (i + 1) * m] for i in range(n)]


def pieces_of(x):
    out = []
    for _ in range(PIECES):
        hi = lax.reduce_precision(x, 8, 7)
        out.append(hi)
        x = x - hi
    return out


def params(limit=16):
    return pltpu.CompilerParams(vmem_limit_bytes=limit * 2**20)


def prep_kernel(heads, rows, d_ref, run_ref, cols_ref, seat_ref):
    seat_ref[...] = jnp.zeros_like(seat_ref) + lax.axis_index("seq")
    run = d_ref[...]
    lane = lax.broadcasted_iota(jnp.int32, (heads, rows), 1)
    step = 1
    while step < rows:
        run = run + jnp.where(lane >= step, pltpu.roll(run, step, 1), 0.0)
        step *= 2
    enter = jnp.zeros((heads, 1), F32)
    before, after = [], []
    for i in range(rows // CHUNK):
        leave = run[:, (i + 1) * CHUNK - 1 : (i + 1) * CHUNK]
        before.append(jnp.broadcast_to(enter, (heads, CHUNK)))
        after.append(jnp.broadcast_to(leave, (heads, CHUNK)))
        enter = leave
    eq = jnp.exp(run - jnp.concatenate(before, 1))
    ek = jnp.exp(jnp.concatenate(after, 1) - run)
    run_ref[...] = run
    tall = jnp.concatenate([run, eq, ek, jnp.exp(run)], 0)
    if 4 * heads < 128:
        tall = jnp.concatenate([tall, jnp.zeros((128 - 4 * heads, rows), F32)], 0)
    cols_ref[...] = tall.T


def prepare(log_decay):
    rows, heads = log_decay.shape
    return pl.pallas_call(
        functools.partial(prep_kernel, heads, rows),
        out_shape=(
            jax.ShapeDtypeStruct((heads, rows), F32),
            jax.ShapeDtypeStruct((rows, 128), F32),
            jax.ShapeDtypeStruct((heads, 128), jnp.int32),
        ),
        compiler_params=params(),
        name="prepare",
    )(log_decay.T)


def local_kernel(heads, group, first_of, loads, which, *refs):
    q_ref, k_ref, v_ref, run_ref, cols_ref = refs[:5]
    mixed_ref, state_ref, mark_ref = refs[-3 - 2 * loads :][:3]
    if loads:
        w_ref, held_ref, sem = refs[5], refs[-2], refs[-1]
        copy = pltpu.make_async_copy(w_ref.at[which], held_ref, sem)
        pl.when(pl.program_id(0) == 0)(copy.start)
    mark_ref[...] = jnp.zeros_like(mark_ref)
    rows, width = q_ref.shape[1], q_ref.shape[2] // group
    first = first_of(pl.program_id(0)) * group
    cols = pltpu.roll(cols_ref[...], 128 - first, 1)
    ri = lax.broadcasted_iota(jnp.int32, (CHUNK, CHUNK), 0)
    ci = lax.broadcasted_iota(jnp.int32, (CHUNK, CHUNK), 1)
    causal = ri >= ci
    for g in range(group):
        lanes = slice(g * width, (g + 1) * width)
        run_row = run_ref[pl.ds(first + g, 1), :]
        state = None
        for i in range(rows // CHUNK):
            part = slice(i * CHUNK, (i + 1) * CHUNK)
            q, k, v = q_ref[0, part, lanes], k_ref[0, part, lanes], v_ref[0, part, lanes]
            run_col = cols[part, g : g + 1]
            eq = cols[part, heads + g : heads + g + 1]
            ek = cols[part, 2 * heads + g : 2 * heads + g + 1]
            scores = lax.dot_general(q, k, NT, preferred_element_type=F32)
            decay = jnp.exp(jnp.where(causal, run_col - run_row[:, part], -jnp.inf))
            weights = (scores * decay).astype(BF16)
            out = lax.dot_general(weights, v, NN, preferred_element_type=F32)
            faded = (k.astype(F32) * ek).astype(BF16)
            fresh = lax.dot_general(faded, v, TN, preferred_element_type=F32)
            if state is None:
                state = fresh
            else:
                out = out + eq * lax.dot_general(
                    q, state.astype(BF16), NN, preferred_element_type=F32
                )
                state = eq[CHUNK - 1 :, :] * state + fresh
            mixed_ref[part, lanes] = out.astype(mixed_ref.dtype)
        state_ref[g] = state.astype(BF16)
    if loads:
        pl.when(pl.program_id(0) == pl.num_programs(0) - 1)(copy.wait)


def place_block(axis, turn, per):
    return lambda h: ((axis.index() + axis.n + turn) % axis.n) * per + h


def local_pass(qkv, run, cols, heads, y_axis, turn, w, which, done, behind, zeros, group=4):
    rows, width = qkv.shape[1], qkv.shape[2] // heads
    share = heads // y_axis.n
    group = min(group, share)
    block = place_block(y_axis, turn, share // group)
    loads = 0 if w is None else 1
    hbm = pl.BlockSpec(memory_space=pl.ANY)

    def take(part):
        return pl.BlockSpec((1, rows, group * width), lambda h: (part, 0, block(h)))

    more = ([w] if loads else []) + list(done) + list(behind)
    aliases = {5 + loads + i: i for i in range(len(done))}
    out_specs = [
        pl.BlockSpec((rows, group * width), lambda h: (0, block(h))),
        pl.BlockSpec((group, width, width), lambda h: (h, 0, 0)),
        pl.BlockSpec((8, zeros), lambda h: (0, 0)),
    ]
    out_shape = [
        jax.ShapeDtypeStruct((rows, heads * width), BF16),
        jax.ShapeDtypeStruct((share, width, width), BF16),
        jax.ShapeDtypeStruct((8, zeros), BF16),
    ]
    if loads:
        out_specs.append(hbm)
        out_shape.append(pltpu.VMEM(w.shape[1:], w.dtype))
    return pl.pallas_call(
        functools.partial(local_kernel, heads, group, block, loads, which),
        grid=(share // group,),
        in_specs=[
            take(0),
            take(1),
            take(2),
            pl.BlockSpec(run.shape, lambda h: (0, 0)),
            pl.BlockSpec(cols.shape, lambda h: (0, 0)),
        ]
        + [hbm] * len(more),
        out_specs=out_specs,
        out_shape=out_shape,
        scratch_shapes=[pltpu.SemaphoreType.DMA] * loads,
        input_output_aliases=aliases,
        compiler_params=params(20),
        cost_estimate=pl.CostEstimate(flops=1, bytes_accessed=1, transcendentals=0),
        name="local_pass",
    )(qkv, qkv, qkv, run, cols, *more)


def final_kernel(heads, group, first_of, *refs):
    q_ref, mixed_ref, cols_ref, carried_ref, gain_ref = refs[:5]
    out_ref, mark_ref = refs[-2:]
    mark_ref[...] = jnp.zeros_like(mark_ref)
    width = q_ref.shape[2] // group
    first = first_of(pl.program_id(0)) * group
    cols = pltpu.roll(cols_ref[...], 128 - first, 1)
    for g in range(group):
        lanes = slice(g * width, (g + 1) * width)
        er = cols[:, 3 * heads + g : 3 * heads + g + 1]
        far = lax.dot_general(q_ref[0, :, lanes], carried_ref[g], NN, preferred_element_type=F32)
        mixed = mixed_ref[:, lanes].astype(F32) + er * far
        mean = jnp.mean(mixed * mixed, axis=-1, keepdims=True)
        out_ref[:, lanes] = (mixed * lax.rsqrt(mean + EPS) * gain_ref[:, lanes]).astype(BF16)


def final_pass(qkv, mixed, cols, carried, gain, heads, y_axis, back, done, behind, zeros, group=4):
    rows, width = qkv.shape[1], qkv.shape[2] // heads
    share = carried.shape[0]
    group = min(group, share)

    block = place_block(y_axis, -back, share // group)
    more = [a for a in (done, behind) if a is not None]
    return pl.pallas_call(
        functools.partial(final_kernel, heads, group, block),
        grid=(share // group,),
        in_specs=[
            pl.BlockSpec((1, rows, group * width), lambda h: (0, 0, block(h))),
            pl.BlockSpec((rows, group * width), lambda h: (0, block(h))),
            pl.BlockSpec(cols.shape, lambda h: (0, 0)),
            pl.BlockSpec((group, width, width), lambda h: (h, 0, 0)),
            pl.BlockSpec((1, group * width), lambda h: (0, block(h))),
        ]
        + [pl.BlockSpec(memory_space=pl.ANY)] * len(more),
        out_specs=(
            pl.BlockSpec((rows, group * width), lambda h: (0, block(h))),
            pl.BlockSpec((8, zeros), lambda h: (0, 0)),
        ),
        out_shape=(
            jax.ShapeDtypeStruct((rows, heads * width), BF16),
            jax.ShapeDtypeStruct((8, zeros), BF16),
        ),
        input_output_aliases={} if done is None else {5: 0},
        compiler_params=params(20),
        cost_estimate=pl.CostEstimate(flops=1, bytes_accessed=1, transcendentals=0),
        name="final_pass",
    )(qkv, mixed, cols, carried, gain, *more)


def pick(parts, at):
    out = parts[0]
    for p in range(1, len(parts)):
        out = jnp.where((at == p).reshape((-1,) + (1,) * (out.ndim - 1)), parts[p], out)
    return out


def carry_scan(shares, last, seat, z_axis, y_axis):
    share, width = shares[0].shape[:2]
    ny = y_axis.n
    pad = 16
    y = seat[:share] & (ny - 1)
    turned = [(y + k) & (ny - 1) for k in range(ny)]
    fade = jnp.exp(last)
    mine = [pick(rows_split(fade, ny), turned[k]) for k in range(ny)]

    def packed(body, fade):
        rows = jnp.stack(pieces_of(fade), 0)
        rows = jnp.pad(rows, ((0, pad - PIECES), (0, width - share)))
        body = body.reshape(share * width, width)
        return jnp.concatenate([body.astype(BF16), rows.astype(BF16)], 0)

    def unpacked(g):
        body = g[: share * width].reshape(share, width, width).astype(F32)
        return body, jnp.sum(g[share * width :, :share].astype(F32), 0)

    got = [y_axis.send(packed(shares[k], mine[k]), k) for k in range(1, ny)]
    tie = yield
    states, fades = zip((shares[0].astype(F32), mine[0]), *[unpacked(g) for g in got])
    places = [turned[-k % ny] for k in range(ny)]

    def reach(k, end):
        r = jnp.where(places[k] < end, jnp.ones((share,), F32), 0.0)
        for m in range(ny):
            if m != k:
                r = r * jnp.where((places[m] > places[k]) & (places[m] < end), fades[m], 1.0)
        return r[:, None, None]

    def whole(end):
        r = jnp.ones((share,), F32)
        for m in range(ny):
            r = r * jnp.where(places[m] < end, fades[m], 1.0)
        return r[:, None, None]

    inner = sum(reach(k, ny) * states[k] for k in range(ny))
    through = whole(ny)
    carried, behind = jnp.zeros((share, width, width), F32), jnp.ones((share,), F32)
    group, fall = inner + tie[:, None], through[:, 0, 0]
    z = seat[:share] >> (ny.bit_length() - 1)
    step = 1
    while step < z_axis.n:
        upper = (z & step) != 0
        last_step = 2 * step == z_axis.n
        if last_step:
            tie = yield group
            group = group + tie[:, None]
        out = group.astype(BF16) if last_step else packed(group, fall)
        tie = yield out
        came = lax.ppermute(out, z_axis.name, z_axis.pairs(step, last_step))
        if last_step:
            came = came.astype(F32) + tie[:, None]
        else:
            came, more = unpacked(came + tie[:1].astype(BF16))
            group = (
                jnp.where(upper, 1.0, more)[:, None, None] * group
                + jnp.where(upper, fall, 1.0)[:, None, None] * came
            )
        carried = carried + jnp.where(upper, behind, 0.0)[:, None, None] * came
        if not last_step:
            behind, fall = jnp.where(upper, behind * more, behind), fall * more
        step *= 2

    def entering(j):
        end = turned[j]
        return (
            whole(end) * carried + sum(reach(k, end) * states[k] for k in range(ny))
        ).astype(BF16)

    yield [entering(0)] + [y_axis.send(entering(j), j) for j in range(1, ny)]


def hidden_kernel(steps, split, *refs):
    xs, w_ref, h_ref, gate, up = refs[:4], refs[4], refs[5], refs[6], refs[7]
    step = pl.program_id(0)

    @pl.when(step == 0)
    def _():
        gate[...] = jnp.zeros_like(gate)
        up[...] = jnp.zeros_like(up)

    def add(pair):
        x = jnp.concatenate([pair[0][...], pair[1][...]], 0)
        gate[...] += lax.dot_general(w_ref[0], x, NT, preferred_element_type=F32)
        up[...] += lax.dot_general(w_ref[1], x, NT, preferred_element_type=F32)

    pl.when(step < split)(lambda: add(xs[:2]))
    pl.when(step >= split)(lambda: add(xs[2:]))

    @pl.when(step == steps - 1)
    def _():
        g = gate[...]
        h_ref[...] = (g / (1.0 + jnp.exp(-g)) * up[...]).T.astype(BF16)


def hidden_pass(xs, w_in, block=1024):
    units, wide = w_in.shape[1], w_in.shape[2]
    tokens = xs[0].shape[0] * 2
    steps = wide // block
    split = steps // 2
    half = tokens // 2
    first = pl.BlockSpec((half, block), lambda s: (0, jnp.minimum(s, split - 1)))
    second = pl.BlockSpec((half, block), lambda s: (0, jnp.maximum(s - split, 0)))
    return pl.pallas_call(
        functools.partial(hidden_kernel, steps, split),
        grid=(steps,),
        in_specs=[first, first, second, second]
        + [pl.BlockSpec((2, units, block), lambda s: (0, 0, s))],
        out_specs=pl.BlockSpec((tokens, units), lambda s: (0, 0)),
        out_shape=jax.ShapeDtypeStruct((tokens, units), BF16),
        scratch_shapes=[pltpu.VMEM((units, tokens), F32), pltpu.VMEM((units, tokens), F32)],
        compiler_params=params(56),
        cost_estimate=pl.CostEstimate(flops=1, bytes_accessed=1, transcendentals=0),
        name="hidden_pass",
    )(*xs, w_in)


def down_kernel(h_ref, w_ref, p0_ref, p1_ref, o0_ref, o1_ref):
    half = o0_ref.shape[0]
    out = lax.dot_general(h_ref[...], w_ref[...], NN, preferred_element_type=F32)
    o0_ref[...] = (out[:half] * p0_ref[...]).astype(BF16)
    o1_ref[...] = (out[half:] * p1_ref[...]).astype(BF16)


def down_pass(h, w_out, probs, start, width, block=1024):
    tokens, units = h.shape
    half = tokens // 2
    off = start // block
    out = jax.ShapeDtypeStruct((half, width), BF16)
    spec = pl.BlockSpec((half, block), lambda s: (0, s))
    weight = pl.BlockSpec((half, 1), lambda s: (0, 0))
    return pl.pallas_call(
        down_kernel,
        grid=(width // block,),
        in_specs=[
            pl.BlockSpec((tokens, units), lambda s: (0, 0)),
            pl.BlockSpec((units, block), lambda s: (0, off + s)),
            weight,
            weight,
        ],
        out_specs=(spec, spec),
        out_shape=(out, out),
        compiler_params=params(56),
        cost_estimate=pl.CostEstimate(flops=1, bytes_accessed=1, transcendentals=0),
        name="down_pass",
    )(h, w_out, *probs)


def across(pieces, lanes, outer):
    m = pieces[0].shape[0] // outer
    return [p[o * m : (o + 1) * m, lanes] for o in range(outer) for p in pieces]


def store_ordered(ref, lanes, value, outer, inner):
    m = ref.shape[0] // (outer * inner)
    for o in range(outer):
        for i in range(inner):
            src, dst = (o * inner + i) * m, (i * outer + o) * m
            ref[dst : dst + m, lanes] = value[src : src + m]


def own_weights(pieces, lanes, experts, outer):
    r = jnp.concatenate(across(pieces, lanes, outer), 0).astype(F32)
    lane = lax.broadcasted_iota(jnp.int32, r.shape, 1)
    mine = (lane % experts == lax.axis_index("exp")) & (lane < PIECES * experts)
    return jnp.sum(jnp.where(mine, r, 0.0), axis=1, keepdims=True)


def chunks(w, scratch, sems, start, width, block, first):
    out = []
    for j, at in enumerate(range(0, width, block)):
        src = w.at[(slice(None),) * (len(w.shape) - 1) + (pl.ds(start + at, block),)]
        out.append(pltpu.make_async_copy(src, scratch.at[j], sems.at[first + j]))
    return out


def lead_kernel(experts, nx, ny, block, *refs):
    a, a2, refs = refs[:nx], refs[nx : 2 * nx], refs[2 * nx :]
    b, b2, refs = refs[:ny], refs[ny : 2 * ny], refs[2 * ny :]
    wg, wu, w_out, o, o2, h, flow, mark, rest, acc, wo, sems = refs
    units, wide = wg.shape
    half = wide // 2
    rows = nx * a[0].shape[0]
    copies = chunks(w_out, wo, sems, 0, half, block, 0)
    copies.append(
        pltpu.make_async_copy(w_out.at[:, pl.ds(half, half)], rest, sems.at[len(copies)])
    )
    for c in copies:
        c.start()
    mark[...] = jnp.zeros_like(mark)
    lanes = slice(half, half + 128)
    flow[:rows] = jnp.broadcast_to(own_weights(b, lanes, experts, nx), (rows, 128))
    flow[rows:] = jnp.broadcast_to(own_weights(b2, lanes, experts, nx), (rows, 128))
    for at in range(0, wide, block):
        if at < half:
            lanes = slice(at, at + block)
            x = jnp.concatenate([p[:, lanes] for p in (*a, *a2)], 0)
        else:
            lanes = slice(at - half, at - half + block)
            x = jnp.concatenate(across(b, lanes, nx) + across(b2, lanes, nx), 0)
        for i, w in enumerate((wg, wu)):
            d = lax.dot_general(w[:, at : at + block], x, NT, preferred_element_type=F32)
            if at == 0:
                acc[i] = d
            else:
                acc[i] += d
    g = acc[0]
    h[...] = (g / (1.0 + jnp.exp(-g)) * acc[1]).T.astype(BF16)
    for j, at in enumerate(range(0, half, block)):
        copies[j].wait()
        lanes = slice(at, at + block)
        d = lax.dot_general(h[...], wo[j], NN, preferred_element_type=F32)
        d = (d * flow[:, :1]).astype(BF16)
        o[:, lanes] = d[:rows]
        o2[:, lanes] = d[rows:]
    copies[-1].wait()


def rest_kernel(nx, ny, block, h, flow, w, behind, o, o2):
    rows = o.shape[0]
    for at in range(0, w.shape[1], block):
        lanes = slice(at, at + block)
        d = lax.dot_general(h[...], w[:, lanes], NN, preferred_element_type=F32)
        d = (d * flow[:, :1]).astype(BF16)
        store_ordered(o, lanes, d[:rows], nx, ny)
        store_ordered(o2, lanes, d[rows:], nx, ny)


def lead_pass(a, a2, b, b2, held, w_out, experts, nx, ny, zeros, block=1024):
    units, wide = held[0].shape
    tokens = 2 * nx * a[0].shape[0]
    n_out = wide // 2 // block
    vmem = pl.BlockSpec(memory_space=pltpu.VMEM)
    hbm = pl.BlockSpec(memory_space=pl.ANY)
    half = pltpu.VMEM((tokens // 2, wide // 2), BF16)
    mark = jax.ShapeDtypeStruct(zeros, F32)
    o, o2, h, flow, mark0, rest = pl.pallas_call(
        functools.partial(lead_kernel, experts, nx, ny, block),
        in_specs=[vmem] * (2 * (nx + ny) + 2) + [hbm],
        out_specs=(vmem,) * 6,
        out_shape=(
            half,
            half,
            pltpu.VMEM((tokens, units), BF16),
            pltpu.VMEM((tokens, 128), F32),
            mark,
            pltpu.VMEM((units, wide // 2), BF16),
        ),
        scratch_shapes=[
            pltpu.VMEM((2, units, tokens), F32),
            pltpu.VMEM((n_out, units, block), BF16),
            pltpu.SemaphoreType.DMA((n_out + 1,)),
        ],
        compiler_params=params(20),
        cost_estimate=pl.CostEstimate(flops=1, bytes_accessed=1, transcendentals=0),
        name="lead_pass",
    )(*a, *a2, *b, *b2, *held, w_out)
    return (o, o2), (h, flow, rest), mark0


def rest_pass(h, flow, w, behind, nx, ny, block=1024):
    tokens, units = h.shape
    vmem = pl.BlockSpec(memory_space=pltpu.VMEM)
    half = pltpu.VMEM((tokens // 2, w.shape[1]), BF16)
    return pl.pallas_call(
        functools.partial(rest_kernel, nx, ny, block),
        in_specs=[vmem] * 3 + [pl.BlockSpec(memory_space=pl.ANY)],
        out_specs=(vmem,) * 2,
        out_shape=(half, half),
        compiler_params=params(20),
        cost_estimate=pl.CostEstimate(flops=1, bytes_accessed=1, transcendentals=0),
        name="rest_pass",
    )(h, flow, w, behind)


def streamed_experts(a, a2, b, b2, w_in, w_out, experts, nx, ny):
    a, a2, b, b2 = [jnp.concatenate(p, 0) for p in (a, a2, b, b2)]
    half = a.shape[1]

    def turned(r, m, n):
        return r.reshape(m, n, -1, r.shape[1]).transpose(1, 0, 2, 3).reshape(r.shape)

    b, b2 = turned(b, ny, nx), turned(b2, ny, nx)

    def weights_of(rows):
        r = rows[:, half : half + PIECES * experts].astype(F32).reshape(-1, PIECES, experts)
        mine = jnp.arange(experts)[None, None] == lax.axis_index("exp")
        return jnp.sum(jnp.where(mine, r, 0.0), axis=(1, 2))[:, None]

    flow = (weights_of(b), weights_of(b2))
    h = hidden_pass((a, a2, b, b2), w_in)
    pa = down_pass(h, w_out, flow, 0, half)
    pb = down_pass(h, w_out, flow, half, half)
    return pa, tuple(turned(p, nx, ny) for p in pb)


def route_columns(ids, probs, experts):
    named = ids[:, :, None] == jnp.arange(experts, dtype=jnp.int32)[None, None]
    weight = jnp.sum(jnp.where(named, probs[:, :, None], 0.0), axis=1)
    route = jnp.concatenate(pieces_of(weight), 1)
    return jnp.pad(route, ((0, 0), (0, 128 - route.shape[1]))).astype(BF16)


def in_hbm(a):
    return pltpu.with_memory_space_constraint(a, pltpu.HBM)


def nothing(a, rows, lanes):
    probe = a[-rows:, :lanes].astype(F32)
    return jnp.where(probe != probe, 1.0, 0.0)


def on_device(axes, projected, log_decay, norm_gain, moe_tokens, expert_ids, route_probs, w_in, w_out):
    x_axis, core, z_axis, y_axis = axes
    nx, ny, nz = x_axis.n, y_axis.n, z_axis.n
    heads = log_decay.shape[1]
    half = moe_tokens.shape[1] // 2
    experts = w_in.shape[0] * lax.axis_size("exp")
    tokens = moe_tokens.shape[0] * lax.axis_size("seq") * lax.axis_size("exp")
    fits = tokens <= 512 and ny == 2
    zeros = (heads // ny, projected.shape[2] // heads)
    qkv = in_hbm(projected.transpose(1, 0, 2))
    w_in = w_in[0].transpose(1, 2, 0)
    w_out = w_out[0]
    route = route_columns(expert_ids, route_probs, experts)

    z = gather(z_axis, jnp.concatenate([moe_tokens, route], 1))
    run, cols, seat = prepare(log_decay)
    done, held, shares = (), [], {}
    for i in range(ny):
        turn = (i + 1) % ny
        w = in_hbm(w_in) if fits else None
        behind = (z,) * (i == ny - 1)
        made = local_pass(
            qkv, run, cols, heads, y_axis, turn, w, i, done, behind, z.shape[1] - half
        )
        done, shares[turn], mark = made[:1], made[1], made[2]
        held += made[3:]
    mixed = done[0]
    scan = carry_scan(shares, run[:, -1], seat[:, 0], z_axis, y_axis)
    next(scan)
    a, b = z[:, :half], z[:, half:]
    a, b = gather(y_axis, a), gather(x_axis, b)
    a, b = parts_of(x_axis, a + mark[:1, :half]), parts_of(y_axis, b + mark[:1])
    scan.send(nothing(a[-1], *zeros))
    a2, b2 = [core.send(p, 1) for p in a], [core.send(p, 1) for p in b]
    if fits:
        pa, more, mark = lead_pass(
            a, a2, b, b2, held, in_hbm(w_out), experts, nx, ny, zeros
        )
        hop = scan.send(mark)
        pb = rest_pass(*more, hop, nx, ny)
    else:
        pa, pb = streamed_experts(a, a2, b, b2, w_in, w_out, experts, nx, ny)
        scan.send(jnp.zeros(zeros, F32))
    for _ in range((nz - 1).bit_length() - 2):
        scan.send(jnp.zeros(zeros, F32))
    a, b = scatter(core, pa), scatter(core, pb)
    scan.send(nothing(a, *zeros) + nothing(b, *zeros))
    a, b = scatter(x_axis, rows_split(a, nx)), scatter(y_axis, rows_split(b, ny))
    carried = scan.send(nothing(a, *zeros))
    attn_out = None

    def final(k, behind):
        gain = norm_gain[None]
        return final_pass(
            qkv, mixed, cols, carried[k], gain, heads, y_axis, k, attn_out, behind, 2 * half
        )

    attn_out, mark = final(0, a)
    a, b = scatter(y_axis, rows_split(a, ny)), scatter(x_axis, rows_split(b, nx))
    both = jnp.concatenate([a, b], 1) + mark[:1]
    for k in range(1, ny):
        attn_out, _ = final(k, both)
    moe_out = scatter(z_axis, rows_split(both, nz))
    return attn_out, moe_out


def solution(mesh):
    nz, ny = factors(mesh.shape["seq"])
    nx = mesh.shape["exp"] // 2
    axes = (
        Axis("exp", nx, 2, 1),
        Axis("exp", 2, 1, nx),
        Axis("seq", nz, ny, 1),
        Axis("seq", ny, 1, nz),
    )
    in_specs = (
        P("seq", None, "exp"),
        P("seq", "exp"),
        P("exp"),
        P(("seq", "exp"), None),
        P(("seq", "exp"), None),
        P(("seq", "exp"), None),
        P("exp", None, None, "seq"),
        P("exp", "seq", None),
    )
    out_specs = (P("seq", "exp"), P(("seq", "exp"), None))
    return jax.shard_map(
        functools.partial(on_device, axes),
        mesh=mesh,
        in_specs=in_specs,
        out_specs=out_specs,
        check_vma=False,
    )
```
